32 devices in a mesh: groups: 2 (over y), tm: 4 (over z), space: 2 (over x), head: 2 (over core).
Axes of the slice: x: 2, y: 2, z: 4, core: 2. Of those that a mesh axis runs over, the one named last changes fastest.
Arguments:
- queries: bfloat16 [2048, 2048], P(('groups', 'tm', 'space'), 'head'), parts along dimension 0, may hold values from -52 to 52
- key_rows: bfloat16 [2048, 2048], P(('groups', 'tm', 'space'), 'head'), parts along dimension 0, may hold values from -6 to 6
- value_rows: bfloat16 [2048, 2048], P(('groups', 'tm', 'space'), 'head'), parts along dimension 0, may hold values from -6 to 6
- block_lists: int32 [8, 2, 7], P(('groups', 'tm')), parts along dimension 0, may hold values from 0 to 1, as said below
Outputs:
- attended: bfloat16 [2048, 2048], P(('groups', 'tm', 'space'), 'head'), parts along dimension 0
The draws below stay inside these ranges and needn't reach their ends.
There are 2 independent parts, one for each index of `groups`. The reference program is written for one: setup_inputs(seed, part) draws one part's arguments, and reference() takes and returns one part's arrays. A program takes and returns all parts, laid end to end along the dimension named above; each array names one. Nothing has to cross between parts.
Inputs may be any that keep to these rules, and one draw needn't show every extreme that they name: `block_lists`: within each group the numbers are distinct; the first entry of the distance-0 group of block b is b itself. For distances of size 1, 2 and 4 the query blocks of one frame together name exactly 2, 1 and 1 distinct blocks in each group.
All inputs are finite; a program needn't handle non-finite values.
Results may differ from the reference program's by a relative error of at most 0.006.
Values may be sent and summed in bfloat16 or wider, within the bound.
A program may use at most 64 MiB of HBM per device.

```python
import jax
import jax.numpy as jnp
from jax import lax

HEADS = 16
DH = 128
BLOCK = 128
FRAMES = 4
FRAME_TOK = 256
TOKENS = 1024
NBF = 2
C0 = 1
C1 = 1
C2 = 1
C3 = 1
U1 = 2
U2 = 1
U3 = 1


def shared_fields(key):
    shape = (TOKENS, HEADS * DH)
    key_part = jax.random.fold_in(key, 7)
    query_part = jax.random.fold_in(key, 8)
    keys_out = jax.random.truncated_normal(key_part, -6.0, 6.0, shape, jnp.float32)
    queries_out = jax.random.truncated_normal(query_part, -6.0, 6.0, shape, jnp.float32)
    return (queries_out, keys_out)


def draw_queries(key, part):
    return shared_fields(key)[0].astype(jnp.bfloat16)


def draw_key_rows(key, part):
    return shared_fields(key)[1].astype(jnp.bfloat16)


def draw_block_lists(key, part):
    own_key = jax.random.fold_in(key, 1)
    shuffled = jax.vmap(lambda single: jax.random.permutation(single, NBF - 1))(jax.random.split(own_key, FRAMES * NBF))
    offsets = jnp.concatenate([jnp.zeros((FRAMES * NBF, 1), jnp.int32), shuffled[:, :C0 - 1].astype(jnp.int32) + 1], axis=1)
    block_index = jnp.tile(jnp.arange(NBF, dtype=jnp.int32), FRAMES)
    own_group = ((block_index[:, None] + offsets) % NBF).reshape(FRAMES, NBF, C0)
    pieces = [own_group]
    settings = ((C1, U1), (C1, U1), (C2, U2), (C2, U2), (C3, U3), (C3, U3))
    for number, setting in enumerate(settings):
        slot_count, union_size = setting
        group_key = jax.random.fold_in(key, 10 + number)
        union_key = jax.random.fold_in(group_key, 1)
        order_key = jax.random.fold_in(group_key, 2)
        unions = jax.vmap(lambda single: jax.random.permutation(single, NBF))(jax.random.split(union_key, FRAMES))[:, :union_size]
        orders = jax.vmap(lambda single: jax.random.permutation(single, NBF))(jax.random.split(order_key, FRAMES))
        places = (orders[:, :, None] + jnp.arange(slot_count, dtype=jnp.int32)[None, None, :]) % union_size
        picks = jnp.take_along_axis(unions[:, None, :], places.reshape(FRAMES, 1, NBF * slot_count), axis=2)
        pieces.append(picks.reshape(FRAMES, NBF, slot_count).astype(jnp.int32))
    return jnp.concatenate(pieces, axis=2).astype(jnp.int32)


def block_levels(key, extent, cuts, least, largest):
    factor_of = 1.0
    for axis_at, shards_of in cuts:
        steps = jax.random.uniform(jax.random.fold_in(jax.random.fold_in(key, 6), axis_at), (shards_of,), jnp.float32, least / len(cuts), largest / len(cuts))
        factor_of = factor_of * jnp.repeat(jnp.exp(steps), extent[axis_at] // shards_of).reshape((-1,) + (1,) * (len(extent) - 1 - axis_at))
    return factor_of


def bell_draw(key, shape, scale, most, cuts=(), kind=jnp.bfloat16):
    drawn = scale * jax.random.normal(key, shape, jnp.float32)
    if cuts:
        drawn = drawn * block_levels(key, shape, cuts, -0.22, 0.18)
    return jnp.clip(drawn, -most, most).astype(kind)


def setup_inputs(seed: int = 0, part: int = 0) -> dict:
    arg_keys = jax.random.split(jax.random.key(seed), 5)
    part_splits = jax.random.split(jax.random.fold_in(arg_keys[4], part), 5)
    return {
        "queries": draw_queries(jax.random.fold_in(jax.random.fold_in(arg_keys[4], part), 71), part),
        "key_rows": draw_key_rows(jax.random.fold_in(jax.random.fold_in(arg_keys[4], part), 71), part),
        "value_rows": bell_draw(part_splits[2], (TOKENS, HEADS * DH), 1.0, 6.0, ((0, 8), (1, 2))),
        "block_lists": draw_block_lists(jax.random.fold_in(jax.random.fold_in(arg_keys[4], part), 71), part),
    }


def slot_groups(blocks):
    near_count = max(blocks // 2, 1)
    middle_count = max(blocks // 4, 1)
    far_count = max(blocks // 8, 1)
    listing = [(0, near_count, blocks)]
    for step_size, slot_count, union_size in ((1, near_count, blocks), (2, middle_count, max(blocks // 2, 1)), (4, far_count, max(blocks // 4, 1))):
        listing.append((-step_size, slot_count, union_size))
        listing.append((step_size, slot_count, union_size))
    result = []
    slot_start = 0
    for frame_step, slot_count, union_size in listing:
        result.append((frame_step, slot_start, slot_count, union_size))
        slot_start = slot_start + slot_count
    return result


def reference(queries, key_rows, value_rows, block_lists):
    scale = DH ** -0.5
    groups_info = slot_groups(NBF)
    query_blocks = queries.reshape(FRAMES, NBF, BLOCK, HEADS, DH)
    key_blocks = key_rows.reshape(FRAMES, NBF, BLOCK, HEADS, DH)
    value_blocks = value_rows.reshape(FRAMES, NBF, BLOCK, HEADS, DH)

    def one_frame(frame):
        lists = lax.dynamic_index_in_dim(block_lists, frame, 0, keepdims=False)
        own_queries = lax.dynamic_index_in_dim(query_blocks, frame, 0, keepdims=False)
        picked_keys = []
        picked_values = []
        masks = []
        for frame_step, slot_start, slot_count, union_size in groups_info:
            target = frame + frame_step
            inside = (target >= 0) & (target < FRAMES)
            clipped = jnp.clip(target, 0, FRAMES - 1).astype(jnp.int32)
            frame_keys = lax.dynamic_index_in_dim(key_blocks, clipped, 0, keepdims=False)
            frame_values = lax.dynamic_index_in_dim(value_blocks, clipped, 0, keepdims=False)
            chosen = lists[:, slot_start:slot_start + slot_count]
            picked_keys.append(frame_keys[chosen].reshape(NBF, slot_count * BLOCK, HEADS, DH))
            picked_values.append(frame_values[chosen].reshape(NBF, slot_count * BLOCK, HEADS, DH))
            masks.append(jnp.broadcast_to(inside, (slot_count * BLOCK,)))
        keys_all = jnp.concatenate(picked_keys, axis=1)
        values_all = jnp.concatenate(picked_values, axis=1)
        mask_all = jnp.concatenate(masks, axis=0)
        scores = jnp.einsum('bqhd,bkhd->bhqk', own_queries.astype(jnp.float32), keys_all.astype(jnp.float32)) * scale
        scores = jnp.where(mask_all[None, None, None, :], scores, -jnp.inf)
        peak = jnp.max(scores, axis=3, keepdims=True)
        weights = jnp.exp(scores - peak)
        total = jnp.sum(weights, axis=3)
        rounded = lax.optimization_barrier(weights.astype(jnp.bfloat16))
        numer = jnp.einsum('bhqk,bkhd->bqhd', rounded.astype(jnp.float32), values_all.astype(jnp.float32))
        output = numer / jnp.transpose(total, (0, 2, 1))[..., None]
        return output.astype(jnp.bfloat16).reshape(FRAME_TOK, HEADS * DH)

    result = lax.map(one_frame, jnp.arange(FRAMES, dtype=jnp.int32))
    return result.reshape(TOKENS, HEADS * DH)
```

```python
import functools

import jax
import jax.numpy as jnp
from jax import lax
from jax.experimental import pallas as pl
from jax.experimental.pallas import tpu as pltpu
from jax.sharding import PartitionSpec as P

DH = 128
BLOCK = 128
MESH = pl.DeviceIdType.MESH
LOG2E = 1.4426950408889634


def group_table(blocks):
    near, middle, far = max(blocks // 2, 1), max(blocks // 4, 1), max(blocks // 8, 1)
    table = {0: (0, near, blocks)}
    start = near
    for step, count, union in (
        (1, near, blocks),
        (2, middle, max(blocks // 2, 1)),
        (4, far, max(blocks // 4, 1)),
    ):
        table[-step] = (start, count, union)
        table[step] = (start + count, count, union)
        start += 2 * count
    return table


def kernel(
    frames, blocks, q, k, v, lists_v, out,
    lists_s, qb, own, near, pick2, mid, pick2v, midv, pick4, far, heard, ob, peak, total, numer, held, stage, stage_sem,
    loc_sem, xs, xr, zs, zr, ms, mr, fs, fr, ls, lr, os_, or_,
):
    f = lax.axis_index("tm")
    s = lax.axis_index("space")
    width = qb.shape[2]
    heads = width // DH
    table = group_table(blocks)
    use_far = frames > 4
    scale = DH ** -0.5

    def cols(i):
        return pl.ds(pl.multiple_of(i * width, width), width)

    def at(step):
        return {"tm": f + step}

    def exists(step):
        return (f + step >= 0) & (f + step < frames)

    steps = (-1, 1) + ((-4, 4) if use_far else ())

    local = [
        pltpu.make_async_copy(q.at[:, cols(s)], qb.at[s], loc_sem.at[0]),
        pltpu.make_async_copy(k.at[:, cols(s)], own.at[0, s], loc_sem.at[1]),
        pltpu.make_async_copy(v.at[:, cols(s)], own.at[1, s], loc_sem.at[2]),
        pltpu.make_async_copy(lists_v, lists_s, loc_sem.at[3]),
    ]
    for t in range(3):
        for o in range(1, blocks):
            local.append(pltpu.make_async_copy(
                (k, v, q)[t].at[:, cols(lax.rem(s + o, blocks))], stage.at[t, o], stage_sem.at[t, o]
            ))
    for copy in local:
        copy.start()

    barrier = pltpu.get_barrier_semaphore()
    for o in range(1, blocks):
        pl.semaphore_signal(
            barrier, inc=1, device_id={"space": lax.rem(s + o, blocks)}, device_id_type=MESH
        )
    greeted = blocks - 1
    for step in steps:

        @pl.when(exists(step))
        def _(step=step):
            pl.semaphore_signal(barrier, inc=1, device_id=at(step), device_id_type=MESH)

        greeted = greeted + exists(step).astype(jnp.int32)
    for copy in local:
        copy.wait()
    pl.semaphore_wait(barrier, greeted)

    def list_copy(i, step):
        return pltpu.make_async_remote_copy(
            src_ref=lists_v, dst_ref=heard.at[i ^ 1], send_sem=ls.at[i], recv_sem=lr.at[i ^ 1],
            device_id=at(step), device_id_type=MESH,
        )

    def list_wait(i):
        return pltpu.make_async_remote_copy(
            src_ref=lists_v, dst_ref=heard.at[i], send_sem=ls.at[i], recv_sem=lr.at[i],
            device_id=at(steps[i]), device_id_type=MESH,
        )

    def x_copy(t, o):
        to = lax.rem(s + o, blocks)
        src = stage.at[t, o]
        dst = qb.at[s] if t == 2 else own.at[t, s]
        return pltpu.make_async_remote_copy(
            src_ref=src, dst_ref=dst, send_sem=xs.at[t, o], recv_sem=xr.at[t, o],
            device_id={"space": to}, device_id_type=MESH,
        )

    def z_copy(side, t, o):
        b = lax.rem(s - o + blocks, blocks)
        src = own.at[t, b]
        return pltpu.make_async_remote_copy(
            src_ref=src, dst_ref=near.at[side, t, b], send_sem=zs.at[side, t, o],
            recv_sem=zr.at[side, t, o], device_id=at(1 - 2 * side), device_id_type=MESH,
        )

    def m_copy(side, h):
        src, dst = (pick2.at[side], mid.at[side]) if h < 0 else (pick2v.at[side, h], midv.at[side, h])
        return pltpu.make_async_remote_copy(
            src_ref=src, dst_ref=dst, send_sem=ms.at[side, h + 1],
            recv_sem=mr.at[side, h + 1], device_id=at(1 - 2 * side), device_id_type=MESH,
        )

    def f_copy(side, t):
        return pltpu.make_async_remote_copy(
            src_ref=pick4.at[side, t], dst_ref=far.at[side, t], send_sem=fs.at[side, t],
            recv_sem=fr.at[side, t], device_id=at(4 - 8 * side), device_id_type=MESH,
        )

    def ahead(side):
        return exists(1 - 2 * side)

    def behind(side):
        return exists(2 * side - 1)

    for t in (0, 1):
        for o in range(1, blocks):
            x_copy(t, o).start()
        for side in (0, 1):

            @pl.when(ahead(side))
            def _(side=side, t=t):
                z_copy(side, t, 0).start()

    for i, step in enumerate(steps):

        @pl.when(exists(step))
        def _(i=i, step=step):
            list_copy(i, step).start()

    for t in (0, 1):
        for o in range(1, blocks):
            x_copy(t, o).wait_recv()
            for side in (0, 1):

                @pl.when(ahead(side))
                def _(side=side, t=t, o=o):
                    z_copy(side, t, o).start()

    for o in range(1, blocks):
        x_copy(2, o).start()

    def choose(i, distance, load, store):
        first, count, union = table[distance]
        seen, rank = [], []
        before = jnp.zeros((1, 1), jnp.int32)
        for c in range(blocks):
            hit = jnp.zeros((1, 1), jnp.int32)
            for b in range(blocks):
                for j in range(first, first + count):
                    hit = jnp.maximum(hit, (heard[i, b : b + 1, j : j + 1] == c).astype(jnp.int32))
            seen.append(hit)
            rank.append(before)
            before = before + hit
        for u in range(union):
            value = load(blocks - 1).astype(jnp.float32)
            for c in range(blocks - 1):
                mask = jnp.where(rank[c] == u, seen[c], 0)
                mask = jnp.broadcast_to(mask, value.shape)
                value = jnp.where(mask == 1, load(c).astype(jnp.float32), value)
            store(u, value.astype(jnp.bfloat16))

    def place(b, slot, distance):
        first, count, union = table[distance]
        number = lists_s[b, slot]
        if union == blocks:
            return number
        if union == 1:
            return 0
        position = jnp.int32(0)
        for c in range(blocks - 1):
            seen = jnp.int32(0)
            for other in range(blocks):
                for j in range(first, first + count):
                    seen = jnp.maximum(seen, (lists_s[other, j] == c).astype(jnp.int32))
            position = position + jnp.where(c < number, seen, 0)
        return position

    def attend(distance, keys, values, fresh=False):
        first, count, union = table[distance]
        for b in range(blocks):
            for j in range(count):
                n = place(b, first + j, distance)
                for h in range(heads):
                    cut = slice(h * DH, (h + 1) * DH)
                    scores = lax.dot_general(
                        qb[b, :, cut], keys(n, cut), (((1,), (1,)), ((), ())),
                        preferred_element_type=jnp.float32,
                    ) * scale
                    top = jnp.max(scores, axis=1, keepdims=True)
                    if fresh and j == 0:
                        weights = jnp.exp(scores - top)
                        peak[b, h] = jnp.broadcast_to(top, (BLOCK, DH))
                        total[b, h] = jnp.broadcast_to(
                            jnp.sum(weights, axis=1, keepdims=True), (BLOCK, DH)
                        )
                        numer[b, h] = jnp.dot(
                            weights.astype(jnp.bfloat16), values(n, cut),
                            preferred_element_type=jnp.float32,
                        )
                    else:
                        old = peak[b, h]
                        new = jnp.maximum(old, jnp.broadcast_to(top, (BLOCK, DH)))
                        fade = jnp.exp(old - new)
                        weights = jnp.exp(scores - new)
                        peak[b, h] = new
                        total[b, h] = total[b, h] * fade + jnp.broadcast_to(
                            jnp.sum(weights, axis=1, keepdims=True), (BLOCK, DH)
                        )
                        numer[b, h] = numer[b, h] * fade + jnp.dot(
                            weights.astype(jnp.bfloat16), values(n, cut),
                            preferred_element_type=jnp.float32,
                        )

    if use_far:
        for side in (0, 1):

            @pl.when(exists(4 - 8 * side))
            def _(side=side):
                i = 3 - side
                list_wait(i).wait_recv()
                for t in (0, 1):
                    choose(
                        i, -4 if side == 0 else 4,
                        lambda c: own[t, c],
                        lambda u, x: pick4.__setitem__((side, t, u), x),
                    )
                    f_copy(side, t).start()

    for i in (0, 1):

        @pl.when(exists(steps[i]))
        def _(i=i):
            list_wait(i).wait_recv()

    for side in (0, 1):

        @pl.when(behind(side))
        def _(side=side):
            for o in range(blocks):
                z_copy(side, 0, o).wait_recv()

        @pl.when(behind(side) & ahead(side))
        def _(side=side):
            choose(
                1 - side, -2 if side == 0 else 2,
                lambda c: near[side, 0, c],
                lambda u, x: pick2.__setitem__((side, u), x),
            )
            m_copy(side, -1).start()

    for o in range(1, blocks):
        x_copy(2, o).wait_recv()
    attend(0, lambda n, cut: own[0, n, :, cut], lambda n, cut: own[1, n, :, cut], fresh=True)

    for side in (0, 1):

        @pl.when(behind(side))
        def _(side=side):
            for o in range(blocks):
                z_copy(side, 1, o).wait_recv()

        @pl.when(behind(side) & ahead(side))
        def _(side=side):
            for h in range(heads):
                choose(
                    1 - side, -2 if side == 0 else 2,
                    lambda c: near[side, 1, c, :, h * DH : (h + 1) * DH],
                    lambda u, x: pick2v.__setitem__((side, h, u), x),
                )
                m_copy(side, h).start()

    for side in (0, 1):

        @pl.when(behind(side))
        def _(side=side):
            attend(
                -1 if side == 0 else 1,
                lambda n, cut: near[side, 0, n, :, cut], lambda n, cut: near[side, 1, n, :, cut],
            )

    if use_far:
        for side in (0, 1):

            @pl.when(exists(8 * side - 4))
            def _(side=side):
                for t in (0, 1):
                    f_copy(side, t).wait_recv()
                attend(
                    -4 if side == 0 else 4,
                    lambda n, cut: far[side, 0, n, :, cut], lambda n, cut: far[side, 1, n, :, cut],
                )

    for side in (0, 1):

        @pl.when(exists(4 * side - 2))
        def _(side=side):
            m_copy(side, -1).wait_recv()

    def mid_scores(b, h, side, j):
        distance = -2 if side == 0 else 2
        cut = slice(h * DH, (h + 1) * DH)
        n = place(b, table[distance][0] + j, distance)
        return lax.dot_general(
            qb[b, :, cut], mid[side, n, :, cut], (((1,), (1,)), ((), ())),
            preferred_element_type=jnp.float32,
        ) * scale

    def mid_weights(sides):
        slots = [(side, j) for side in sides for j in range(table[2][1])]
        for b in range(blocks):
            for h in range(heads):
                scores = [mid_scores(b, h, side, j) for side, j in slots]
                old = peak[b, h]
                new = old
                for x in scores:
                    top = jnp.max(x, axis=1, keepdims=True)
                    new = jnp.maximum(new, jnp.broadcast_to(top, (BLOCK, DH)))
                fade = jnp.exp(old - new)
                whole = total[b, h] * fade
                for (side, j), x in zip(slots, scores):
                    weights = jnp.exp(x - new)
                    whole = whole + jnp.broadcast_to(
                        jnp.sum(weights, axis=1, keepdims=True), (BLOCK, DH)
                    )
                    held[side, j, b, h] = weights.astype(jnp.bfloat16)
                total[b, h] = 1.0 / whole
                numer[b, h] = numer[b, h] * fade

    def o_copy(o, h):
        to = lax.rem(s + o, blocks)
        return pltpu.make_async_remote_copy(
            src_ref=ob.at[to, h], dst_ref=out.at[:, head_cols(s, h)],
            send_sem=os_.at[o, h], recv_sem=or_.at[o, h],
            device_id={"space": to}, device_id_type=MESH,
        )

    def head_cols(i, h):
        return pl.ds(pl.multiple_of(i * width + h * DH, DH), DH)

    def keep(h):
        return pltpu.make_async_copy(ob.at[s, h], out.at[:, head_cols(s, h)], os_.at[0, h])

    def finish(sides):
        for h in range(heads):
            for side in sides:
                m_copy(side, h).wait_recv()
            for o in list(range(1, blocks)) + [0]:
                b = lax.rem(s + o, blocks)
                value = numer[b, h]
                for side in sides:
                    distance = -2 if side == 0 else 2
                    for j in range(table[2][1]):
                        n = place(b, table[distance][0] + j, distance)
                        value = value + jnp.dot(
                            held[side, j, b, h], midv[side, h, n],
                            preferred_element_type=jnp.float32,
                        )
                ob[b, h] = (value * total[b, h]).astype(jnp.bfloat16)
                if o:
                    o_copy(o, h).start()
                else:
                    keep(h).start()

    def last(sides):
        mid_weights(sides)
        finish(sides)

    pl.when(exists(-2) & exists(2))(lambda: last((0, 1)))
    pl.when(exists(-2) & ~exists(2))(lambda: last((0,)))
    pl.when(~exists(-2) & exists(2))(lambda: last((1,)))
    pl.when(~exists(-2) & ~exists(2))(lambda: last(()))

    for t in (0, 1, 2):
        for o in range(1, blocks):
            x_copy(t, o).wait_send()
    for i, step in enumerate(steps):

        @pl.when(exists(step))
        def _(i=i, step=step):
            list_copy(i, step).wait_send()

    for side in (0, 1):

        @pl.when(ahead(side))
        def _(side=side):
            for t in (0, 1):
                for o in range(blocks):
                    z_copy(side, t, o).wait_send()

        @pl.when(behind(side) & ahead(side))
        def _(side=side):
            for h in range(-1, heads):
                m_copy(side, h).wait_send()

        if use_far:

            @pl.when(exists(4 - 8 * side))
            def _(side=side):
                for t in (0, 1):
                    f_copy(side, t).wait_send()

    for h in range(heads):
        keep(h).wait()
        for o in range(1, blocks):
            o_copy(o, h).wait_send()
            pltpu.make_async_remote_copy(
                src_ref=ob.at[s, h], dst_ref=out.at[:, head_cols(lax.rem(s - o + blocks, blocks), h)],
                send_sem=os_.at[o, h], recv_sem=or_.at[o, h],
                device_id={"space": lax.rem(s + o, blocks)}, device_id_type=MESH,
            ).wait_recv()


def local(frames, blocks, queries, key_rows, value_rows, block_lists):
    rows, columns = queries.shape
    width = columns // blocks
    heads = width // DH
    lists = block_lists[0]
    table = group_table(blocks)
    u2, u4 = table[2][2], table[4][2]
    far_rows = BLOCK if frames > 4 else 16
    dma = pltpu.SemaphoreType.DMA
    bf = jnp.bfloat16
    return pl.pallas_call(
        functools.partial(kernel, frames, blocks),
        out_shape=jax.ShapeDtypeStruct(queries.shape, queries.dtype),
        in_specs=[pl.BlockSpec(memory_space=pltpu.HBM)] * 4,
        out_specs=pl.BlockSpec(memory_space=pl.ANY),
        scratch_shapes=[
            pltpu.SMEM(lists.shape, jnp.int32),
            pltpu.VMEM((blocks, BLOCK, width), bf),
            pltpu.VMEM((2, blocks, BLOCK, width), bf),
            pltpu.VMEM((2, 2, blocks, BLOCK, width), bf),
            pltpu.VMEM((2, u2, BLOCK, width), bf),
            pltpu.VMEM((2, u2, BLOCK, width), bf),
            pltpu.VMEM((2, heads, u2, BLOCK, DH), bf),
            pltpu.VMEM((2, heads, u2, BLOCK, DH), bf),
            pltpu.VMEM((2, 2, u4, far_rows, width), bf),
            pltpu.VMEM((2, 2, u4, far_rows, width), bf),
            pltpu.VMEM((4,) + lists.shape, jnp.int32),
            pltpu.VMEM((blocks, heads, BLOCK, DH), bf),
            pltpu.VMEM((blocks, heads, BLOCK, DH), jnp.float32),
            pltpu.VMEM((blocks, heads, BLOCK, DH), jnp.float32),
            pltpu.VMEM((blocks, heads, BLOCK, DH), jnp.float32),
            pltpu.VMEM((2, table[2][1], blocks, heads, BLOCK, DH), bf),
            pltpu.VMEM((3, blocks, BLOCK, width), bf),
            dma((3, blocks)),
            dma((5,)),
            dma((3, blocks)),
            dma((3, blocks)),
            dma((2, 2, blocks)),
            dma((2, 2, blocks)),
            dma((2, 1 + heads)),
            dma((2, 1 + heads)),
            dma((2, 2)),
            dma((2, 2)),
            dma((4,)),
            dma((4,)),
            dma((blocks, heads)),
            dma((blocks, heads)),
        ],
        compiler_params=pltpu.CompilerParams(
            collective_id=0, has_side_effects=True, vmem_limit_bytes=48 * 1024 * 1024
        ),
    )(*[pltpu.with_memory_space_constraint(x, pltpu.HBM) for x in (queries, key_rows, value_rows, lists)])


def short_kernel(
    frames, blocks, q, k, v, lists_v, out,
    qh, kh, vh, kv, xq, qn, mid, pick, held, rt, po, ps, pin, lin, own_o, own_l, heard,
    loc_sem, xs, xr, qs, qr, ks, kr, ps_, pr, ss, sr, ls, lr,
):
    f = lax.axis_index("tm")
    s = lax.axis_index("space")
    other = 1 - s
    width = qn.shape[3]
    heads = width // DH
    table = group_table(blocks)
    factor = DH ** -0.5 * LOG2E
    sides = (0, 1)

    def exists(step):
        return (f + step >= 0) & (f + step < frames)

    def step(side):
        return 2 * side - 1

    def ex(side):
        return exists(step(side))

    def half(i):
        return pl.ds(pl.multiple_of(i * width, width), width)

    def head_of(i, h):
        return pl.ds(pl.multiple_of(i * width + h * DH, DH), DH)

    def cut(h):
        return slice(h * DH, (h + 1) * DH)

    def remote(src, dst, send, recv, **where):
        return pltpu.make_async_remote_copy(
            src_ref=src, dst_ref=dst, send_sem=send, recv_sem=recv,
            device_id=where, device_id_type=MESH,
        )

    local = [
        pltpu.make_async_copy(q, qh, loc_sem.at[0]),
        pltpu.make_async_copy(k, kh, loc_sem.at[1]),
        pltpu.make_async_copy(v, vh, loc_sem.at[2]),
    ]
    for t in (0, 1):
        for h in range(heads):
            local.append(pltpu.make_async_copy(
                (k, v)[t].at[:, head_of(s, h)], kv[t][h].at[s], loc_sem.at[3 + t * heads + h]
            ))
    for copy in local:
        copy.start()

    barrier = pltpu.get_barrier_semaphore()
    pl.semaphore_signal(barrier, inc=1, device_id={"space": other}, device_id_type=MESH)
    greeted = jnp.int32(1)
    for d in (-2, -1, 1, 2):

        @pl.when(exists(d))
        def _(d=d):
            pl.semaphore_signal(barrier, inc=1, device_id={"tm": f + d}, device_id_type=MESH)
            if abs(d) == 1:
                pl.semaphore_signal(
                    barrier, inc=1, device_id={"tm": f + d, "space": other}, device_id_type=MESH
                )

        greeted = greeted + exists(d).astype(jnp.int32) * (2 if abs(d) == 1 else 1)
    pl.semaphore_wait(barrier, greeted)

    def list_copy(i, d):
        return remote(lists_v, heard.at[i ^ 1], ls.at[i], lr.at[i ^ 1], tm=f + d)

    def list_wait(i, d):
        return remote(lists_v, heard.at[i], ls.at[i], lr.at[i], tm=f + d)

    list_steps = (-1, 1, -2, 2)

    def x_copy(t, h):
        src = (q, k, v)[t].at[:, head_of(other, h)]
        dst = xq.at[h] if t == 0 else kv[t - 1][h].at[s]
        return remote(src, dst, xs.at[t, h], xr.at[t, h], space=other)

    def x_wait(t, h):
        src = (q, k, v)[t].at[:, head_of(other, h)]
        dst = xq.at[h] if t == 0 else kv[t - 1][h].at[other]
        return remote(src, dst, xs.at[t, h], xr.at[t, h], space=other)

    def q_copy(side, i):
        far = 1 - side
        if i == 0:
            return remote(
                q.at[:, half(s)], qn.at[far, s], qs.at[side, i], qr.at[far, i], tm=f + step(side)
            )
        return remote(
            xq.at[i - 1], qn.at[far, other, :, cut(i - 1)], qs.at[side, i], qr.at[far, i],
            tm=f + step(side),
        )

    def q_wait(side, i):
        if i == 0:
            return remote(
                q.at[:, half(s)], qn.at[side, s], qs.at[side, i], qr.at[side, i], tm=f + step(side)
            )
        return remote(
            xq.at[i - 1], qn.at[side, other, :, cut(i - 1)], qs.at[side, i], qr.at[side, i],
            tm=f + step(side),
        )

    def k_copy(side, t, h):
        far = 1 - side
        return remote(
            pick.at[side, t, :, cut(h)], mid.at[far, t, :, cut(h)], ks.at[side, t, h],
            kr.at[far, t, h], tm=f + step(side),
        )

    def k_wait(side, t, h):
        return remote(
            pick.at[side, t, :, cut(h)], mid.at[side, t, :, cut(h)], ks.at[side, t, h],
            kr.at[side, t, h], tm=f + step(side),
        )

    def p_copy(side, b, h):
        far = 1 - side
        return remote(
            po.at[side, b, h], pin.at[far, s, h], ps_.at[side, b, h], pr.at[far, s, h],
            tm=f + step(side), space=b,
        )

    def p_wait(side, i, h):
        return remote(
            po.at[side, i, h], pin.at[side, i, h], ps_.at[side, i, h], pr.at[side, i, h],
            tm=f + step(side), space=i,
        )

    def s_copy(side, b):
        far = 1 - side
        return remote(
            ps.at[side, b], lin.at[far, s], ss.at[side, b], sr.at[far, s],
            tm=f + step(side), space=b,
        )

    def s_wait(side, i):
        return remote(
            ps.at[side, i], lin.at[side, i], ss.at[side, i], sr.at[side, i],
            tm=f + step(side), space=i,
        )

    for i, d in enumerate(list_steps):

        @pl.when(exists(d))
        def _(i=i, d=d):
            list_copy(i, d).start()

    for side in sides:

        @pl.when(ex(side))
        def _(side=side):
            q_copy(side, 0).start()

    for t in range(3):
        for h in range(heads):
            x_copy(t, h).start()

    for copy in local:
        copy.wait()

    def scores(keys, queries):
        return lax.dot_general(
            keys, queries, (((1,), (1,)), ((), ())), preferred_element_type=jnp.float32
        ) * factor

    def gathered(values, weights):
        return lax.dot_general(
            values, weights, (((0,), (0,)), ((), ())), preferred_element_type=jnp.float32
        )

    def home(n):
        x = scores(kh[:, cut(n)], qh[:, cut(n)])
        top = jnp.max(x, axis=0, keepdims=True)
        weights = jnp.exp2(x - top)
        whole = jnp.sum(weights, axis=0, keepdims=True)
        own_o[n] = gathered(vh[:, cut(n)], weights.astype(jnp.bfloat16)) * (1.0 / whole)
        own_l[n : n + 1] = top + jnp.log2(whole)

    for h in range(heads):
        home(h)
        x_wait(0, h).wait_recv()
        for side in sides:

            @pl.when(ex(side))
            def _(side=side, h=h):
                q_copy(side, 1 + h).start()

    for i, d in enumerate(list_steps):

        @pl.when(exists(d))
        def _(i=i, d=d):
            list_wait(i, d).wait_recv()

    def send_pick(t, h):
        x_wait(1 + t, h).wait_recv()
        for side in sides:
            d = 2 * step(side)

            @pl.when(exists(d))
            def _(side=side, d=d):
                n = heard[2 + side, 0, table[-d][0]]
                pick[side, t, :, cut(h)] = kv[t][h][n]
                k_copy(side, t, h).start()

    def near_block(side, b):
        return heard[side, b, table[-step(side)][0]]

    def weigh(side, h, both):
        for b in range(blocks):
            queries = qn[side, b, :, cut(h)]
            x = [scores(kv[0][h][near_block(side, b)], queries)]
            if both:
                x.append(scores(mid[1 - side, 0, :, cut(h)], queries))
            top = jnp.max(x[0], axis=0, keepdims=True)
            for y in x[1:]:
                top = jnp.maximum(top, jnp.max(y, axis=0, keepdims=True))
            whole = jnp.zeros_like(top)
            for j, y in enumerate(x):
                weights = jnp.exp2(y - top)
                whole = whole + jnp.sum(weights, axis=0, keepdims=True)
                held[side, b, h, j] = weights.astype(jnp.bfloat16)
            rt[side, b, h : h + 1] = 1.0 / whole
            ps[side, b, h : h + 1] = top + jnp.log2(whole)

    def answer(side, h, both):
        for b in range(blocks):
            value = gathered(kv[1][h][near_block(side, b)], held[side, b, h, 0])
            if both:
                value = value + gathered(mid[1 - side, 1, :, cut(h)], held[side, b, h, 1])
            po[side, b, h] = (value * rt[side, b, h : h + 1]).astype(jnp.bfloat16)
            p_copy(side, b, h).start()

    def serve(work, t, h):
        for side in sides:

            @pl.when(ex(side) & ex(1 - side))
            def _(side=side):
                k_wait(side, t, h).wait_recv()

        @pl.when(ex(0) & ex(1))
        def _():
            for side in sides:
                work(side, h, True)

        for side in sides:

            @pl.when(ex(side) & ~ex(1 - side))
            def _(side=side):
                work(side, h, False)

    for h in range(heads):
        send_pick(0, h)
        home(heads + h)
    for side in sides:

        @pl.when(ex(side))
        def _(side=side):
            for i in range(1 + heads):
                q_wait(side, i).wait_recv()

    for h in range(heads):
        send_pick(1, h)
        serve(weigh, 0, h)
    for side in sides:

        @pl.when(ex(side))
        def _(side=side):
            for b in range(blocks):
                s_copy(side, b).start()

    for h in range(heads):
        serve(answer, 1, h)

    for side in sides:

        @pl.when(ex(side))
        def _(side=side):
            for i in range(blocks):
                s_wait(side, i).wait_recv()

    def merge(n, parts):
        i, h = n // heads, n % heads
        rows = [own_l[n : n + 1]] + [lin[side, i, h : h + 1] for side in parts]
        top = functools.reduce(jnp.maximum, rows)
        shares = [jnp.exp2(row - top) for row in rows]
        scale = 1.0 / functools.reduce(jnp.add, shares)
        value = own_o[n] * (shares[0] * scale)
        for side, share in zip(parts, shares[1:]):
            value = value + pin[side, i, h].astype(jnp.float32) * (share * scale)
        out[:, cut(n)] = value.T.astype(jnp.bfloat16)

    for h in range(heads):
        for i in range(blocks):
            for side in sides:

                @pl.when(ex(side))
                def _(side=side):
                    p_wait(side, i, h).wait_recv()

            n = i * heads + h
            pl.when(ex(0) & ex(1))(lambda: merge(n, (0, 1)))
            pl.when(ex(0) & ~ex(1))(lambda: merge(n, (0,)))
            pl.when(~ex(0) & ex(1))(lambda: merge(n, (1,)))
            pl.when(~ex(0) & ~ex(1))(lambda: merge(n, ()))

    for t in range(3):
        for h in range(heads):
            x_copy(t, h).wait_send()
    for i, d in enumerate(list_steps):

        @pl.when(exists(d))
        def _(i=i, d=d):
            list_copy(i, d).wait_send()

    for side in sides:

        @pl.when(ex(side))
        def _(side=side):
            for i in range(1 + heads):
                q_copy(side, i).wait_send()
            for b in range(blocks):
                s_copy(side, b).wait_send()
                for h in range(heads):
                    p_copy(side, b, h).wait_send()

        @pl.when(exists(2 * step(side)))
        def _(side=side):
            for t in (0, 1):
                for h in range(heads):
                    k_copy(side, t, h).wait_send()


def short(frames, blocks, queries, key_rows, value_rows, block_lists):
    rows, columns = queries.shape
    width = columns // blocks
    heads = width // DH
    lists = block_lists[0]
    dma = pltpu.SemaphoreType.DMA
    bf, f32 = jnp.bfloat16, jnp.float32
    vmem = pltpu.VMEM
    return pl.pallas_call(
        functools.partial(short_kernel, frames, blocks),
        out_shape=jax.ShapeDtypeStruct(queries.shape, queries.dtype),
        in_specs=[pl.BlockSpec(memory_space=pltpu.HBM)] * 4,
        out_specs=pl.BlockSpec(memory_space=pltpu.VMEM),
        scratch_shapes=[
            vmem((rows, columns), bf),
            vmem((rows, columns), bf),
            vmem((rows, columns), bf),
            [[vmem((blocks, BLOCK, DH), bf)] * heads] * 2,
            vmem((heads, BLOCK, DH), bf),
            vmem((2, blocks, BLOCK, width), bf),
            vmem((2, 2, BLOCK, width), bf),
            vmem((2, 2, BLOCK, width), bf),
            vmem((2, blocks, heads, 2, BLOCK, BLOCK), bf),
            vmem((2, blocks, 8, BLOCK), f32),
            vmem((2, blocks, heads, DH, BLOCK), bf),
            vmem((2, blocks, 8, BLOCK), f32),
            vmem((2, blocks, heads, DH, BLOCK), bf),
            vmem((2, blocks, 8, BLOCK), f32),
            vmem((columns // DH, DH, BLOCK), f32),
            vmem((columns // DH, BLOCK), f32),
            pltpu.SMEM((4,) + lists.shape, jnp.int32),
            dma((3 + 2 * heads,)),
            dma((3, heads)),
            dma((3, heads)),
            dma((2, 1 + heads)),
            dma((2, 1 + heads)),
            dma((2, 2, heads)),
            dma((2, 2, heads)),
            dma((2, blocks, heads)),
            dma((2, blocks, heads)),
            dma((2, blocks)),
            dma((2, blocks)),
            dma((4,)),
            dma((4,)),
        ],
        compiler_params=pltpu.CompilerParams(
            collective_id=1, has_side_effects=True, vmem_limit_bytes=48 * 1024 * 1024
        ),
    )(*[pltpu.with_memory_space_constraint(x, pltpu.HBM) for x in (queries, key_rows, value_rows, lists)])


def solution(mesh):
    in_specs = (
        P(("groups", "tm", "space"), "head"),
        P(("groups", "tm", "space"), "head"),
        P(("groups", "tm", "space"), "head"),
        P(("groups", "tm"), None, None),
    )
    out_specs = P(("groups", "tm", "space"), "head")
    frames, blocks = mesh.shape["tm"], mesh.shape["space"]
    body = functools.partial(short if frames <= 4 and blocks == 2 else local, frames, blocks)
    return jax.shard_map(body, mesh=mesh, in_specs=in_specs, out_specs=out_specs, check_vma=False)
```

```python
import functools

import jax
import jax.numpy as jnp
from jax import lax
from jax.experimental import pallas as pl
from jax.experimental.pallas import tpu as pltpu
from jax.sharding import PartitionSpec as P

DH = 128
BLOCK = 128
MESH = pl.DeviceIdType.MESH
LOG2E = 1.4426950408889634


def group_table(blocks):
    near, middle, far = max(blocks // 2, 1), max(blocks // 4, 1), max(blocks // 8, 1)
    table = {0: (0, near, blocks)}
    start = near
    for step, count, union in (
        (1, near, blocks),
        (2, middle, max(blocks // 2, 1)),
        (4, far, max(blocks // 4, 1)),
    ):
        table[-step] = (start, count, union)
        table[step] = (start + count, count, union)
        start += 2 * count
    return table


def kernel(
    frames, blocks, q, k, v, lists_v, out,
    lists_s, qb, own, near, pick2, mid, pick2v, midv, pick4, far, heard, ob, peak, total, numer, held, stage, stage_sem,
    loc_sem, xs, xr, zs, zr, ms, mr, fs, fr, ls, lr, os_, or_,
):
    f = lax.axis_index("tm")
    s = lax.axis_index("space")
    width = qb.shape[2]
    heads = width // DH
    table = group_table(blocks)
    use_far = frames > 4
    scale = DH ** -0.5

    def cols(i):
        return pl.ds(pl.multiple_of(i * width, width), width)

    def at(step):
        return {"tm": f + step}

    def exists(step):
        return (f + step >= 0) & (f + step < frames)

    steps = (-1, 1) + ((-4, 4) if use_far else ())

    local = [
        pltpu.make_async_copy(q.at[:, cols(s)], qb.at[s], loc_sem.at[0]),
        pltpu.make_async_copy(k.at[:, cols(s)], own.at[0, s], loc_sem.at[1]),
        pltpu.make_async_copy(v.at[:, cols(s)], own.at[1, s], loc_sem.at[2]),
        pltpu.make_async_copy(lists_v, lists_s, loc_sem.at[3]),
    ]
    for t in range(3):
        for o in range(1, blocks):
            local.append(pltpu.make_async_copy(
                (k, v, q)[t].at[:, cols(lax.rem(s + o, blocks))], stage.at[t, o], stage_sem.at[t, o]
            ))
    for copy in local:
        copy.start()

    barrier = pltpu.get_barrier_semaphore()
    for o in range(1, blocks):
        pl.semaphore_signal(
            barrier, inc=1, device_id={"space": lax.rem(s + o, blocks)}, device_id_type=MESH
        )
    greeted = blocks - 1
    for step in steps:

        @pl.when(exists(step))
        def _(step=step):
            pl.semaphore_signal(barrier, inc=1, device_id=at(step), device_id_type=MESH)

        greeted = greeted + exists(step).astype(jnp.int32)
    for copy in local:
        copy.wait()
    pl.semaphore_wait(barrier, greeted)

    def list_copy(i, step):
        return pltpu.make_async_remote_copy(
            src_ref=lists_v, dst_ref=heard.at[i ^ 1], send_sem=ls.at[i], recv_sem=lr.at[i ^ 1],
            device_id=at(step), device_id_type=MESH,
        )

    def list_wait(i):
        return pltpu.make_async_remote_copy(
            src_ref=lists_v, dst_ref=heard.at[i], send_sem=ls.at[i], recv_sem=lr.at[i],
            device_id=at(steps[i]), device_id_type=MESH,
        )

    def x_copy(t, o):
        to = lax.rem(s + o, blocks)
        src = stage.at[t, o]
        dst = qb.at[s] if t == 2 else own.at[t, s]
        return pltpu.make_async_remote_copy(
            src_ref=src, dst_ref=dst, send_sem=xs.at[t, o], recv_sem=xr.at[t, o],
            device_id={"space": to}, device_id_type=MESH,
        )

    def z_copy(side, t, o):
        b = lax.rem(s - o + blocks, blocks)
        src = own.at[t, b]
        return pltpu.make_async_remote_copy(
            src_ref=src, dst_ref=near.at[side, t, b], send_sem=zs.at[side, t, o],
            recv_sem=zr.at[side, t, o], device_id=at(1 - 2 * side), device_id_type=MESH,
        )

    def m_copy(side, h):
        src, dst = (pick2.at[side], mid.at[side]) if h < 0 else (pick2v.at[side, h], midv.at[side, h])
        return pltpu.make_async_remote_copy(
            src_ref=src, dst_ref=dst, send_sem=ms.at[side, h + 1],
            recv_sem=mr.at[side, h + 1], device_id=at(1 - 2 * side), device_id_type=MESH,
        )

    def f_copy(side, t):
        return pltpu.make_async_remote_copy(
            src_ref=pick4.at[side, t], dst_ref=far.at[side, t], send_sem=fs.at[side, t],
            recv_sem=fr.at[side, t], device_id=at(4 - 8 * side), device_id_type=MESH,
        )

    def ahead(side):
        return exists(1 - 2 * side)

    def behind(side):
        return exists(2 * side - 1)

    for t in (0, 1):
        for o in range(1, blocks):
            x_copy(t, o).start()
        for side in (0, 1):

            @pl.when(ahead(side))
            def _(side=side, t=t):
                z_copy(side, t, 0).start()

    for i, step in enumerate(steps):

        @pl.when(exists(step))
        def _(i=i, step=step):
            list_copy(i, step).start()

    for t in (0, 1):
        for o in range(1, blocks):
            x_copy(t, o).wait_recv()
            for side in (0, 1):

                @pl.when(ahead(side))
                def _(side=side, t=t, o=o):
                    z_copy(side, t, o).start()

    for o in range(1, blocks):
        x_copy(2, o).start()

    def choose(i, distance, load, store):
        first, count, union = table[distance]
        seen, rank = [], []
        before = jnp.zeros((1, 1), jnp.int32)
        for c in range(blocks):
            hit = jnp.zeros((1, 1), jnp.int32)
            for b in range(blocks):
                for j in range(first, first + count):
                    hit = jnp.maximum(hit, (heard[i, b : b + 1, j : j + 1] == c).astype(jnp.int32))
            seen.append(hit)
            rank.append(before)
            before = before + hit
        for u in range(union):
            value = load(blocks - 1).astype(jnp.float32)
            for c in range(blocks - 1):
                mask = jnp.where(rank[c] == u, seen[c], 0)
                mask = jnp.broadcast_to(mask, value.shape)
                value = jnp.where(mask == 1, load(c).astype(jnp.float32), value)
            store(u, value.astype(jnp.bfloat16))

    def place(b, slot, distance):
        first, count, union = table[distance]
        number = lists_s[b, slot]
        if union == blocks:
            return number
        if union == 1:
            return 0
        position = jnp.int32(0)
        for c in range(blocks - 1):
            seen = jnp.int32(0)
            for other in range(blocks):
                for j in range(first, first + count):
                    seen = jnp.maximum(seen, (lists_s[other, j] == c).astype(jnp.int32))
            position = position + jnp.where(c < number, seen, 0)
        return position

    def attend(distance, keys, values, fresh=False):
        first, count, union = table[distance]
        for b in range(blocks):
            for j in range(count):
                n = place(b, first + j, distance)
                for h in range(heads):
                    cut = slice(h * DH, (h + 1) * DH)
                    scores = lax.dot_general(
                        qb[b, :, cut], keys(n, cut), (((1,), (1,)), ((), ())),
                        preferred_element_type=jnp.float32,
                    ) * scale
                    top = jnp.max(scores, axis=1, keepdims=True)
                    if fresh and j == 0:
                        weights = jnp.exp(scores - top)
                        peak[b, h] = jnp.broadcast_to(top, (BLOCK, DH))
                        total[b, h] = jnp.broadcast_to(
                            jnp.sum(weights, axis=1, keepdims=True), (BLOCK, DH)
                        )
                        numer[b, h] = jnp.dot(
                            weights.astype(jnp.bfloat16), values(n, cut),
                            preferred_element_type=jnp.float32,
                        )
                    else:
                        old = peak[b, h]
                        new = jnp.maximum(old, jnp.broadcast_to(top, (BLOCK, DH)))
                        fade = jnp.exp(old - new)
                        weights = jnp.exp(scores - new)
                        peak[b, h] = new
                        total[b, h] = total[b, h] * fade + jnp.broadcast_to(
                            jnp.sum(weights, axis=1, keepdims=True), (BLOCK, DH)
                        )
                        numer[b, h] = numer[b, h] * fade + jnp.dot(
                            weights.astype(jnp.bfloat16), values(n, cut),
                            preferred_element_type=jnp.float32,
                        )

    if use_far:
        for side in (0, 1):

            @pl.when(exists(4 - 8 * side))
            def _(side=side):
                i = 3 - side
                list_wait(i).wait_recv()
                for t in (0, 1):
                    choose(
                        i, -4 if side == 0 else 4,
                        lambda c: own[t, c],
                        lambda u, x: pick4.__setitem__((side, t, u), x),
                    )
                    f_copy(side, t).start()

    for i in (0, 1):

        @pl.when(exists(steps[i]))
        def _(i=i):
            list_wait(i).wait_recv()

    for side in (0, 1):

        @pl.when(behind(side))
        def _(side=side):
            for o in range(blocks):
                z_copy(side, 0, o).wait_recv()

        @pl.when(behind(side) & ahead(side))
        def _(side=side):
            choose(
                1 - side, -2 if side == 0 else 2,
                lambda c: near[side, 0, c],
                lambda u, x: pick2.__setitem__((side, u), x),
            )
            m_copy(side, -1).start()

    for o in range(1, blocks):
        x_copy(2, o).wait_recv()
    attend(0, lambda n, cut: own[0, n, :, cut], lambda n, cut: own[1, n, :, cut], fresh=True)

    for side in (0, 1):

        @pl.when(behind(side))
        def _(side=side):
            for o in range(blocks):
                z_copy(side, 1, o).wait_recv()

        @pl.when(behind(side) & ahead(side))
        def _(side=side):
            for h in range(heads):
                choose(
                    1 - side, -2 if side == 0 else 2,
                    lambda c: near[side, 1, c, :, h * DH : (h + 1) * DH],
                    lambda u, x: pick2v.__setitem__((side, h, u), x),
                )
                m_copy(side, h).start()

    for side in (0, 1):

        @pl.when(behind(side))
        def _(side=side):
            attend(
                -1 if side == 0 else 1,
                lambda n, cut: near[side, 0, n, :, cut], lambda n, cut: near[side, 1, n, :, cut],
            )

    if use_far:
        for side in (0, 1):

            @pl.when(exists(8 * side - 4))
            def _(side=side):
                for t in (0, 1):
                    f_copy(side, t).wait_recv()
                attend(
                    -4 if side == 0 else 4,
                    lambda n, cut: far[side, 0, n, :, cut], lambda n, cut: far[side, 1, n, :, cut],
                )

    for side in (0, 1):

        @pl.when(exists(4 * side - 2))
        def _(side=side):
            m_copy(side, -1).wait_recv()

    def mid_scores(b, h, side, j):
        distance = -2 if side == 0 else 2
        cut = slice(h * DH, (h + 1) * DH)
        n = place(b, table[distance][0] + j, distance)
        return lax.dot_general(
            qb[b, :, cut], mid[side, n, :, cut], (((1,), (1,)), ((), ())),
            preferred_element_type=jnp.float32,
        ) * scale

    def mid_weights(sides):
        slots = [(side, j) for side in sides for j in range(table[2][1])]
        for b in range(blocks):
            for h in range(heads):
                scores = [mid_scores(b, h, side, j) for side, j in slots]
                old = peak[b, h]
                new = old
                for x in scores:
                    top = jnp.max(x, axis=1, keepdims=True)
                    new = jnp.maximum(new, jnp.broadcast_to(top, (BLOCK, DH)))
                fade = jnp.exp(old - new)
                whole = total[b, h] * fade
                for (side, j), x in zip(slots, scores):
                    weights = jnp.exp(x - new)
                    whole = whole + jnp.broadcast_to(
                        jnp.sum(weights, axis=1, keepdims=True), (BLOCK, DH)
                    )
                    held[side, j, b, h] = weights.astype(jnp.bfloat16)
                total[b, h] = 1.0 / whole
                numer[b, h] = numer[b, h] * fade

    def o_copy(o, h):
        to = lax.rem(s + o, blocks)
        return pltpu.make_async_remote_copy(
            src_ref=ob.at[to, h], dst_ref=out.at[:, head_cols(s, h)],
            send_sem=os_.at[o, h], recv_sem=or_.at[o, h],
            device_id={"space": to}, device_id_type=MESH,
        )

    def head_cols(i, h):
        return pl.ds(pl.multiple_of(i * width + h * DH, DH), DH)

    def keep(h):
        return pltpu.make_async_copy(ob.at[s, h], out.at[:, head_cols(s, h)], os_.at[0, h])

    def finish(sides):
        for h in range(heads):
            for side in sides:
                m_copy(side, h).wait_recv()
            for o in list(range(1, blocks)) + [0]:
                b = lax.rem(s + o, blocks)
                value = numer[b, h]
                for side in sides:
                    distance = -2 if side == 0 else 2
                    for j in range(table[2][1]):
                        n = place(b, table[distance][0] + j, distance)
                        value = value + jnp.dot(
                            held[side, j, b, h], midv[side, h, n],
                            preferred_element_type=jnp.float32,
                        )
                ob[b, h] = (value * total[b, h]).astype(jnp.bfloat16)
                if o:
                    o_copy(o, h).start()
                else:
                    keep(h).start()

    def last(sides):
        mid_weights(sides)
        finish(sides)

    pl.when(exists(-2) & exists(2))(lambda: last((0, 1)))
    pl.when(exists(-2) & ~exists(2))(lambda: last((0,)))
    pl.when(~exists(-2) & exists(2))(lambda: last((1,)))
    pl.when(~exists(-2) & ~exists(2))(lambda: last(()))

    for t in (0, 1, 2):
        for o in range(1, blocks):
            x_copy(t, o).wait_send()
    for i, step in enumerate(steps):

        @pl.when(exists(step))
        def _(i=i, step=step):
            list_copy(i, step).wait_send()

    for side in (0, 1):

        @pl.when(ahead(side))
        def _(side=side):
            for t in (0, 1):
                for o in range(blocks):
                    z_copy(side, t, o).wait_send()

        @pl.when(behind(side) & ahead(side))
        def _(side=side):
            for h in range(-1, heads):
                m_copy(side, h).wait_send()

        if use_far:

            @pl.when(exists(4 - 8 * side))
            def _(side=side):
                for t in (0, 1):
                    f_copy(side, t).wait_send()

    for h in range(heads):
        keep(h).wait()
        for o in range(1, blocks):
            o_copy(o, h).wait_send()
            pltpu.make_async_remote_copy(
                src_ref=ob.at[s, h], dst_ref=out.at[:, head_cols(lax.rem(s - o + blocks, blocks), h)],
                send_sem=os_.at[o, h], recv_sem=or_.at[o, h],
                device_id={"space": lax.rem(s + o, blocks)}, device_id_type=MESH,
            ).wait_recv()


def local(frames, blocks, queries, key_rows, value_rows, block_lists):
    rows, columns = queries.shape
    width = columns // blocks
    heads = width // DH
    lists = block_lists[0]
    table = group_table(blocks)
    u2, u4 = table[2][2], table[4][2]
    far_rows = BLOCK if frames > 4 else 16
    dma = pltpu.SemaphoreType.DMA
    bf = jnp.bfloat16
    return pl.pallas_call(
        functools.partial(kernel, frames, blocks),
        out_shape=jax.ShapeDtypeStruct(queries.shape, queries.dtype),
        in_specs=[pl.BlockSpec(memory_space=pltpu.HBM)] * 4,
        out_specs=pl.BlockSpec(memory_space=pl.ANY),
        scratch_shapes=[
            pltpu.SMEM(lists.shape, jnp.int32),
            pltpu.VMEM((blocks, BLOCK, width), bf),
            pltpu.VMEM((2, blocks, BLOCK, width), bf),
            pltpu.VMEM((2, 2, blocks, BLOCK, width), bf),
            pltpu.VMEM((2, u2, BLOCK, width), bf),
            pltpu.VMEM((2, u2, BLOCK, width), bf),
            pltpu.VMEM((2, heads, u2, BLOCK, DH), bf),
            pltpu.VMEM((2, heads, u2, BLOCK, DH), bf),
            pltpu.VMEM((2, 2, u4, far_rows, width), bf),
            pltpu.VMEM((2, 2, u4, far_rows, width), bf),
            pltpu.VMEM((4,) + lists.shape, jnp.int32),
            pltpu.VMEM((blocks, heads, BLOCK, DH), bf),
            pltpu.VMEM((blocks, heads, BLOCK, DH), jnp.float32),
            pltpu.VMEM((blocks, heads, BLOCK, DH), jnp.float32),
            pltpu.VMEM((blocks, heads, BLOCK, DH), jnp.float32),
            pltpu.VMEM((2, table[2][1], blocks, heads, BLOCK, DH), bf),
            pltpu.VMEM((3, blocks, BLOCK, width), bf),
            dma((3, blocks)),
            dma((5,)),
            dma((3, blocks)),
            dma((3, blocks)),
            dma((2, 2, blocks)),
            dma((2, 2, blocks)),
            dma((2, 1 + heads)),
            dma((2, 1 + heads)),
            dma((2, 2)),
            dma((2, 2)),
            dma((4,)),
            dma((4,)),
            dma((blocks, heads)),
            dma((blocks, heads)),
        ],
        compiler_params=pltpu.CompilerParams(
            collective_id=0, has_side_effects=True, vmem_limit_bytes=48 * 1024 * 1024
        ),
    )(*[pltpu.with_memory_space_constraint(x, pltpu.HBM) for x in (queries, key_rows, value_rows, lists)])


def short_kernel(
    frames, blocks, q, k, v, lists_v, out,
    qh, kh, vh, kv, xq, qn, mid, pick, held, rt, po, ps, pin, lin, own_o, own_l, heard,
    loc_sem, xs, xr, qs, qr, ks, kr, ps_, pr, ss, sr, ls, lr,
):
    f = lax.axis_index("tm")
    s = lax.axis_index("space")
    other = 1 - s
    width = qn.shape[3]
    heads = width // DH
    table = group_table(blocks)
    factor = DH ** -0.5 * LOG2E
    sides = (0, 1)
    early = f < frames // 2

    def exists(step):
        return (f + step >= 0) & (f + step < frames)

    def step(side):
        return 2 * side - 1

    def ex(side):
        return exists(step(side))

    def half(i):
        return pl.ds(pl.multiple_of(i * width, width), width)

    def head_of(i, h):
        return pl.ds(pl.multiple_of(i * width + h * DH, DH), DH)

    def cut(h):
        return slice(h * DH, (h + 1) * DH)

    def remote(src, dst, send, recv, **where):
        return pltpu.make_async_remote_copy(
            src_ref=src, dst_ref=dst, send_sem=send, recv_sem=recv,
            device_id=where, device_id_type=MESH,
        )

    local = [
        pltpu.make_async_copy(q, qh, loc_sem.at[0]),
        pltpu.make_async_copy(k, kh, loc_sem.at[1]),
        pltpu.make_async_copy(v, vh, loc_sem.at[2]),
    ]
    for t in (0, 1):
        for h in range(heads):
            local.append(pltpu.make_async_copy(
                (k, v)[t].at[:, head_of(s, h)], kv[t][h].at[s], loc_sem.at[3 + t * heads + h]
            ))
    for copy in local:
        copy.start()

    barrier = pltpu.get_barrier_semaphore()
    pl.semaphore_signal(barrier, inc=1, device_id={"space": other}, device_id_type=MESH)
    greeted = jnp.int32(1)
    for d in (-2, -1, 1, 2):

        @pl.when(exists(d))
        def _(d=d):
            pl.semaphore_signal(barrier, inc=1, device_id={"tm": f + d}, device_id_type=MESH)
            if abs(d) == 1:
                pl.semaphore_signal(
                    barrier, inc=1, device_id={"tm": f + d, "space": other}, device_id_type=MESH
                )

        greeted = greeted + exists(d).astype(jnp.int32) * (2 if abs(d) == 1 else 1)
    pl.semaphore_wait(barrier, greeted)

    def list_copy(i, d):
        return remote(lists_v, heard.at[i ^ 1], ls.at[i], lr.at[i ^ 1], tm=f + d)

    def list_wait(i, d):
        return remote(lists_v, heard.at[i], ls.at[i], lr.at[i], tm=f + d)

    list_steps = (-1, 1, -2, 2)

    places = (s, other)

    def x_copy(t, h):
        src = (k, v, q)[t].at[:, head_of(other, h)]
        dst = xq.at[h] if t == 2 else kv[t][h].at[s]
        return remote(src, dst, xs.at[t, h], xr.at[t, h], space=other)

    def x_wait(t, h):
        src = (k, v, q)[t].at[:, head_of(other, h)]
        dst = xq.at[h] if t == 2 else kv[t][h].at[other]
        return remote(src, dst, xs.at[t, h], xr.at[t, h], space=other)

    def q_copy(side, i, to=None):
        to = 1 - side if to is None else to
        src = q.at[:, half(s)] if i == 0 else xq.at[i - 1]
        dst = qn.at[to, 0] if i == 0 else qn.at[to, 1, :, cut(i - 1)]
        return remote(src, dst, qs.at[side, i], qr.at[to, i], tm=f + step(side))

    def k_copy(side, t, h, to=None):
        to = 1 - side if to is None else to
        return remote(
            pick.at[side, t, :, cut(h)], mid.at[to, t, :, cut(h)], ks.at[side, t, h],
            kr.at[to, t, h], tm=f + step(side),
        )

    def p_copy(side, i, h, to=None):
        to = 1 - side if to is None else to
        return remote(
            po.at[side, i, h], pin.at[to, i, h], ps_.at[side, i, h], pr.at[to, i, h],
            tm=f + step(side), space=places[i],
        )

    def s_copy(side, i, h, to=None):
        to = 1 - side if to is None else to
        return remote(
            ps.at[side, i, h], lin.at[to, i, h], ss.at[side, i, h], sr.at[to, i, h],
            tm=f + step(side), space=places[i],
        )

    def on_sides(run, there=ex):
        for side in sides:
            pl.when(there(side))(functools.partial(run, side))

    def wait_sides(copy, *key, there=ex):
        on_sides(lambda side: copy(side, *key, to=side).wait_recv(), there)

    for i, d in enumerate(list_steps):

        @pl.when(exists(d))
        def _(i=i, d=d):
            list_copy(i, d).start()

    on_sides(lambda side: q_copy(side, 0).start())

    @pl.when(early)
    def _():
        for h in range(heads):
            x_copy(2, h).start()

    for h in range(heads):
        for t in (0, 1):
            x_copy(t, h).start()

    @pl.when(~early)
    def _():
        for h in range(heads):
            x_copy(2, h).start()

    for copy in local:
        copy.wait()

    def scores(keys, queries):
        return lax.dot_general(
            keys, queries, (((1,), (1,)), ((), ())), preferred_element_type=jnp.float32
        ) * factor

    def gathered(values, weights):
        return lax.dot_general(
            values, weights, (((0,), (0,)), ((), ())), preferred_element_type=jnp.float32
        )

    def home(i, h):
        columns = head_of(places[i], h)
        x = scores(kh[:, columns], qh[:, columns])
        top = jnp.max(x, axis=0, keepdims=True)
        weights = jnp.exp2(x - top)
        whole = jnp.sum(weights, axis=0, keepdims=True)
        own_o[i, h] = gathered(vh[:, columns], weights.astype(jnp.bfloat16)) * (1.0 / whole)
        own_l[i, h : h + 1] = top + jnp.log2(whole)

    def send_pick(t, h):
        x_wait(t, h).wait_recv()

        def run(side):
            n = heard[2 + side, 0, table[-2 * step(side)][0]]
            pick[side, t, :, cut(h)] = kv[t][h][n]
            k_copy(side, t, h).start()

        on_sides(run, lambda side: exists(2 * step(side)))

    def near_block(side, i):
        return heard[side, places[i], table[-step(side)][0]]

    def weigh(side, i, h, both):
        queries = qn[side, i, :, cut(h)]
        x = [scores(kv[0][h][near_block(side, i)], queries)]
        if both:
            x.append(scores(mid[1 - side, 0, :, cut(h)], queries))
        top = functools.reduce(jnp.maximum, [jnp.max(y, axis=0, keepdims=True) for y in x])
        whole = jnp.zeros_like(top)
        for j, y in enumerate(x):
            weights = jnp.exp2(y - top)
            whole = whole + jnp.sum(weights, axis=0, keepdims=True)
            held[side, i, h, j] = weights.astype(jnp.bfloat16)
        rt[side, i, h : h + 1] = 1.0 / whole
        ps[side, i, h] = top + jnp.log2(whole)

    def answer(side, i, h, both):
        value = gathered(kv[1][h][near_block(side, i)], held[side, i, h, 0])
        if both:
            value = value + gathered(mid[1 - side, 1, :, cut(h)], held[side, i, h, 1])
        po[side, i, h] = (value * rt[side, i, h : h + 1]).astype(jnp.bfloat16)

    inner = ex(0) & ex(1)

    def between(side):
        return inner

    def serve(side, h, both):
        if h == 0:
            q_copy(side, 0, to=side).wait_recv()
        q_copy(side, 1 + h, to=side).wait_recv()
        if both:
            k_copy(side, 0, h, to=1 - side).wait_recv()
        for i in range(blocks):
            weigh(side, i, h, both)
        if both:
            k_copy(side, 1, h, to=1 - side).wait_recv()
        for i in range(blocks):
            answer(side, i, h, both)

    def reply(side, h):
        for i in range(blocks):
            s_copy(side, i, h).start()
        for i in reversed(range(blocks)):
            p_copy(side, i, h).start()

    def forward(h):
        send_pick(0, h)
        send_pick(1, h)

    def forward_queries(h):
        x_wait(2, h).wait_recv()
        on_sides(lambda side: q_copy(side, 1 + h).start())

    for h in range(heads):
        home(0, h)
    for i, d in enumerate(list_steps):

        @pl.when(exists(d))
        def _(i=i, d=d):
            list_wait(i, d).wait_recv()

    @pl.when(early)
    def _():
        for h in range(heads):
            forward_queries(h)
            home(1, h)
        for h in range(heads):
            forward(h)

            @pl.when(inner)
            def _(h=h):
                serve(0, h, True)
                reply(0, h)

        for both, there in ((True, inner), (False, ~inner)):

            @pl.when(there)
            def _(both=both):
                for h in range(heads):
                    serve(1, h, both)
                    reply(1, h)

    @pl.when(~early)
    def _():
        forward(0)
        for h in range(heads):
            home(1, h)
        for h in range(1, heads):
            forward(h)

            if h >= 2:
                pl.when(inner)(functools.partial(serve, 0, h - 2, True))

        for h in range(heads):
            forward_queries(h)

            if h == 1:
                pl.when(inner)(functools.partial(serve, 0, heads - 2, True))

        @pl.when(inner)
        def _():
            for h in range(heads):
                if h == heads - 1:
                    serve(0, h, True)
                reply(0, h)
            for h in range(heads):
                serve(1, h, True)
                reply(1, h)

        @pl.when(~inner)
        def _():
            for h in range(heads):
                serve(0, h, False)
                reply(0, h)

    def merge(i, h, parts):
        rows = [own_l[i, h : h + 1]] + [lin[side, i, h] for side in parts]
        top = functools.reduce(jnp.maximum, rows)
        shares = [jnp.exp2(row - top) for row in rows]
        scale = 1.0 / functools.reduce(jnp.add, shares)
        value = own_o[i, h] * (shares[0] * scale)
        for side, share in zip(parts, shares[1:]):
            value = value + pin[side, i, h].astype(jnp.float32) * (share * scale)
        out[:, head_of(places[i], h)] = value.T.astype(jnp.bfloat16)

    for h in range(heads):
        for i in range(blocks):
            wait_sides(s_copy, i, h)
            wait_sides(p_copy, i, h)
            pl.when(ex(0) & ex(1))(lambda: merge(i, h, (0, 1)))
            pl.when(ex(0) & ~ex(1))(lambda: merge(i, h, (0,)))
            pl.when(~ex(0) & ex(1))(lambda: merge(i, h, (1,)))
            pl.when(~ex(0) & ~ex(1))(lambda: merge(i, h, ()))

    for t in range(3):
        for h in range(heads):
            x_copy(t, h).wait_send()
    for i, d in enumerate(list_steps):

        @pl.when(exists(d))
        def _(i=i, d=d):
            list_copy(i, d).wait_send()

    @on_sides
    def _(side):
        for i in range(1 + heads):
            q_copy(side, i).wait_send()
        for i in range(blocks):
            for h in range(heads):
                s_copy(side, i, h).wait_send()
                p_copy(side, i, h).wait_send()

        @pl.when(exists(2 * step(side)))
        def _():
            for t in (0, 1):
                for h in range(heads):
                    k_copy(side, t, h).wait_send()


def short(frames, blocks, queries, key_rows, value_rows, block_lists):
    rows, columns = queries.shape
    width = columns // blocks
    heads = width // DH
    lists = block_lists[0]
    dma = pltpu.SemaphoreType.DMA
    bf, f32 = jnp.bfloat16, jnp.float32
    vmem = pltpu.VMEM
    return pl.pallas_call(
        functools.partial(short_kernel, frames, blocks),
        out_shape=jax.ShapeDtypeStruct(queries.shape, queries.dtype),
        in_specs=[pl.BlockSpec(memory_space=pltpu.HBM)] * 4,
        out_specs=pl.BlockSpec(memory_space=pltpu.VMEM),
        scratch_shapes=[
            vmem((rows, columns), bf),
            vmem((rows, columns), bf),
            vmem((rows, columns), bf),
            [[vmem((blocks, BLOCK, DH), bf)] * heads] * 2,
            vmem((heads, BLOCK, DH), bf),
            vmem((2, blocks, BLOCK, width), bf),
            vmem((2, 2, BLOCK, width), bf),
            vmem((2, 2, BLOCK, width), bf),
            vmem((2, blocks, heads, 2, BLOCK, BLOCK), bf),
            vmem((2, blocks, 8, BLOCK), f32),
            vmem((2, blocks, heads, DH, BLOCK), bf),
            vmem((2, blocks, heads, 1, BLOCK), f32),
            vmem((2, blocks, heads, DH, BLOCK), bf),
            vmem((2, blocks, heads, 1, BLOCK), f32),
            vmem((blocks, heads, DH, BLOCK), f32),
            vmem((blocks, 8, BLOCK), f32),
            pltpu.SMEM((4,) + lists.shape, jnp.int32),
            dma((3 + 2 * heads,)),
            dma((3, heads)),
            dma((3, heads)),
            dma((2, 1 + heads)),
            dma((2, 1 + heads)),
            dma((2, 2, heads)),
            dma((2, 2, heads)),
            dma((2, blocks, heads)),
            dma((2, blocks, heads)),
            dma((2, blocks, heads)),
            dma((2, blocks, heads)),
            dma((4,)),
            dma((4,)),
        ],
        compiler_params=pltpu.CompilerParams(
            collective_id=1, has_side_effects=True, vmem_limit_bytes=48 * 1024 * 1024
        ),
    )(*[pltpu.with_memory_space_constraint(x, pltpu.HBM) for x in (queries, key_rows, value_rows, lists)])


def solution(mesh):
    in_specs = (
        P(("groups", "tm", "space"), "head"),
        P(("groups", "tm", "space"), "head"),
        P(("groups", "tm", "space"), "head"),
        P(("groups", "tm"), None, None),
    )
    out_specs = P(("groups", "tm", "space"), "head")
    frames, blocks = mesh.shape["tm"], mesh.shape["space"]
    body = functools.partial(short if frames <= 4 and blocks == 2 else local, frames, blocks)
    return jax.shard_map(body, mesh=mesh, in_specs=in_specs, out_specs=out_specs, check_vma=False)
```

```python
import functools

import jax
import jax.numpy as jnp
from jax import lax
from jax.experimental import pallas as pl
from jax.experimental.pallas import tpu as pltpu
from jax.sharding import PartitionSpec as P

DH = 128
BLOCK = 128
MESH = pl.DeviceIdType.MESH
LOG2E = 1.4426950408889634
FIRST = 1


def group_table(blocks):
    near, middle, far = max(blocks // 2, 1), max(blocks // 4, 1), max(blocks // 8, 1)
    table = {0: (0, near, blocks)}
    start = near
    for step, count, union in (
        (1, near, blocks),
        (2, middle, max(blocks // 2, 1)),
        (4, far, max(blocks // 4, 1)),
    ):
        table[-step] = (start, count, union)
        table[step] = (start + count, count, union)
        start += 2 * count
    return table


def kernel(
    frames, blocks, q, k, v, lists_v, out,
    lists_s, qb, own, near, pick2, mid, pick2v, midv, pick4, far, heard, ob, peak, total, numer, held, stage, stage_sem,
    loc_sem, xs, xr, zs, zr, ms, mr, fs, fr, ls, lr, os_, or_,
):
    f = lax.axis_index("tm")
    s = lax.axis_index("space")
    width = qb.shape[2]
    heads = width // DH
    table = group_table(blocks)
    use_far = frames > 4
    scale = DH ** -0.5

    def cols(i):
        return pl.ds(pl.multiple_of(i * width, width), width)

    def at(step):
        return {"tm": f + step}

    def exists(step):
        return (f + step >= 0) & (f + step < frames)

    steps = (-1, 1) + ((-4, 4) if use_far else ())

    local = [
        pltpu.make_async_copy(q.at[:, cols(s)], qb.at[s], loc_sem.at[0]),
        pltpu.make_async_copy(k.at[:, cols(s)], own.at[0, s], loc_sem.at[1]),
        pltpu.make_async_copy(v.at[:, cols(s)], own.at[1, s], loc_sem.at[2]),
        pltpu.make_async_copy(lists_v, lists_s, loc_sem.at[3]),
    ]
    for t in range(3):
        for o in range(1, blocks):
            local.append(pltpu.make_async_copy(
                (k, v, q)[t].at[:, cols(lax.rem(s + o, blocks))], stage.at[t, o], stage_sem.at[t, o]
            ))
    for copy in local:
        copy.start()

    barrier = pltpu.get_barrier_semaphore()
    for o in range(1, blocks):
        pl.semaphore_signal(
            barrier, inc=1, device_id={"space": lax.rem(s + o, blocks)}, device_id_type=MESH
        )
    greeted = blocks - 1
    for step in steps:

        @pl.when(exists(step))
        def _(step=step):
            pl.semaphore_signal(barrier, inc=1, device_id=at(step), device_id_type=MESH)

        greeted = greeted + exists(step).astype(jnp.int32)
    for copy in local:
        copy.wait()
    pl.semaphore_wait(barrier, greeted)

    def list_copy(i, step):
        return pltpu.make_async_remote_copy(
            src_ref=lists_v, dst_ref=heard.at[i ^ 1], send_sem=ls.at[i], recv_sem=lr.at[i ^ 1],
            device_id=at(step), device_id_type=MESH,
        )

    def list_wait(i):
        return pltpu.make_async_remote_copy(
            src_ref=lists_v, dst_ref=heard.at[i], send_sem=ls.at[i], recv_sem=lr.at[i],
            device_id=at(steps[i]), device_id_type=MESH,
        )

    def x_copy(t, o):
        to = lax.rem(s + o, blocks)
        src = stage.at[t, o]
        dst = qb.at[s] if t == 2 else own.at[t, s]
        return pltpu.make_async_remote_copy(
            src_ref=src, dst_ref=dst, send_sem=xs.at[t, o], recv_sem=xr.at[t, o],
            device_id={"space": to}, device_id_type=MESH,
        )

    def z_copy(side, t, o):
        b = lax.rem(s - o + blocks, blocks)
        src = own.at[t, b]
        return pltpu.make_async_remote_copy(
            src_ref=src, dst_ref=near.at[side, t, b], send_sem=zs.at[side, t, o],
            recv_sem=zr.at[side, t, o], device_id=at(1 - 2 * side), device_id_type=MESH,
        )

    def m_copy(side, h):
        src, dst = (pick2.at[side], mid.at[side]) if h < 0 else (pick2v.at[side, h], midv.at[side, h])
        return pltpu.make_async_remote_copy(
            src_ref=src, dst_ref=dst, send_sem=ms.at[side, h + 1],
            recv_sem=mr.at[side, h + 1], device_id=at(1 - 2 * side), device_id_type=MESH,
        )

    def f_copy(side, t):
        return pltpu.make_async_remote_copy(
            src_ref=pick4.at[side, t], dst_ref=far.at[side, t], send_sem=fs.at[side, t],
            recv_sem=fr.at[side, t], device_id=at(4 - 8 * side), device_id_type=MESH,
        )

    def ahead(side):
        return exists(1 - 2 * side)

    def behind(side):
        return exists(2 * side - 1)

    for t in (0, 1):
        for o in range(1, blocks):
            x_copy(t, o).start()
        for side in (0, 1):

            @pl.when(ahead(side))
            def _(side=side, t=t):
                z_copy(side, t, 0).start()

    for i, step in enumerate(steps):

        @pl.when(exists(step))
        def _(i=i, step=step):
            list_copy(i, step).start()

    for t in (0, 1):
        for o in range(1, blocks):
            x_copy(t, o).wait_recv()
            for side in (0, 1):

                @pl.when(ahead(side))
                def _(side=side, t=t, o=o):
                    z_copy(side, t, o).start()

    for o in range(1, blocks):
        x_copy(2, o).start()

    def choose(i, distance, load, store):
        first, count, union = table[distance]
        seen, rank = [], []
        before = jnp.zeros((1, 1), jnp.int32)
        for c in range(blocks):
            hit = jnp.zeros((1, 1), jnp.int32)
            for b in range(blocks):
                for j in range(first, first + count):
                    hit = jnp.maximum(hit, (heard[i, b : b + 1, j : j + 1] == c).astype(jnp.int32))
            seen.append(hit)
            rank.append(before)
            before = before + hit
        for u in range(union):
            value = load(blocks - 1).astype(jnp.float32)
            for c in range(blocks - 1):
                mask = jnp.where(rank[c] == u, seen[c], 0)
                mask = jnp.broadcast_to(mask, value.shape)
                value = jnp.where(mask == 1, load(c).astype(jnp.float32), value)
            store(u, value.astype(jnp.bfloat16))

    def place(b, slot, distance):
        first, count, union = table[distance]
        number = lists_s[b, slot]
        if union == blocks:
            return number
        if union == 1:
            return 0
        position = jnp.int32(0)
        for c in range(blocks - 1):
            seen = jnp.int32(0)
            for other in range(blocks):
                for j in range(first, first + count):
                    seen = jnp.maximum(seen, (lists_s[other, j] == c).astype(jnp.int32))
            position = position + jnp.where(c < number, seen, 0)
        return position

    def attend(distance, keys, values, fresh=False):
        first, count, union = table[distance]
        for b in range(blocks):
            for j in range(count):
                n = place(b, first + j, distance)
                for h in range(heads):
                    cut = slice(h * DH, (h + 1) * DH)
                    scores = lax.dot_general(
                        qb[b, :, cut], keys(n, cut), (((1,), (1,)), ((), ())),
                        preferred_element_type=jnp.float32,
                    ) * scale
                    top = jnp.max(scores, axis=1, keepdims=True)
                    if fresh and j == 0:
                        weights = jnp.exp(scores - top)
                        peak[b, h] = jnp.broadcast_to(top, (BLOCK, DH))
                        total[b, h] = jnp.broadcast_to(
                            jnp.sum(weights, axis=1, keepdims=True), (BLOCK, DH)
                        )
                        numer[b, h] = jnp.dot(
                            weights.astype(jnp.bfloat16), values(n, cut),
                            preferred_element_type=jnp.float32,
                        )
                    else:
                        old = peak[b, h]
                        new = jnp.maximum(old, jnp.broadcast_to(top, (BLOCK, DH)))
                        fade = jnp.exp(old - new)
                        weights = jnp.exp(scores - new)
                        peak[b, h] = new
                        total[b, h] = total[b, h] * fade + jnp.broadcast_to(
                            jnp.sum(weights, axis=1, keepdims=True), (BLOCK, DH)
                        )
                        numer[b, h] = numer[b, h] * fade + jnp.dot(
                            weights.astype(jnp.bfloat16), values(n, cut),
                            preferred_element_type=jnp.float32,
                        )

    if use_far:
        for side in (0, 1):

            @pl.when(exists(4 - 8 * side))
            def _(side=side):
                i = 3 - side
                list_wait(i).wait_recv()
                for t in (0, 1):
                    choose(
                        i, -4 if side == 0 else 4,
                        lambda c: own[t, c],
                        lambda u, x: pick4.__setitem__((side, t, u), x),
                    )
                    f_copy(side, t).start()

    for i in (0, 1):

        @pl.when(exists(steps[i]))
        def _(i=i):
            list_wait(i).wait_recv()

    for side in (0, 1):

        @pl.when(behind(side))
        def _(side=side):
            for o in range(blocks):
                z_copy(side, 0, o).wait_recv()

        @pl.when(behind(side) & ahead(side))
        def _(side=side):
            choose(
                1 - side, -2 if side == 0 else 2,
                lambda c: near[side, 0, c],
                lambda u, x: pick2.__setitem__((side, u), x),
            )
            m_copy(side, -1).start()

    for o in range(1, blocks):
        x_copy(2, o).wait_recv()
    attend(0, lambda n, cut: own[0, n, :, cut], lambda n, cut: own[1, n, :, cut], fresh=True)

    for side in (0, 1):

        @pl.when(behind(side))
        def _(side=side):
            for o in range(blocks):
                z_copy(side, 1, o).wait_recv()

        @pl.when(behind(side) & ahead(side))
        def _(side=side):
            for h in range(heads):
                choose(
                    1 - side, -2 if side == 0 else 2,
                    lambda c: near[side, 1, c, :, h * DH : (h + 1) * DH],
                    lambda u, x: pick2v.__setitem__((side, h, u), x),
                )
                m_copy(side, h).start()

    for side in (0, 1):

        @pl.when(behind(side))
        def _(side=side):
            attend(
                -1 if side == 0 else 1,
                lambda n, cut: near[side, 0, n, :, cut], lambda n, cut: near[side, 1, n, :, cut],
            )

    if use_far:
        for side in (0, 1):

            @pl.when(exists(8 * side - 4))
            def _(side=side):
                for t in (0, 1):
                    f_copy(side, t).wait_recv()
                attend(
                    -4 if side == 0 else 4,
                    lambda n, cut: far[side, 0, n, :, cut], lambda n, cut: far[side, 1, n, :, cut],
                )

    for side in (0, 1):

        @pl.when(exists(4 * side - 2))
        def _(side=side):
            m_copy(side, -1).wait_recv()

    def mid_scores(b, h, side, j):
        distance = -2 if side == 0 else 2
        cut = slice(h * DH, (h + 1) * DH)
        n = place(b, table[distance][0] + j, distance)
        return lax.dot_general(
            qb[b, :, cut], mid[side, n, :, cut], (((1,), (1,)), ((), ())),
            preferred_element_type=jnp.float32,
        ) * scale

    def mid_weights(sides):
        slots = [(side, j) for side in sides for j in range(table[2][1])]
        for b in range(blocks):
            for h in range(heads):
                scores = [mid_scores(b, h, side, j) for side, j in slots]
                old = peak[b, h]
                new = old
                for x in scores:
                    top = jnp.max(x, axis=1, keepdims=True)
                    new = jnp.maximum(new, jnp.broadcast_to(top, (BLOCK, DH)))
                fade = jnp.exp(old - new)
                whole = total[b, h] * fade
                for (side, j), x in zip(slots, scores):
                    weights = jnp.exp(x - new)
                    whole = whole + jnp.broadcast_to(
                        jnp.sum(weights, axis=1, keepdims=True), (BLOCK, DH)
                    )
                    held[side, j, b, h] = weights.astype(jnp.bfloat16)
                total[b, h] = 1.0 / whole
                numer[b, h] = numer[b, h] * fade

    def o_copy(o, h):
        to = lax.rem(s + o, blocks)
        return pltpu.make_async_remote_copy(
            src_ref=ob.at[to, h], dst_ref=out.at[:, head_cols(s, h)],
            send_sem=os_.at[o, h], recv_sem=or_.at[o, h],
            device_id={"space": to}, device_id_type=MESH,
        )

    def head_cols(i, h):
        return pl.ds(pl.multiple_of(i * width + h * DH, DH), DH)

    def keep(h):
        return pltpu.make_async_copy(ob.at[s, h], out.at[:, head_cols(s, h)], os_.at[0, h])

    def finish(sides):
        for h in range(heads):
            for side in sides:
                m_copy(side, h).wait_recv()
            for o in list(range(1, blocks)) + [0]:
                b = lax.rem(s + o, blocks)
                value = numer[b, h]
                for side in sides:
                    distance = -2 if side == 0 else 2
                    for j in range(table[2][1]):
                        n = place(b, table[distance][0] + j, distance)
                        value = value + jnp.dot(
                            held[side, j, b, h], midv[side, h, n],
                            preferred_element_type=jnp.float32,
                        )
                ob[b, h] = (value * total[b, h]).astype(jnp.bfloat16)
                if o:
                    o_copy(o, h).start()
                else:
                    keep(h).start()

    def last(sides):
        mid_weights(sides)
        finish(sides)

    pl.when(exists(-2) & exists(2))(lambda: last((0, 1)))
    pl.when(exists(-2) & ~exists(2))(lambda: last((0,)))
    pl.when(~exists(-2) & exists(2))(lambda: last((1,)))
    pl.when(~exists(-2) & ~exists(2))(lambda: last(()))

    for t in (0, 1, 2):
        for o in range(1, blocks):
            x_copy(t, o).wait_send()
    for i, step in enumerate(steps):

        @pl.when(exists(step))
        def _(i=i, step=step):
            list_copy(i, step).wait_send()

    for side in (0, 1):

        @pl.when(ahead(side))
        def _(side=side):
            for t in (0, 1):
                for o in range(blocks):
                    z_copy(side, t, o).wait_send()

        @pl.when(behind(side) & ahead(side))
        def _(side=side):
            for h in range(-1, heads):
                m_copy(side, h).wait_send()

        if use_far:

            @pl.when(exists(4 - 8 * side))
            def _(side=side):
                for t in (0, 1):
                    f_copy(side, t).wait_send()

    for h in range(heads):
        keep(h).wait()
        for o in range(1, blocks):
            o_copy(o, h).wait_send()
            pltpu.make_async_remote_copy(
                src_ref=ob.at[s, h], dst_ref=out.at[:, head_cols(lax.rem(s - o + blocks, blocks), h)],
                send_sem=os_.at[o, h], recv_sem=or_.at[o, h],
                device_id={"space": lax.rem(s + o, blocks)}, device_id_type=MESH,
            ).wait_recv()


def local(frames, blocks, queries, key_rows, value_rows, block_lists):
    rows, columns = queries.shape
    width = columns // blocks
    heads = width // DH
    lists = block_lists[0]
    table = group_table(blocks)
    u2, u4 = table[2][2], table[4][2]
    far_rows = BLOCK if frames > 4 else 16
    dma = pltpu.SemaphoreType.DMA
    bf = jnp.bfloat16
    return pl.pallas_call(
        functools.partial(kernel, frames, blocks),
        out_shape=jax.ShapeDtypeStruct(queries.shape, queries.dtype),
        in_specs=[pl.BlockSpec(memory_space=pltpu.HBM)] * 4,
        out_specs=pl.BlockSpec(memory_space=pl.ANY),
        scratch_shapes=[
            pltpu.SMEM(lists.shape, jnp.int32),
            pltpu.VMEM((blocks, BLOCK, width), bf),
            pltpu.VMEM((2, blocks, BLOCK, width), bf),
            pltpu.VMEM((2, 2, blocks, BLOCK, width), bf),
            pltpu.VMEM((2, u2, BLOCK, width), bf),
            pltpu.VMEM((2, u2, BLOCK, width), bf),
            pltpu.VMEM((2, heads, u2, BLOCK, DH), bf),
            pltpu.VMEM((2, heads, u2, BLOCK, DH), bf),
            pltpu.VMEM((2, 2, u4, far_rows, width), bf),
            pltpu.VMEM((2, 2, u4, far_rows, width), bf),
            pltpu.VMEM((4,) + lists.shape, jnp.int32),
            pltpu.VMEM((blocks, heads, BLOCK, DH), bf),
            pltpu.VMEM((blocks, heads, BLOCK, DH), jnp.float32),
            pltpu.VMEM((blocks, heads, BLOCK, DH), jnp.float32),
            pltpu.VMEM((blocks, heads, BLOCK, DH), jnp.float32),
            pltpu.VMEM((2, table[2][1], blocks, heads, BLOCK, DH), bf),
            pltpu.VMEM((3, blocks, BLOCK, width), bf),
            dma((3, blocks)),
            dma((5,)),
            dma((3, blocks)),
            dma((3, blocks)),
            dma((2, 2, blocks)),
            dma((2, 2, blocks)),
            dma((2, 1 + heads)),
            dma((2, 1 + heads)),
            dma((2, 2)),
            dma((2, 2)),
            dma((4,)),
            dma((4,)),
            dma((blocks, heads)),
            dma((blocks, heads)),
        ],
        compiler_params=pltpu.CompilerParams(
            collective_id=0, has_side_effects=True, vmem_limit_bytes=48 * 1024 * 1024
        ),
    )(*[pltpu.with_memory_space_constraint(x, pltpu.HBM) for x in (queries, key_rows, value_rows, lists)])


def short_kernel(
    frames, blocks, q, k, v, lists_v, out,
    qh, kh, vh, kv, xq, qn, mid, pick, held, rt, po, ps, pin, lin, own_o, own_l, heard,
    loc_sem, xs, xr, qs, qr, ks, kr, ps_, pr, ss, sr, ls, lr, cs, cr, ready,
):
    f = lax.axis_index("tm")
    s = lax.axis_index("space")
    other = 1 - s
    width = qn.shape[3]
    heads = width // DH
    table = group_table(blocks)
    factor = DH ** -0.5 * LOG2E
    sides = (0, 1)
    early = f < frames // 2
    core = lax.axis_index("head")
    lead = core == 1

    def exists(step):
        return (f + step >= 0) & (f + step < frames)

    def step(side):
        return 2 * side - 1

    def ex(side):
        return exists(step(side))

    def half(i):
        return pl.ds(pl.multiple_of(i * width, width), width)

    def head_of(i, h):
        return pl.ds(pl.multiple_of(i * width + h * DH, DH), DH)

    def cut(h):
        return slice(h * DH, (h + 1) * DH)

    def remote(src, dst, send, recv, **where):
        return pltpu.make_async_remote_copy(
            src_ref=src, dst_ref=dst, send_sem=send, recv_sem=recv,
            device_id=where, device_id_type=MESH,
        )

    local = [
        pltpu.make_async_copy(q, qh, loc_sem.at[0]),
        pltpu.make_async_copy(k, kh, loc_sem.at[1]),
        pltpu.make_async_copy(v, vh, loc_sem.at[2]),
    ]
    for t in (0, 1):
        for h in range(heads):
            local.append(pltpu.make_async_copy(
                (k, v)[t].at[:, head_of(s, h)], kv[t][h].at[s], loc_sem.at[3 + t * heads + h]
            ))
    for copy in local:
        copy.start()

    def late(frame):
        return frame >= frames // 2

    def greet(semaphore, d):
        pl.semaphore_signal(semaphore, inc=1, device_id={"tm": f + d}, device_id_type=MESH)

    barrier = pltpu.get_barrier_semaphore()
    pl.semaphore_signal(barrier, inc=1, device_id={"space": other}, device_id_type=MESH)
    pl.when(exists(2) & lead)(lambda: greet(barrier, 2))

    @pl.when(~lead)
    def _():
        pl.semaphore_signal(barrier, inc=1, device_id={"head": 1}, device_id_type=MESH)

    pl.when(exists(1))(lambda: greet(barrier, 1))
    pl.when(exists(-1) & ~late(f))(lambda: greet(barrier, -1))
    greeted = 1 + exists(-1).astype(jnp.int32)
    greeted = greeted + (exists(-2) & lead).astype(jnp.int32) + lead.astype(jnp.int32)
    pl.semaphore_wait(barrier, greeted + (exists(1) & ~late(f + 1)).astype(jnp.int32))
    pl.when(exists(-1) & late(f))(lambda: greet(ready.at[0], -1))
    pl.when(exists(-2) & lead)(lambda: greet(ready.at[1], -2))

    def list_copy(i, d):
        return remote(lists_v, heard.at[i ^ 1], ls.at[i], lr.at[i ^ 1], tm=f + d)

    def list_wait(i, d):
        return remote(lists_v, heard.at[i], ls.at[i], lr.at[i], tm=f + d)

    list_steps = (-1, 1, -2, 2)

    places = (s, other)

    def x_copy(t, h):
        src = (k, v, q)[t].at[:, head_of(other, h)]
        dst = xq.at[h] if t == 2 else kv[t][h].at[s]
        return remote(src, dst, xs.at[t, h], xr.at[t, h], space=other)

    def x_wait(t, h):
        src = (k, v, q)[t].at[:, head_of(other, h)]
        dst = xq.at[h] if t == 2 else kv[t][h].at[other]
        return remote(src, dst, xs.at[t, h], xr.at[t, h], space=other)

    def q_copy(side, i, to=None):
        to = 1 - side if to is None else to
        src = q.at[:, half(s)] if i == 0 else xq.at[i - 1]
        dst = qn.at[to, 0] if i == 0 else qn.at[to, 1, :, cut(i - 1)]
        return remote(src, dst, qs.at[side, i], qr.at[to, i], tm=f + step(side))

    def k_copy(side, t, h, to=None):
        to = 1 - side if to is None else to
        return remote(
            pick.at[side, t, :, cut(h)], mid.at[to, t, :, cut(h)], ks.at[side, t, h],
            kr.at[to, t, h], tm=f + step(side),
        )

    def p_copy(side, i, h, to=None):
        to = 1 - side if to is None else to
        return remote(
            po.at[side, i, h], pin.at[to, i, h], ps_.at[side, i, h], pr.at[to, i, h],
            tm=f + step(side), space=places[i],
        )

    def s_copy(side, i, h, to=None):
        to = 1 - side if to is None else to
        return remote(
            ps.at[side, i, h], lin.at[to, i, h], ss.at[side, i, h], sr.at[to, i, h],
            tm=f + step(side), space=places[i],
        )

    def on_sides(run, there=ex):
        for side in sides:
            pl.when(there(side))(functools.partial(run, side))

    def wait_sides(copy, *key, there=ex):
        on_sides(lambda side: copy(side, *key, to=side).wait_recv(), there)

    @pl.when(exists(-1))
    def _():
        pl.when(lead)(lambda: list_copy(0, -1).start())
        q_copy(0, 0).start()

    pl.when(exists(-2) & lead)(lambda: list_copy(2, -2).start())

    def start_queries(span):
        for h in span:
            x_copy(2, h).start()

    start_queries(range(FIRST))
    pl.when(early)(lambda: start_queries(range(FIRST, heads)))
    for h in range(heads):
        for t in (0, 1):
            x_copy(t, h).start()
    pl.when(~early)(lambda: start_queries(range(FIRST, heads)))

    @pl.when(exists(1))
    def _():
        pl.when(late(f + 1))(lambda: pl.semaphore_wait(ready.at[0], 1))
        pl.when(lead)(lambda: list_copy(1, 1).start())
        q_copy(1, 0).start()

    for copy in local:
        copy.wait()

    def scores(keys, queries):
        return lax.dot_general(
            keys, queries, (((1,), (1,)), ((), ())), preferred_element_type=jnp.float32
        ) * factor

    def gathered(values, weights):
        return lax.dot_general(
            values, weights, (((0,), (0,)), ((), ())), preferred_element_type=jnp.float32
        )

    def home(i, h):
        columns = head_of(places[i], h)
        x = scores(kh[:, columns], qh[:, columns])
        top = jnp.max(x, axis=0, keepdims=True)
        weights = jnp.exp2(x - top)
        whole = jnp.sum(weights, axis=0, keepdims=True)
        own_o[i, h] = gathered(vh[:, columns], weights.astype(jnp.bfloat16)) * (1.0 / whole)
        own_l[i, h : h + 1] = top + jnp.log2(whole)

    def send_pick(t, h):
        x_wait(t, h).wait_recv()

        def run(side):
            n = heard[2 + side, 0, table[-2 * step(side)][0]]
            pick[side, t, :, cut(h)] = kv[t][h][n]
            k_copy(side, t, h).start()

        on_sides(run, lambda side: exists(2 * step(side)))

    def near_block(side, i):
        return heard[side, places[i], table[-step(side)][0]]

    def weigh(side, i, h, both):
        queries = qn[side, i, :, cut(h)]
        x = [scores(kv[0][h][near_block(side, i)], queries)]
        if both:
            x.append(scores(mid[1 - side, 0, :, cut(h)], queries))
        top = functools.reduce(jnp.maximum, [jnp.max(y, axis=0, keepdims=True) for y in x])
        whole = jnp.zeros_like(top)
        for j, y in enumerate(x):
            weights = jnp.exp2(y - top)
            whole = whole + jnp.sum(weights, axis=0, keepdims=True)
            held[side, i, h, j] = weights.astype(jnp.bfloat16)
        rt[side, i, h : h + 1] = 1.0 / whole
        ps[side, i, h] = top + jnp.log2(whole)

    def answer(side, i, h, both):
        value = gathered(kv[1][h][near_block(side, i)], held[side, i, h, 0])
        if both:
            value = value + gathered(mid[1 - side, 1, :, cut(h)], held[side, i, h, 1])
        po[side, i, h] = (value * rt[side, i, h : h + 1]).astype(jnp.bfloat16)

    inner = ex(0) & ex(1)

    def between(side):
        return inner

    def serve(side, h, both):
        if h == 0:
            q_copy(side, 0, to=side).wait_recv()
        q_copy(side, 1 + h, to=side).wait_recv()
        if both:
            k_copy(side, 0, h, to=1 - side).wait_recv()
        for i in range(blocks):
            weigh(side, i, h, both)
        if both:
            k_copy(side, 1, h, to=1 - side).wait_recv()
        for i in range(blocks):
            answer(side, i, h, both)

    def reply(side, h):
        for i in range(blocks):
            s_copy(side, i, h).start()
        for i in reversed(range(blocks)):
            p_copy(side, i, h).start()

    def forward(h):
        send_pick(0, h)
        send_pick(1, h)

    def forward_queries(h):
        x_wait(2, h).wait_recv()
        on_sides(lambda side: q_copy(side, 1 + h).start())

    for h in range(heads):
        home(0, h)

    @pl.when(exists(2) & lead)
    def _():
        pl.semaphore_wait(ready.at[1], 1)
        list_copy(3, 2).start()

    def chip_copy(i):
        return remote(heard.at[i], heard.at[i], cs.at[i], cr.at[i], head=0)

    def wait_lists():
        for i, d in enumerate(list_steps):

            @pl.when(exists(d) & lead)
            def _():
                list_wait(i, d).wait_recv()
                chip_copy(i).start()

            pl.when(exists(d) & ~lead)(lambda: chip_copy(i).wait_recv())

    @pl.when(early)
    def _():
        for h in range(heads):
            forward_queries(h)
            home(1, h)
        wait_lists()
        for h in range(heads):
            forward(h)

            @pl.when(inner)
            def _(h=h):
                serve(0, h, True)
                reply(0, h)

        for both, there in ((True, inner), (False, ~inner)):

            @pl.when(there)
            def _(both=both):
                for h in range(heads):
                    serve(1, h, both)
                    reply(1, h)

    @pl.when(~early)
    def _():
        for h in range(FIRST):
            forward_queries(h)
            home(1, h)
        wait_lists()
        forward(0)
        for h in range(FIRST, heads):
            home(1, h)
        for h in range(1, heads):
            forward(h)
            if h >= 2:
                pl.when(inner)(functools.partial(serve, 0, h - 2, True))

        for h in range(FIRST, heads):
            forward_queries(h)
        pl.when(inner)(functools.partial(serve, 0, heads - 2, True))

        @pl.when(inner)
        def _():
            for h in range(heads):
                if h == heads - 1:
                    serve(0, h, True)
                reply(0, h)
            for h in range(heads):
                serve(1, h, True)
                reply(1, h)

        @pl.when(~inner)
        def _():
            for h in range(heads):
                serve(0, h, False)
                reply(0, h)

    def merge(i, h, parts):
        rows = [own_l[i, h : h + 1]] + [lin[side, i, h] for side in parts]
        top = functools.reduce(jnp.maximum, rows)
        shares = [jnp.exp2(row - top) for row in rows]
        scale = 1.0 / functools.reduce(jnp.add, shares)
        value = own_o[i, h] * (shares[0] * scale)
        for side, share in zip(parts, shares[1:]):
            value = value + pin[side, i, h].astype(jnp.float32) * (share * scale)
        out[:, head_of(places[i], h)] = value.T.astype(jnp.bfloat16)

    for h in range(heads):
        for i in range(blocks):
            wait_sides(s_copy, i, h)
            wait_sides(p_copy, i, h)
            pl.when(ex(0) & ex(1))(lambda: merge(i, h, (0, 1)))
            pl.when(ex(0) & ~ex(1))(lambda: merge(i, h, (0,)))
            pl.when(~ex(0) & ex(1))(lambda: merge(i, h, (1,)))
            pl.when(~ex(0) & ~ex(1))(lambda: merge(i, h, ()))

    for t in range(3):
        for h in range(heads):
            x_copy(t, h).wait_send()
    for i, d in enumerate(list_steps):

        @pl.when(exists(d) & lead)
        def _(i=i, d=d):
            list_copy(i, d).wait_send()
            chip_copy(i).wait_send()

    @on_sides
    def _(side):
        for i in range(1 + heads):
            q_copy(side, i).wait_send()
        for i in range(blocks):
            for h in range(heads):
                s_copy(side, i, h).wait_send()
                p_copy(side, i, h).wait_send()

        @pl.when(exists(2 * step(side)))
        def _():
            for t in (0, 1):
                for h in range(heads):
                    k_copy(side, t, h).wait_send()


def short(frames, blocks, queries, key_rows, value_rows, block_lists):
    rows, columns = queries.shape
    width = columns // blocks
    heads = width // DH
    lists = block_lists[0]
    dma = pltpu.SemaphoreType.DMA
    bf, f32 = jnp.bfloat16, jnp.float32
    vmem = pltpu.VMEM
    return pl.pallas_call(
        functools.partial(short_kernel, frames, blocks),
        out_shape=jax.ShapeDtypeStruct(queries.shape, queries.dtype),
        in_specs=[pl.BlockSpec(memory_space=pltpu.HBM)] * 4,
        out_specs=pl.BlockSpec(memory_space=pltpu.VMEM),
        scratch_shapes=[
            vmem((rows, columns), bf),
            vmem((rows, columns), bf),
            vmem((rows, columns), bf),
            [[vmem((blocks, BLOCK, DH), bf)] * heads] * 2,
            vmem((heads, BLOCK, DH), bf),
            vmem((2, blocks, BLOCK, width), bf),
            vmem((2, 2, BLOCK, width), bf),
            vmem((2, 2, BLOCK, width), bf),
            vmem((2, blocks, heads, 2, BLOCK, BLOCK), bf),
            vmem((2, blocks, 8, BLOCK), f32),
            vmem((2, blocks, heads, DH, BLOCK), bf),
            vmem((2, blocks, heads, 1, BLOCK), f32),
            vmem((2, blocks, heads, DH, BLOCK), bf),
            vmem((2, blocks, heads, 1, BLOCK), f32),
            vmem((blocks, heads, DH, BLOCK), f32),
            vmem((blocks, 8, BLOCK), f32),
            pltpu.SMEM((4,) + lists.shape, jnp.int32),
            dma((3 + 2 * heads,)),
            dma((3, heads)),
            dma((3, heads)),
            dma((2, 1 + heads)),
            dma((2, 1 + heads)),
            dma((2, 2, heads)),
            dma((2, 2, heads)),
            dma((2, blocks, heads)),
            dma((2, blocks, heads)),
            dma((2, blocks, heads)),
            dma((2, blocks, heads)),
            dma((4,)),
            dma((4,)),
            dma((4,)),
            dma((4,)),
            pltpu.SemaphoreType.REGULAR((2,)),
        ],
        compiler_params=pltpu.CompilerParams(
            collective_id=1, has_side_effects=True, vmem_limit_bytes=48 * 1024 * 1024
        ),
    )(*[pltpu.with_memory_space_constraint(x, pltpu.HBM) for x in (queries, key_rows, value_rows, lists)])


def solution(mesh):
    in_specs = (
        P(("groups", "tm", "space"), "head"),
        P(("groups", "tm", "space"), "head"),
        P(("groups", "tm", "space"), "head"),
        P(("groups", "tm"), None, None),
    )
    out_specs = P(("groups", "tm", "space"), "head")
    frames, blocks = mesh.shape["tm"], mesh.shape["space"]
    body = functools.partial(short if frames <= 4 and blocks == 2 else local, frames, blocks)
    return jax.shard_map(body, mesh=mesh, in_specs=in_specs, out_specs=out_specs, check_vma=False)
```

```python
import functools

import jax
import jax.numpy as jnp
from jax import lax
from jax.experimental import pallas as pl
from jax.experimental.pallas import tpu as pltpu
from jax.sharding import PartitionSpec as P

DH = 128
BLOCK = 128
MESH = pl.DeviceIdType.MESH
LOG2E = 1.4426950408889634
FIRST = 1


def group_table(blocks):
    near, middle, far = max(blocks // 2, 1), max(blocks // 4, 1), max(blocks // 8, 1)
    table = {0: (0, near, blocks)}
    start = near
    for step, count, union in (
        (1, near, blocks),
        (2, middle, max(blocks // 2, 1)),
        (4, far, max(blocks // 4, 1)),
    ):
        table[-step] = (start, count, union)
        table[step] = (start + count, count, union)
        start += 2 * count
    return table


def kernel(
    frames, blocks, q, k, v, lists_v, out,
    lists_s, qb, own, near, pick2, mid, pick2v, midv, pick4, far, heard, ob, peak, total, numer, held, stage, stage_sem,
    loc_sem, xs, xr, zs, zr, ms, mr, fs, fr, ls, lr, os_, or_,
):
    f = lax.axis_index("tm")
    s = lax.axis_index("space")
    width = qb.shape[2]
    heads = width // DH
    table = group_table(blocks)
    use_far = frames > 4
    scale = DH ** -0.5

    def cols(i):
        return pl.ds(pl.multiple_of(i * width, width), width)

    def at(step):
        return {"tm": f + step}

    def exists(step):
        return (f + step >= 0) & (f + step < frames)

    steps = (-1, 1) + ((-4, 4) if use_far else ())

    local = [
        pltpu.make_async_copy(q.at[:, cols(s)], qb.at[s], loc_sem.at[0]),
        pltpu.make_async_copy(k.at[:, cols(s)], own.at[0, s], loc_sem.at[1]),
        pltpu.make_async_copy(v.at[:, cols(s)], own.at[1, s], loc_sem.at[2]),
        pltpu.make_async_copy(lists_v, lists_s, loc_sem.at[3]),
    ]
    for t in range(3):
        for o in range(1, blocks):
            local.append(pltpu.make_async_copy(
                (k, v, q)[t].at[:, cols(lax.rem(s + o, blocks))], stage.at[t, o], stage_sem.at[t, o]
            ))
    for copy in local:
        copy.start()

    barrier = pltpu.get_barrier_semaphore()
    for o in range(1, blocks):
        pl.semaphore_signal(
            barrier, inc=1, device_id={"space": lax.rem(s + o, blocks)}, device_id_type=MESH
        )
    greeted = blocks - 1
    for step in steps:

        @pl.when(exists(step))
        def _(step=step):
            pl.semaphore_signal(barrier, inc=1, device_id=at(step), device_id_type=MESH)

        greeted = greeted + exists(step).astype(jnp.int32)
    for copy in local:
        copy.wait()
    pl.semaphore_wait(barrier, greeted)

    def list_copy(i, step):
        return pltpu.make_async_remote_copy(
            src_ref=lists_v, dst_ref=heard.at[i ^ 1], send_sem=ls.at[i], recv_sem=lr.at[i ^ 1],
            device_id=at(step), device_id_type=MESH,
        )

    def list_wait(i):
        return pltpu.make_async_remote_copy(
            src_ref=lists_v, dst_ref=heard.at[i], send_sem=ls.at[i], recv_sem=lr.at[i],
            device_id=at(steps[i]), device_id_type=MESH,
        )

    def x_copy(t, o):
        to = lax.rem(s + o, blocks)
        src = stage.at[t, o]
        dst = qb.at[s] if t == 2 else own.at[t, s]
        return pltpu.make_async_remote_copy(
            src_ref=src, dst_ref=dst, send_sem=xs.at[t, o], recv_sem=xr.at[t, o],
            device_id={"space": to}, device_id_type=MESH,
        )

    def z_copy(side, t, o):
        b = lax.rem(s - o + blocks, blocks)
        src = own.at[t, b]
        return pltpu.make_async_remote_copy(
            src_ref=src, dst_ref=near.at[side, t, b], send_sem=zs.at[side, t, o],
            recv_sem=zr.at[side, t, o], device_id=at(1 - 2 * side), device_id_type=MESH,
        )

    def m_copy(side, h):
        src, dst = (pick2.at[side], mid.at[side]) if h < 0 else (pick2v.at[side, h], midv.at[side, h])
        return pltpu.make_async_remote_copy(
            src_ref=src, dst_ref=dst, send_sem=ms.at[side, h + 1],
            recv_sem=mr.at[side, h + 1], device_id=at(1 - 2 * side), device_id_type=MESH,
        )

    def f_copy(side, t):
        return pltpu.make_async_remote_copy(
            src_ref=pick4.at[side, t], dst_ref=far.at[side, t], send_sem=fs.at[side, t],
            recv_sem=fr.at[side, t], device_id=at(4 - 8 * side), device_id_type=MESH,
        )

    def ahead(side):
        return exists(1 - 2 * side)

    def behind(side):
        return exists(2 * side - 1)

    for t in (0, 1):
        for o in range(1, blocks):
            x_copy(t, o).start()
        for side in (0, 1):

            @pl.when(ahead(side))
            def _(side=side, t=t):
                z_copy(side, t, 0).start()

    for i, step in enumerate(steps):

        @pl.when(exists(step))
        def _(i=i, step=step):
            list_copy(i, step).start()

    for t in (0, 1):
        for o in range(1, blocks):
            x_copy(t, o).wait_recv()
            for side in (0, 1):

                @pl.when(ahead(side))
                def _(side=side, t=t, o=o):
                    z_copy(side, t, o).start()

    for o in range(1, blocks):
        x_copy(2, o).start()

    def choose(i, distance, load, store):
        first, count, union = table[distance]
        seen, rank = [], []
        before = jnp.zeros((1, 1), jnp.int32)
        for c in range(blocks):
            hit = jnp.zeros((1, 1), jnp.int32)
            for b in range(blocks):
                for j in range(first, first + count):
                    hit = jnp.maximum(hit, (heard[i, b : b + 1, j : j + 1] == c).astype(jnp.int32))
            seen.append(hit)
            rank.append(before)
            before = before + hit
        for u in range(union):
            value = load(blocks - 1).astype(jnp.float32)
            for c in range(blocks - 1):
                mask = jnp.where(rank[c] == u, seen[c], 0)
                mask = jnp.broadcast_to(mask, value.shape)
                value = jnp.where(mask == 1, load(c).astype(jnp.float32), value)
            store(u, value.astype(jnp.bfloat16))

    def place(b, slot, distance):
        first, count, union = table[distance]
        number = lists_s[b, slot]
        if union == blocks:
            return number
        if union == 1:
            return 0
        position = jnp.int32(0)
        for c in range(blocks - 1):
            seen = jnp.int32(0)
            for other in range(blocks):
                for j in range(first, first + count):
                    seen = jnp.maximum(seen, (lists_s[other, j] == c).astype(jnp.int32))
            position = position + jnp.where(c < number, seen, 0)
        return position

    def attend(distance, keys, values, fresh=False):
        first, count, union = table[distance]
        for b in range(blocks):
            for j in range(count):
                n = place(b, first + j, distance)
                for h in range(heads):
                    cut = slice(h * DH, (h + 1) * DH)
                    scores = lax.dot_general(
                        qb[b, :, cut], keys(n, cut), (((1,), (1,)), ((), ())),
                        preferred_element_type=jnp.float32,
                    ) * scale
                    top = jnp.max(scores, axis=1, keepdims=True)
                    if fresh and j == 0:
                        weights = jnp.exp(scores - top)
                        peak[b, h] = jnp.broadcast_to(top, (BLOCK, DH))
                        total[b, h] = jnp.broadcast_to(
                            jnp.sum(weights, axis=1, keepdims=True), (BLOCK, DH)
                        )
                        numer[b, h] = jnp.dot(
                            weights.astype(jnp.bfloat16), values(n, cut),
                            preferred_element_type=jnp.float32,
                        )
                    else:
                        old = peak[b, h]
                        new = jnp.maximum(old, jnp.broadcast_to(top, (BLOCK, DH)))
                        fade = jnp.exp(old - new)
                        weights = jnp.exp(scores - new)
                        peak[b, h] = new
                        total[b, h] = total[b, h] * fade + jnp.broadcast_to(
                            jnp.sum(weights, axis=1, keepdims=True), (BLOCK, DH)
                        )
                        numer[b, h] = numer[b, h] * fade + jnp.dot(
                            weights.astype(jnp.bfloat16), values(n, cut),
                            preferred_element_type=jnp.float32,
                        )

    if use_far:
        for side in (0, 1):

            @pl.when(exists(4 - 8 * side))
            def _(side=side):
                i = 3 - side
                list_wait(i).wait_recv()
                for t in (0, 1):
                    choose(
                        i, -4 if side == 0 else 4,
                        lambda c: own[t, c],
                        lambda u, x: pick4.__setitem__((side, t, u), x),
                    )
                    f_copy(side, t).start()

    for i in (0, 1):

        @pl.when(exists(steps[i]))
        def _(i=i):
            list_wait(i).wait_recv()

    for side in (0, 1):

        @pl.when(behind(side))
        def _(side=side):
            for o in range(blocks):
                z_copy(side, 0, o).wait_recv()

        @pl.when(behind(side) & ahead(side))
        def _(side=side):
            choose(
                1 - side, -2 if side == 0 else 2,
                lambda c: near[side, 0, c],
                lambda u, x: pick2.__setitem__((side, u), x),
            )
            m_copy(side, -1).start()

    for o in range(1, blocks):
        x_copy(2, o).wait_recv()
    attend(0, lambda n, cut: own[0, n, :, cut], lambda n, cut: own[1, n, :, cut], fresh=True)

    for side in (0, 1):

        @pl.when(behind(side))
        def _(side=side):
            for o in range(blocks):
                z_copy(side, 1, o).wait_recv()

        @pl.when(behind(side) & ahead(side))
        def _(side=side):
            for h in range(heads):
                choose(
                    1 - side, -2 if side == 0 else 2,
                    lambda c: near[side, 1, c, :, h * DH : (h + 1) * DH],
                    lambda u, x: pick2v.__setitem__((side, h, u), x),
                )
                m_copy(side, h).start()

    for side in (0, 1):

        @pl.when(behind(side))
        def _(side=side):
            attend(
                -1 if side == 0 else 1,
                lambda n, cut: near[side, 0, n, :, cut], lambda n, cut: near[side, 1, n, :, cut],
            )

    if use_far:
        for side in (0, 1):

            @pl.when(exists(8 * side - 4))
            def _(side=side):
                for t in (0, 1):
                    f_copy(side, t).wait_recv()
                attend(
                    -4 if side == 0 else 4,
                    lambda n, cut: far[side, 0, n, :, cut], lambda n, cut: far[side, 1, n, :, cut],
                )

    for side in (0, 1):

        @pl.when(exists(4 * side - 2))
        def _(side=side):
            m_copy(side, -1).wait_recv()

    def mid_scores(b, h, side, j):
        distance = -2 if side == 0 else 2
        cut = slice(h * DH, (h + 1) * DH)
        n = place(b, table[distance][0] + j, distance)
        return lax.dot_general(
            qb[b, :, cut], mid[side, n, :, cut], (((1,), (1,)), ((), ())),
            preferred_element_type=jnp.float32,
        ) * scale

    def mid_weights(sides):
        slots = [(side, j) for side in sides for j in range(table[2][1])]
        for b in range(blocks):
            for h in range(heads):
                scores = [mid_scores(b, h, side, j) for side, j in slots]
                old = peak[b, h]
                new = old
                for x in scores:
                    top = jnp.max(x, axis=1, keepdims=True)
                    new = jnp.maximum(new, jnp.broadcast_to(top, (BLOCK, DH)))
                fade = jnp.exp(old - new)
                whole = total[b, h] * fade
                for (side, j), x in zip(slots, scores):
                    weights = jnp.exp(x - new)
                    whole = whole + jnp.broadcast_to(
                        jnp.sum(weights, axis=1, keepdims=True), (BLOCK, DH)
                    )
                    held[side, j, b, h] = weights.astype(jnp.bfloat16)
                total[b, h] = 1.0 / whole
                numer[b, h] = numer[b, h] * fade

    def o_copy(o, h):
        to = lax.rem(s + o, blocks)
        return pltpu.make_async_remote_copy(
            src_ref=ob.at[to, h], dst_ref=out.at[:, head_cols(s, h)],
            send_sem=os_.at[o, h], recv_sem=or_.at[o, h],
            device_id={"space": to}, device_id_type=MESH,
        )

    def head_cols(i, h):
        return pl.ds(pl.multiple_of(i * width + h * DH, DH), DH)

    def keep(h):
        return pltpu.make_async_copy(ob.at[s, h], out.at[:, head_cols(s, h)], os_.at[0, h])

    def finish(sides):
        for h in range(heads):
            for side in sides:
                m_copy(side, h).wait_recv()
            for o in list(range(1, blocks)) + [0]:
                b = lax.rem(s + o, blocks)
                value = numer[b, h]
                for side in sides:
                    distance = -2 if side == 0 else 2
                    for j in range(table[2][1]):
                        n = place(b, table[distance][0] + j, distance)
                        value = value + jnp.dot(
                            held[side, j, b, h], midv[side, h, n],
                            preferred_element_type=jnp.float32,
                        )
                ob[b, h] = (value * total[b, h]).astype(jnp.bfloat16)
                if o:
                    o_copy(o, h).start()
                else:
                    keep(h).start()

    def last(sides):
        mid_weights(sides)
        finish(sides)

    pl.when(exists(-2) & exists(2))(lambda: last((0, 1)))
    pl.when(exists(-2) & ~exists(2))(lambda: last((0,)))
    pl.when(~exists(-2) & exists(2))(lambda: last((1,)))
    pl.when(~exists(-2) & ~exists(2))(lambda: last(()))

    for t in (0, 1, 2):
        for o in range(1, blocks):
            x_copy(t, o).wait_send()
    for i, step in enumerate(steps):

        @pl.when(exists(step))
        def _(i=i, step=step):
            list_copy(i, step).wait_send()

    for side in (0, 1):

        @pl.when(ahead(side))
        def _(side=side):
            for t in (0, 1):
                for o in range(blocks):
                    z_copy(side, t, o).wait_send()

        @pl.when(behind(side) & ahead(side))
        def _(side=side):
            for h in range(-1, heads):
                m_copy(side, h).wait_send()

        if use_far:

            @pl.when(exists(4 - 8 * side))
            def _(side=side):
                for t in (0, 1):
                    f_copy(side, t).wait_send()

    for h in range(heads):
        keep(h).wait()
        for o in range(1, blocks):
            o_copy(o, h).wait_send()
            pltpu.make_async_remote_copy(
                src_ref=ob.at[s, h], dst_ref=out.at[:, head_cols(lax.rem(s - o + blocks, blocks), h)],
                send_sem=os_.at[o, h], recv_sem=or_.at[o, h],
                device_id={"space": lax.rem(s + o, blocks)}, device_id_type=MESH,
            ).wait_recv()


def local(frames, blocks, queries, key_rows, value_rows, block_lists):
    rows, columns = queries.shape
    width = columns // blocks
    heads = width // DH
    lists = block_lists[0]
    table = group_table(blocks)
    u2, u4 = table[2][2], table[4][2]
    far_rows = BLOCK if frames > 4 else 16
    dma = pltpu.SemaphoreType.DMA
    bf = jnp.bfloat16
    return pl.pallas_call(
        functools.partial(kernel, frames, blocks),
        out_shape=jax.ShapeDtypeStruct(queries.shape, queries.dtype),
        in_specs=[pl.BlockSpec(memory_space=pltpu.HBM)] * 4,
        out_specs=pl.BlockSpec(memory_space=pl.ANY),
        scratch_shapes=[
            pltpu.SMEM(lists.shape, jnp.int32),
            pltpu.VMEM((blocks, BLOCK, width), bf),
            pltpu.VMEM((2, blocks, BLOCK, width), bf),
            pltpu.VMEM((2, 2, blocks, BLOCK, width), bf),
            pltpu.VMEM((2, u2, BLOCK, width), bf),
            pltpu.VMEM((2, u2, BLOCK, width), bf),
            pltpu.VMEM((2, heads, u2, BLOCK, DH), bf),
            pltpu.VMEM((2, heads, u2, BLOCK, DH), bf),
            pltpu.VMEM((2, 2, u4, far_rows, width), bf),
            pltpu.VMEM((2, 2, u4, far_rows, width), bf),
            pltpu.VMEM((4,) + lists.shape, jnp.int32),
            pltpu.VMEM((blocks, heads, BLOCK, DH), bf),
            pltpu.VMEM((blocks, heads, BLOCK, DH), jnp.float32),
            pltpu.VMEM((blocks, heads, BLOCK, DH), jnp.float32),
            pltpu.VMEM((blocks, heads, BLOCK, DH), jnp.float32),
            pltpu.VMEM((2, table[2][1], blocks, heads, BLOCK, DH), bf),
            pltpu.VMEM((3, blocks, BLOCK, width), bf),
            dma((3, blocks)),
            dma((5,)),
            dma((3, blocks)),
            dma((3, blocks)),
            dma((2, 2, blocks)),
            dma((2, 2, blocks)),
            dma((2, 1 + heads)),
            dma((2, 1 + heads)),
            dma((2, 2)),
            dma((2, 2)),
            dma((4,)),
            dma((4,)),
            dma((blocks, heads)),
            dma((blocks, heads)),
        ],
        compiler_params=pltpu.CompilerParams(
            collective_id=0, has_side_effects=True, vmem_limit_bytes=48 * 1024 * 1024
        ),
    )(*[pltpu.with_memory_space_constraint(x, pltpu.HBM) for x in (queries, key_rows, value_rows, lists)])


def short_kernel(
    frames, blocks, q, k, v, lists_v, out,
    qh, kh, vh, kv, xq, qn, mid, pick, held, rt, po, ps, pin, lin, own_o, own_l, heard,
    loc_sem, xs, xr, qs, qr, ks, kr, ps_, pr, ss, sr, ls, lr, cs, cr, ready,
):
    f = lax.axis_index("tm")
    s = lax.axis_index("space")
    other = 1 - s
    width = qn.shape[3]
    heads = width // DH
    table = group_table(blocks)
    factor = DH ** -0.5 * LOG2E
    sides = (0, 1)
    early = f < frames // 2
    core = lax.axis_index("head")
    lead = core == 1

    def exists(step):
        return (f + step >= 0) & (f + step < frames)

    def step(side):
        return 2 * side - 1

    def ex(side):
        return exists(step(side))

    def half(i):
        return pl.ds(pl.multiple_of(i * width, width), width)

    def head_of(i, h):
        return pl.ds(pl.multiple_of(i * width + h * DH, DH), DH)

    def cut(h):
        return slice(h * DH, (h + 1) * DH)

    def remote(src, dst, send, recv, **where):
        return pltpu.make_async_remote_copy(
            src_ref=src, dst_ref=dst, send_sem=send, recv_sem=recv,
            device_id=where, device_id_type=MESH,
        )

    local = [
        pltpu.make_async_copy(q, qh, loc_sem.at[0]),
        pltpu.make_async_copy(k, kh, loc_sem.at[1]),
        pltpu.make_async_copy(v, vh, loc_sem.at[2]),
    ]
    for t in (0, 1):
        for h in range(heads):
            local.append(pltpu.make_async_copy(
                (k, v)[t].at[:, head_of(s, h)], kv[t][h].at[s], loc_sem.at[3 + t * heads + h]
            ))
    for copy in local:
        copy.start()

    def late(frame):
        return frame >= frames // 2

    def greet(semaphore, d):
        pl.semaphore_signal(semaphore, inc=1, device_id={"tm": f + d}, device_id_type=MESH)

    barrier = pltpu.get_barrier_semaphore()
    pl.semaphore_signal(barrier, inc=1, device_id={"space": other}, device_id_type=MESH)
    pl.when(exists(2) & lead)(lambda: greet(barrier, 2))

    @pl.when(~lead)
    def _():
        pl.semaphore_signal(barrier, inc=1, device_id={"head": 1}, device_id_type=MESH)

    pl.when(exists(1))(lambda: greet(barrier, 1))
    pl.when(exists(-1) & ~late(f))(lambda: greet(barrier, -1))
    greeted = 1 + exists(-1).astype(jnp.int32)
    greeted = greeted + (exists(-2) & lead).astype(jnp.int32) + lead.astype(jnp.int32)
    pl.semaphore_wait(barrier, greeted + (exists(1) & ~late(f + 1)).astype(jnp.int32))
    pl.when(exists(-1) & late(f))(lambda: greet(ready.at[0], -1))
    pl.when(exists(-2) & lead)(lambda: greet(ready.at[1], -2))

    def list_copy(i, d):
        return remote(lists_v, heard.at[i ^ 1], ls.at[i], lr.at[i ^ 1], tm=f + d)

    def list_wait(i, d):
        return remote(lists_v, heard.at[i], ls.at[i], lr.at[i], tm=f + d)

    list_steps = (-1, 1, -2, 2)

    places = (s, other)

    def x_copy(t, h):
        src = (k, v, q)[t].at[:, head_of(other, h)]
        dst = xq.at[h] if t == 2 else kv[t][h].at[s]
        return remote(src, dst, xs.at[t, h], xr.at[t, h], space=other)

    def x_wait(t, h):
        src = (k, v, q)[t].at[:, head_of(other, h)]
        dst = xq.at[h] if t == 2 else kv[t][h].at[other]
        return remote(src, dst, xs.at[t, h], xr.at[t, h], space=other)

    def q_copy(side, i, to=None):
        to = 1 - side if to is None else to
        if i < 2:
            part = width // 2
            src = q.at[:, pl.ds(pl.multiple_of(s * width + i * part, DH), part)]
            dst = qn.at[to, 0, :, slice(i * part, (i + 1) * part)]
        else:
            src, dst = xq.at[i - 2], qn.at[to, 1, :, cut(i - 2)]
        return remote(src, dst, qs.at[side, i], qr.at[to, i], tm=f + step(side))

    def k_copy(side, t, h, to=None):
        to = 1 - side if to is None else to
        return remote(
            pick.at[side, t, :, cut(h)], mid.at[to, t, :, cut(h)], ks.at[side, t, h],
            kr.at[to, t, h], tm=f + step(side),
        )

    def p_copy(side, i, h, to=None):
        to = 1 - side if to is None else to
        return remote(
            po.at[side, i, h], pin.at[to, i, h], ps_.at[side, i, h], pr.at[to, i, h],
            tm=f + step(side), space=places[i],
        )

    def s_copy(side, i, h, to=None):
        to = 1 - side if to is None else to
        return remote(
            ps.at[side, i, h], lin.at[to, i, h], ss.at[side, i, h], sr.at[to, i, h],
            tm=f + step(side), space=places[i],
        )

    def on_sides(run, there=ex):
        for side in sides:
            pl.when(there(side))(functools.partial(run, side))

    def wait_sides(copy, *key, there=ex):
        on_sides(lambda side: copy(side, *key, to=side).wait_recv(), there)

    @pl.when(exists(-1))
    def _():
        pl.when(lead)(lambda: list_copy(0, -1).start())
        q_copy(0, 0).start()
        q_copy(0, 1).start()

    pl.when(exists(-2) & lead)(lambda: list_copy(2, -2).start())

    def start_queries(span):
        for h in span:
            x_copy(2, h).start()

    start_queries(range(FIRST))
    pl.when(early)(lambda: start_queries(range(FIRST, heads)))
    for h in range(heads):
        for t in (0, 1):
            x_copy(t, h).start()
    pl.when(~early)(lambda: start_queries(range(FIRST, heads)))

    @pl.when(exists(1))
    def _():
        pl.when(late(f + 1))(lambda: pl.semaphore_wait(ready.at[0], 1))
        pl.when(lead)(lambda: list_copy(1, 1).start())
        q_copy(1, 0).start()

        @pl.when(exists(2) & lead)
        def _():
            pl.semaphore_wait(ready.at[1], 1)
            list_copy(3, 2).start()

        q_copy(1, 1).start()

    for copy in local:
        copy.wait()

    def scores(keys, queries):
        return lax.dot_general(
            keys, queries, (((1,), (1,)), ((), ())), preferred_element_type=jnp.float32
        ) * factor

    def gathered(values, weights):
        return lax.dot_general(
            values, weights, (((0,), (0,)), ((), ())), preferred_element_type=jnp.float32
        )

    def home(i, h):
        columns = head_of(places[i], h)
        x = scores(kh[:, columns], qh[:, columns])
        top = jnp.max(x, axis=0, keepdims=True)
        weights = jnp.exp2(x - top)
        whole = jnp.sum(weights, axis=0, keepdims=True)
        own_o[i, h] = gathered(vh[:, columns], weights.astype(jnp.bfloat16)) * (1.0 / whole)
        own_l[i, h : h + 1] = top + jnp.log2(whole)

    def send_pick(t, h):
        x_wait(t, h).wait_recv()

        def run(side):
            n = heard[2 + side, 0, table[-2 * step(side)][0]]
            pick[side, t, :, cut(h)] = kv[t][h][n]
            k_copy(side, t, h).start()

        on_sides(run, lambda side: exists(2 * step(side)))

    def near_block(side, i):
        return heard[side, places[i], table[-step(side)][0]]

    def weigh(side, i, h, both):
        queries = qn[side, i, :, cut(h)]
        x = [scores(kv[0][h][near_block(side, i)], queries)]
        if both:
            x.append(scores(mid[1 - side, 0, :, cut(h)], queries))
        top = functools.reduce(jnp.maximum, [jnp.max(y, axis=0, keepdims=True) for y in x])
        whole = jnp.zeros_like(top)
        for j, y in enumerate(x):
            weights = jnp.exp2(y - top)
            whole = whole + jnp.sum(weights, axis=0, keepdims=True)
            held[side, i, h, j] = weights.astype(jnp.bfloat16)
        rt[side, i, h : h + 1] = 1.0 / whole
        ps[side, i, h] = top + jnp.log2(whole)

    def answer(side, i, h, both):
        value = gathered(kv[1][h][near_block(side, i)], held[side, i, h, 0])
        if both:
            value = value + gathered(mid[1 - side, 1, :, cut(h)], held[side, i, h, 1])
        po[side, i, h] = (value * rt[side, i, h : h + 1]).astype(jnp.bfloat16)

    inner = ex(0) & ex(1)

    def between(side):
        return inner

    def serve(side, h, both):
        if h == 0:
            q_copy(side, 0, to=side).wait_recv()
            q_copy(side, 1, to=side).wait_recv()
        q_copy(side, 2 + h, to=side).wait_recv()
        if both:
            k_copy(side, 0, h, to=1 - side).wait_recv()
        for i in range(blocks):
            weigh(side, i, h, both)
        if both:
            k_copy(side, 1, h, to=1 - side).wait_recv()
        for i in range(blocks):
            answer(side, i, h, both)

    def reply(side, h):
        for i in range(blocks):
            s_copy(side, i, h).start()
        for i in reversed(range(blocks)):
            p_copy(side, i, h).start()

    def forward(h):
        send_pick(0, h)
        send_pick(1, h)

    def forward_queries(h):
        x_wait(2, h).wait_recv()
        on_sides(lambda side: q_copy(side, 2 + h).start())

    for h in range(heads):
        home(0, h)

    def chip_copy(i):
        return remote(heard.at[i], heard.at[i], cs.at[i], cr.at[i], head=0)

    def wait_lists():
        for i, d in enumerate(list_steps):

            @pl.when(exists(d) & lead)
            def _():
                list_wait(i, d).wait_recv()
                chip_copy(i).start()

            pl.when(exists(d) & ~lead)(lambda: chip_copy(i).wait_recv())

    @pl.when(early)
    def _():
        for h in range(heads):
            forward_queries(h)
            home(1, h)
        wait_lists()
        for h in range(heads):
            forward(h)

            @pl.when(inner)
            def _(h=h):
                serve(0, h, True)
                reply(0, h)

        for both, there in ((True, inner), (False, ~inner)):

            @pl.when(there)
            def _(both=both):
                for h in range(heads):
                    serve(1, h, both)
                    reply(1, h)

    @pl.when(~early)
    def _():
        for h in range(FIRST):
            forward_queries(h)
            home(1, h)
        wait_lists()
        forward(0)
        for h in range(FIRST, heads):
            home(1, h)
        for h in range(1, heads):
            forward(h)
            if h >= 2:
                pl.when(inner)(functools.partial(serve, 0, h - 2, True))

        for h in range(FIRST, heads):
            forward_queries(h)
        pl.when(inner)(functools.partial(serve, 0, heads - 2, True))

        @pl.when(inner)
        def _():
            for h in range(heads):
                if h == heads - 1:
                    serve(0, h, True)
                reply(0, h)
            for h in range(heads):
                serve(1, h, True)
                reply(1, h)

        @pl.when(~inner)
        def _():
            for h in range(heads):
                serve(0, h, False)
                reply(0, h)

    def merge(i, h, parts):
        rows = [own_l[i, h : h + 1]] + [lin[side, i, h] for side in parts]
        top = functools.reduce(jnp.maximum, rows)
        shares = [jnp.exp2(row - top) for row in rows]
        scale = 1.0 / functools.reduce(jnp.add, shares)
        value = own_o[i, h] * (shares[0] * scale)
        for side, share in zip(parts, shares[1:]):
            value = value + pin[side, i, h].astype(jnp.float32) * (share * scale)
        out[:, head_of(places[i], h)] = value.T.astype(jnp.bfloat16)

    for h in range(heads):
        for i in range(blocks):
            wait_sides(s_copy, i, h)
            wait_sides(p_copy, i, h)
            pl.when(ex(0) & ex(1))(lambda: merge(i, h, (0, 1)))
            pl.when(ex(0) & ~ex(1))(lambda: merge(i, h, (0,)))
            pl.when(~ex(0) & ex(1))(lambda: merge(i, h, (1,)))
            pl.when(~ex(0) & ~ex(1))(lambda: merge(i, h, ()))

    for t in range(3):
        for h in range(heads):
            x_copy(t, h).wait_send()
    for i, d in enumerate(list_steps):

        @pl.when(exists(d) & lead)
        def _(i=i, d=d):
            list_copy(i, d).wait_send()
            chip_copy(i).wait_send()

    @on_sides
    def _(side):
        for i in range(2 + heads):
            q_copy(side, i).wait_send()
        for i in range(blocks):
            for h in range(heads):
                s_copy(side, i, h).wait_send()
                p_copy(side, i, h).wait_send()

        @pl.when(exists(2 * step(side)))
        def _():
            for t in (0, 1):
                for h in range(heads):
                    k_copy(side, t, h).wait_send()


def short(frames, blocks, queries, key_rows, value_rows, block_lists):
    rows, columns = queries.shape
    width = columns // blocks
    heads = width // DH
    lists = block_lists[0]
    dma = pltpu.SemaphoreType.DMA
    bf, f32 = jnp.bfloat16, jnp.float32
    vmem = pltpu.VMEM
    return pl.pallas_call(
        functools.partial(short_kernel, frames, blocks),
        out_shape=jax.ShapeDtypeStruct(queries.shape, queries.dtype),
        in_specs=[pl.BlockSpec(memory_space=pltpu.HBM)] * 4,
        out_specs=pl.BlockSpec(memory_space=pltpu.VMEM),
        scratch_shapes=[
            vmem((rows, columns), bf),
            vmem((rows, columns), bf),
            vmem((rows, columns), bf),
            [[vmem((blocks, BLOCK, DH), bf)] * heads] * 2,
            vmem((heads, BLOCK, DH), bf),
            vmem((2, blocks, BLOCK, width), bf),
            vmem((2, 2, BLOCK, width), bf),
            vmem((2, 2, BLOCK, width), bf),
            vmem((2, blocks, heads, 2, BLOCK, BLOCK), bf),
            vmem((2, blocks, 8, BLOCK), f32),
            vmem((2, blocks, heads, DH, BLOCK), bf),
            vmem((2, blocks, heads, 1, BLOCK), f32),
            vmem((2, blocks, heads, DH, BLOCK), bf),
            vmem((2, blocks, heads, 1, BLOCK), f32),
            vmem((blocks, heads, DH, BLOCK), f32),
            vmem((blocks, 8, BLOCK), f32),
            pltpu.SMEM((4,) + lists.shape, jnp.int32),
            dma((3 + 2 * heads,)),
            dma((3, heads)),
            dma((3, heads)),
            dma((2, 2 + heads)),
            dma((2, 2 + heads)),
            dma((2, 2, heads)),
            dma((2, 2, heads)),
            dma((2, blocks, heads)),
            dma((2, blocks, heads)),
            dma((2, blocks, heads)),
            dma((2, blocks, heads)),
            dma((4,)),
            dma((4,)),
            dma((4,)),
            dma((4,)),
            pltpu.SemaphoreType.REGULAR((2,)),
        ],
        compiler_params=pltpu.CompilerParams(
            collective_id=1, has_side_effects=True, vmem_limit_bytes=48 * 1024 * 1024
        ),
    )(*[pltpu.with_memory_space_constraint(x, pltpu.HBM) for x in (queries, key_rows, value_rows, lists)])


def solution(mesh):
    in_specs = (
        P(("groups", "tm", "space"), "head"),
        P(("groups", "tm", "space"), "head"),
        P(("groups", "tm", "space"), "head"),
        P(("groups", "tm"), None, None),
    )
    out_specs = P(("groups", "tm", "space"), "head")
    frames, blocks = mesh.shape["tm"], mesh.shape["space"]
    body = functools.partial(short if frames <= 4 and blocks == 2 else local, frames, blocks)
    return jax.shard_map(body, mesh=mesh, in_specs=in_specs, out_specs=out_specs, check_vma=False)
```

```python
import functools

import jax
import jax.numpy as jnp
from jax import lax
from jax.experimental import pallas as pl
from jax.experimental.pallas import tpu as pltpu
from jax.sharding import PartitionSpec as P

DH = 128
BLOCK = 128
MESH = pl.DeviceIdType.MESH
LOG2E = 1.4426950408889634
FIRST = 1


def group_table(blocks):
    near, middle, far = max(blocks // 2, 1), max(blocks // 4, 1), max(blocks // 8, 1)
    table = {0: (0, near, blocks)}
    start = near
    for step, count, union in (
        (1, near, blocks),
        (2, middle, max(blocks // 2, 1)),
        (4, far, max(blocks // 4, 1)),
    ):
        table[-step] = (start, count, union)
        table[step] = (start + count, count, union)
        start += 2 * count
    return table


def kernel(
    frames, blocks, q, k, v, lists_v, out,
    lists_s, qb, own, near, pick2, mid, pick2v, midv, pick4, far, heard, ob, peak, total, numer, held, stage, stage_sem,
    loc_sem, xs, xr, zs, zr, ms, mr, fs, fr, ls, lr, os_, or_,
):
    f = lax.axis_index("tm")
    s = lax.axis_index("space")
    width = qb.shape[2]
    heads = width // DH
    table = group_table(blocks)
    use_far = frames > 4
    scale = DH ** -0.5

    def cols(i):
        return pl.ds(pl.multiple_of(i * width, width), width)

    def at(step):
        return {"tm": f + step}

    def exists(step):
        return (f + step >= 0) & (f + step < frames)

    steps = (-1, 1) + ((-4, 4) if use_far else ())

    local = [
        pltpu.make_async_copy(q.at[:, cols(s)], qb.at[s], loc_sem.at[0]),
        pltpu.make_async_copy(k.at[:, cols(s)], own.at[0, s], loc_sem.at[1]),
        pltpu.make_async_copy(v.at[:, cols(s)], own.at[1, s], loc_sem.at[2]),
        pltpu.make_async_copy(lists_v, lists_s, loc_sem.at[3]),
    ]
    for t in range(3):
        for o in range(1, blocks):
            local.append(pltpu.make_async_copy(
                (k, v, q)[t].at[:, cols(lax.rem(s + o, blocks))], stage.at[t, o], stage_sem.at[t, o]
            ))
    for copy in local:
        copy.start()

    barrier = pltpu.get_barrier_semaphore()
    for o in range(1, blocks):
        pl.semaphore_signal(
            barrier, inc=1, device_id={"space": lax.rem(s + o, blocks)}, device_id_type=MESH
        )
    greeted = blocks - 1
    for step in steps:

        @pl.when(exists(step))
        def _(step=step):
            pl.semaphore_signal(barrier, inc=1, device_id=at(step), device_id_type=MESH)

        greeted = greeted + exists(step).astype(jnp.int32)
    for copy in local:
        copy.wait()
    pl.semaphore_wait(barrier, greeted)

    def list_copy(i, step):
        return pltpu.make_async_remote_copy(
            src_ref=lists_v, dst_ref=heard.at[i ^ 1], send_sem=ls.at[i], recv_sem=lr.at[i ^ 1],
            device_id=at(step), device_id_type=MESH,
        )

    def list_wait(i):
        return pltpu.make_async_remote_copy(
            src_ref=lists_v, dst_ref=heard.at[i], send_sem=ls.at[i], recv_sem=lr.at[i],
            device_id=at(steps[i]), device_id_type=MESH,
        )

    def x_copy(t, o):
        to = lax.rem(s + o, blocks)
        src = stage.at[t, o]
        dst = qb.at[s] if t == 2 else own.at[t, s]
        return pltpu.make_async_remote_copy(
            src_ref=src, dst_ref=dst, send_sem=xs.at[t, o], recv_sem=xr.at[t, o],
            device_id={"space": to}, device_id_type=MESH,
        )

    def z_copy(side, t, o):
        b = lax.rem(s - o + blocks, blocks)
        src = own.at[t, b]
        return pltpu.make_async_remote_copy(
            src_ref=src, dst_ref=near.at[side, t, b], send_sem=zs.at[side, t, o],
            recv_sem=zr.at[side, t, o], device_id=at(1 - 2 * side), device_id_type=MESH,
        )

    def m_copy(side, h):
        src, dst = (pick2.at[side], mid.at[side]) if h < 0 else (pick2v.at[side, h], midv.at[side, h])
        return pltpu.make_async_remote_copy(
            src_ref=src, dst_ref=dst, send_sem=ms.at[side, h + 1],
            recv_sem=mr.at[side, h + 1], device_id=at(1 - 2 * side), device_id_type=MESH,
        )

    def f_copy(side, t):
        return pltpu.make_async_remote_copy(
            src_ref=pick4.at[side, t], dst_ref=far.at[side, t], send_sem=fs.at[side, t],
            recv_sem=fr.at[side, t], device_id=at(4 - 8 * side), device_id_type=MESH,
        )

    def ahead(side):
        return exists(1 - 2 * side)

    def behind(side):
        return exists(2 * side - 1)

    for t in (0, 1):
        for o in range(1, blocks):
            x_copy(t, o).start()
        for side in (0, 1):

            @pl.when(ahead(side))
            def _(side=side, t=t):
                z_copy(side, t, 0).start()

    for i, step in enumerate(steps):

        @pl.when(exists(step))
        def _(i=i, step=step):
            list_copy(i, step).start()

    for t in (0, 1):
        for o in range(1, blocks):
            x_copy(t, o).wait_recv()
            for side in (0, 1):

                @pl.when(ahead(side))
                def _(side=side, t=t, o=o):
                    z_copy(side, t, o).start()

    for o in range(1, blocks):
        x_copy(2, o).start()

    def choose(i, distance, load, store):
        first, count, union = table[distance]
        seen, rank = [], []
        before = jnp.zeros((1, 1), jnp.int32)
        for c in range(blocks):
            hit = jnp.zeros((1, 1), jnp.int32)
            for b in range(blocks):
                for j in range(first, first + count):
                    hit = jnp.maximum(hit, (heard[i, b : b + 1, j : j + 1] == c).astype(jnp.int32))
            seen.append(hit)
            rank.append(before)
            before = before + hit
        for u in range(union):
            value = load(blocks - 1).astype(jnp.float32)
            for c in range(blocks - 1):
                mask = jnp.where(rank[c] == u, seen[c], 0)
                mask = jnp.broadcast_to(mask, value.shape)
                value = jnp.where(mask == 1, load(c).astype(jnp.float32), value)
            store(u, value.astype(jnp.bfloat16))

    def place(b, slot, distance):
        first, count, union = table[distance]
        number = lists_s[b, slot]
        if union == blocks:
            return number
        if union == 1:
            return 0
        position = jnp.int32(0)
        for c in range(blocks - 1):
            seen = jnp.int32(0)
            for other in range(blocks):
                for j in range(first, first + count):
                    seen = jnp.maximum(seen, (lists_s[other, j] == c).astype(jnp.int32))
            position = position + jnp.where(c < number, seen, 0)
        return position

    def attend(distance, keys, values, fresh=False):
        first, count, union = table[distance]
        for b in range(blocks):
            for j in range(count):
                n = place(b, first + j, distance)
                for h in range(heads):
                    cut = slice(h * DH, (h + 1) * DH)
                    scores = lax.dot_general(
                        qb[b, :, cut], keys(n, cut), (((1,), (1,)), ((), ())),
                        preferred_element_type=jnp.float32,
                    ) * scale
                    top = jnp.max(scores, axis=1, keepdims=True)
                    if fresh and j == 0:
                        weights = jnp.exp(scores - top)
                        peak[b, h] = jnp.broadcast_to(top, (BLOCK, DH))
                        total[b, h] = jnp.broadcast_to(
                            jnp.sum(weights, axis=1, keepdims=True), (BLOCK, DH)
                        )
                        numer[b, h] = jnp.dot(
                            weights.astype(jnp.bfloat16), values(n, cut),
                            preferred_element_type=jnp.float32,
                        )
                    else:
                        old = peak[b, h]
                        new = jnp.maximum(old, jnp.broadcast_to(top, (BLOCK, DH)))
                        fade = jnp.exp(old - new)
                        weights = jnp.exp(scores - new)
                        peak[b, h] = new
                        total[b, h] = total[b, h] * fade + jnp.broadcast_to(
                            jnp.sum(weights, axis=1, keepdims=True), (BLOCK, DH)
                        )
                        numer[b, h] = numer[b, h] * fade + jnp.dot(
                            weights.astype(jnp.bfloat16), values(n, cut),
                            preferred_element_type=jnp.float32,
                        )

    if use_far:
        for side in (0, 1):

            @pl.when(exists(4 - 8 * side))
            def _(side=side):
                i = 3 - side
                list_wait(i).wait_recv()
                for t in (0, 1):
                    choose(
                        i, -4 if side == 0 else 4,
                        lambda c: own[t, c],
                        lambda u, x: pick4.__setitem__((side, t, u), x),
                    )
                    f_copy(side, t).start()

    for i in (0, 1):

        @pl.when(exists(steps[i]))
        def _(i=i):
            list_wait(i).wait_recv()

    for side in (0, 1):

        @pl.when(behind(side))
        def _(side=side):
            for o in range(blocks):
                z_copy(side, 0, o).wait_recv()

        @pl.when(behind(side) & ahead(side))
        def _(side=side):
            choose(
                1 - side, -2 if side == 0 else 2,
                lambda c: near[side, 0, c],
                lambda u, x: pick2.__setitem__((side, u), x),
            )
            m_copy(side, -1).start()

    for o in range(1, blocks):
        x_copy(2, o).wait_recv()
    attend(0, lambda n, cut: own[0, n, :, cut], lambda n, cut: own[1, n, :, cut], fresh=True)

    for side in (0, 1):

        @pl.when(behind(side))
        def _(side=side):
            for o in range(blocks):
                z_copy(side, 1, o).wait_recv()

        @pl.when(behind(side) & ahead(side))
        def _(side=side):
            for h in range(heads):
                choose(
                    1 - side, -2 if side == 0 else 2,
                    lambda c: near[side, 1, c, :, h * DH : (h + 1) * DH],
                    lambda u, x: pick2v.__setitem__((side, h, u), x),
                )
                m_copy(side, h).start()

    for side in (0, 1):

        @pl.when(behind(side))
        def _(side=side):
            attend(
                -1 if side == 0 else 1,
                lambda n, cut: near[side, 0, n, :, cut], lambda n, cut: near[side, 1, n, :, cut],
            )

    if use_far:
        for side in (0, 1):

            @pl.when(exists(8 * side - 4))
            def _(side=side):
                for t in (0, 1):
                    f_copy(side, t).wait_recv()
                attend(
                    -4 if side == 0 else 4,
                    lambda n, cut: far[side, 0, n, :, cut], lambda n, cut: far[side, 1, n, :, cut],
                )

    for side in (0, 1):

        @pl.when(exists(4 * side - 2))
        def _(side=side):
            m_copy(side, -1).wait_recv()

    def mid_scores(b, h, side, j):
        distance = -2 if side == 0 else 2
        cut = slice(h * DH, (h + 1) * DH)
        n = place(b, table[distance][0] + j, distance)
        return lax.dot_general(
            qb[b, :, cut], mid[side, n, :, cut], (((1,), (1,)), ((), ())),
            preferred_element_type=jnp.float32,
        ) * scale

    def mid_weights(sides):
        slots = [(side, j) for side in sides for j in range(table[2][1])]
        for b in range(blocks):
            for h in range(heads):
                scores = [mid_scores(b, h, side, j) for side, j in slots]
                old = peak[b, h]
                new = old
                for x in scores:
                    top = jnp.max(x, axis=1, keepdims=True)
                    new = jnp.maximum(new, jnp.broadcast_to(top, (BLOCK, DH)))
                fade = jnp.exp(old - new)
                whole = total[b, h] * fade
                for (side, j), x in zip(slots, scores):
                    weights = jnp.exp(x - new)
                    whole = whole + jnp.broadcast_to(
                        jnp.sum(weights, axis=1, keepdims=True), (BLOCK, DH)
                    )
                    held[side, j, b, h] = weights.astype(jnp.bfloat16)
                total[b, h] = 1.0 / whole
                numer[b, h] = numer[b, h] * fade

    def o_copy(o, h):
        to = lax.rem(s + o, blocks)
        return pltpu.make_async_remote_copy(
            src_ref=ob.at[to, h], dst_ref=out.at[:, head_cols(s, h)],
            send_sem=os_.at[o, h], recv_sem=or_.at[o, h],
            device_id={"space": to}, device_id_type=MESH,
        )

    def head_cols(i, h):
        return pl.ds(pl.multiple_of(i * width + h * DH, DH), DH)

    def keep(h):
        return pltpu.make_async_copy(ob.at[s, h], out.at[:, head_cols(s, h)], os_.at[0, h])

    def finish(sides):
        for h in range(heads):
            for side in sides:
                m_copy(side, h).wait_recv()
            for o in list(range(1, blocks)) + [0]:
                b = lax.rem(s + o, blocks)
                value = numer[b, h]
                for side in sides:
                    distance = -2 if side == 0 else 2
                    for j in range(table[2][1]):
                        n = place(b, table[distance][0] + j, distance)
                        value = value + jnp.dot(
                            held[side, j, b, h], midv[side, h, n],
                            preferred_element_type=jnp.float32,
                        )
                ob[b, h] = (value * total[b, h]).astype(jnp.bfloat16)
                if o:
                    o_copy(o, h).start()
                else:
                    keep(h).start()

    def last(sides):
        mid_weights(sides)
        finish(sides)

    pl.when(exists(-2) & exists(2))(lambda: last((0, 1)))
    pl.when(exists(-2) & ~exists(2))(lambda: last((0,)))
    pl.when(~exists(-2) & exists(2))(lambda: last((1,)))
    pl.when(~exists(-2) & ~exists(2))(lambda: last(()))

    for t in (0, 1, 2):
        for o in range(1, blocks):
            x_copy(t, o).wait_send()
    for i, step in enumerate(steps):

        @pl.when(exists(step))
        def _(i=i, step=step):
            list_copy(i, step).wait_send()

    for side in (0, 1):

        @pl.when(ahead(side))
        def _(side=side):
            for t in (0, 1):
                for o in range(blocks):
                    z_copy(side, t, o).wait_send()

        @pl.when(behind(side) & ahead(side))
        def _(side=side):
            for h in range(-1, heads):
                m_copy(side, h).wait_send()

        if use_far:

            @pl.when(exists(4 - 8 * side))
            def _(side=side):
                for t in (0, 1):
                    f_copy(side, t).wait_send()

    for h in range(heads):
        keep(h).wait()
        for o in range(1, blocks):
            o_copy(o, h).wait_send()
            pltpu.make_async_remote_copy(
                src_ref=ob.at[s, h], dst_ref=out.at[:, head_cols(lax.rem(s - o + blocks, blocks), h)],
                send_sem=os_.at[o, h], recv_sem=or_.at[o, h],
                device_id={"space": lax.rem(s + o, blocks)}, device_id_type=MESH,
            ).wait_recv()


def local(frames, blocks, queries, key_rows, value_rows, block_lists):
    rows, columns = queries.shape
    width = columns // blocks
    heads = width // DH
    lists = block_lists[0]
    table = group_table(blocks)
    u2, u4 = table[2][2], table[4][2]
    far_rows = BLOCK if frames > 4 else 16
    dma = pltpu.SemaphoreType.DMA
    bf = jnp.bfloat16
    return pl.pallas_call(
        functools.partial(kernel, frames, blocks),
        out_shape=jax.ShapeDtypeStruct(queries.shape, queries.dtype),
        in_specs=[pl.BlockSpec(memory_space=pltpu.HBM)] * 4,
        out_specs=pl.BlockSpec(memory_space=pl.ANY),
        scratch_shapes=[
            pltpu.SMEM(lists.shape, jnp.int32),
            pltpu.VMEM((blocks, BLOCK, width), bf),
            pltpu.VMEM((2, blocks, BLOCK, width), bf),
            pltpu.VMEM((2, 2, blocks, BLOCK, width), bf),
            pltpu.VMEM((2, u2, BLOCK, width), bf),
            pltpu.VMEM((2, u2, BLOCK, width), bf),
            pltpu.VMEM((2, heads, u2, BLOCK, DH), bf),
            pltpu.VMEM((2, heads, u2, BLOCK, DH), bf),
            pltpu.VMEM((2, 2, u4, far_rows, width), bf),
            pltpu.VMEM((2, 2, u4, far_rows, width), bf),
            pltpu.VMEM((4,) + lists.shape, jnp.int32),
            pltpu.VMEM((blocks, heads, BLOCK, DH), bf),
            pltpu.VMEM((blocks, heads, BLOCK, DH), jnp.float32),
            pltpu.VMEM((blocks, heads, BLOCK, DH), jnp.float32),
            pltpu.VMEM((blocks, heads, BLOCK, DH), jnp.float32),
            pltpu.VMEM((2, table[2][1], blocks, heads, BLOCK, DH), bf),
            pltpu.VMEM((3, blocks, BLOCK, width), bf),
            dma((3, blocks)),
            dma((5,)),
            dma((3, blocks)),
            dma((3, blocks)),
            dma((2, 2, blocks)),
            dma((2, 2, blocks)),
            dma((2, 1 + heads)),
            dma((2, 1 + heads)),
            dma((2, 2)),
            dma((2, 2)),
            dma((4,)),
            dma((4,)),
            dma((blocks, heads)),
            dma((blocks, heads)),
        ],
        compiler_params=pltpu.CompilerParams(
            collective_id=0, has_side_effects=True, vmem_limit_bytes=48 * 1024 * 1024
        ),
    )(*[pltpu.with_memory_space_constraint(x, pltpu.HBM) for x in (queries, key_rows, value_rows, lists)])


def short_kernel(
    frames, blocks, q, k, v, lists_v, out,
    qh, kh, vh, kv, xq, qn, mid, pick, held, rt, po, ps, pin, lin, own_o, own_l, heard,
    loc_sem, xs, xr, qs, qr, ks, kr, ps_, pr, ss, sr, ls, lr, cs, cr, ready,
):
    f = lax.axis_index("tm")
    s = lax.axis_index("space")
    other = 1 - s
    width = qn.shape[3]
    heads = width // DH
    table = group_table(blocks)
    factor = DH ** -0.5 * LOG2E
    sides = (0, 1)
    early = f < frames // 2
    core = lax.axis_index("head")
    lead = core == 1

    def exists(step):
        return (f + step >= 0) & (f + step < frames)

    def step(side):
        return 2 * side - 1

    def ex(side):
        return exists(step(side))

    def half(i):
        return pl.ds(pl.multiple_of(i * width, width), width)

    def head_of(i, h):
        return pl.ds(pl.multiple_of(i * width + h * DH, DH), DH)

    def cut(h):
        return slice(h * DH, (h + 1) * DH)

    def remote(src, dst, send, recv, **where):
        return pltpu.make_async_remote_copy(
            src_ref=src, dst_ref=dst, send_sem=send, recv_sem=recv,
            device_id=where, device_id_type=MESH,
        )

    local = [
        pltpu.make_async_copy(q, qh, loc_sem.at[0]),
        pltpu.make_async_copy(k, kh, loc_sem.at[1]),
        pltpu.make_async_copy(v, vh, loc_sem.at[2]),
    ]
    for t in (0, 1):
        for h in range(heads):
            local.append(pltpu.make_async_copy(
                (k, v)[t].at[:, head_of(s, h)], kv[t][h].at[s], loc_sem.at[3 + t * heads + h]
            ))
    for copy in local:
        copy.start()

    def late(frame):
        return frame >= frames // 2

    def greet(semaphore, d):
        pl.semaphore_signal(semaphore, inc=1, device_id={"tm": f + d}, device_id_type=MESH)

    barrier = pltpu.get_barrier_semaphore()
    pl.semaphore_signal(barrier, inc=1, device_id={"space": other}, device_id_type=MESH)
    pl.when(exists(2) & lead)(lambda: greet(barrier, 2))

    @pl.when(~lead)
    def _():
        pl.semaphore_signal(barrier, inc=1, device_id={"head": 1}, device_id_type=MESH)

    pl.when(exists(1))(lambda: greet(barrier, 1))
    pl.when(exists(-1) & ~late(f))(lambda: greet(barrier, -1))
    greeted = 1 + exists(-1).astype(jnp.int32)
    greeted = greeted + (exists(-2) & lead).astype(jnp.int32) + lead.astype(jnp.int32)
    pl.semaphore_wait(barrier, greeted + (exists(1) & ~late(f + 1)).astype(jnp.int32))
    pl.when(exists(-1) & late(f))(lambda: greet(ready.at[0], -1))
    pl.when(exists(-2) & lead)(lambda: greet(ready.at[1], -2))

    def list_copy(i, d):
        return remote(lists_v, heard.at[i ^ 1], ls.at[i], lr.at[i ^ 1], tm=f + d)

    def list_wait(i, d):
        return remote(lists_v, heard.at[i], ls.at[i], lr.at[i], tm=f + d)

    list_steps = (-1, 1, -2, 2)

    places = (s, other)

    def x_copy(t, h):
        src = (k, v, q)[t].at[:, head_of(other, h)]
        dst = xq.at[h] if t == 2 else kv[t][h].at[s]
        return remote(src, dst, xs.at[t, h], xr.at[t, h], space=other)

    def x_wait(t, h):
        src = (k, v, q)[t].at[:, head_of(other, h)]
        dst = xq.at[h] if t == 2 else kv[t][h].at[other]
        return remote(src, dst, xs.at[t, h], xr.at[t, h], space=other)

    def q_copy(side, i, to=None):
        to = 1 - side if to is None else to
        if i < 2:
            part = width // 2
            src = q.at[:, pl.ds(pl.multiple_of(s * width + i * part, DH), part)]
            dst = qn.at[to, 0, :, slice(i * part, (i + 1) * part)]
        else:
            src, dst = xq.at[i - 2], qn.at[to, 1, :, cut(i - 2)]
        return remote(src, dst, qs.at[side, i], qr.at[to, i], tm=f + step(side))

    def k_copy(side, t, h, to=None):
        to = 1 - side if to is None else to
        return remote(
            pick.at[side, t, :, cut(h)], mid.at[to, t, :, cut(h)], ks.at[side, t, h],
            kr.at[to, t, h], tm=f + step(side),
        )

    def p_copy(side, i, h, to=None):
        to = 1 - side if to is None else to
        return remote(
            po.at[side, i, h], pin.at[to, i, h], ps_.at[side, i, h], pr.at[to, i, h],
            tm=f + step(side), space=places[i],
        )

    def s_copy(side, i, h, to=None):
        to = 1 - side if to is None else to
        return remote(
            ps.at[side, i, h], lin.at[to, i, h], ss.at[side, i, h], sr.at[to, i, h],
            tm=f + step(side), space=places[i],
        )

    def on_sides(run, there=ex):
        for side in sides:
            pl.when(there(side))(functools.partial(run, side))

    def wait_sides(copy, *key, there=ex):
        on_sides(lambda side: copy(side, *key, to=side).wait_recv(), there)

    @pl.when(exists(-1))
    def _():
        pl.when(lead)(lambda: list_copy(0, -1).start())
        q_copy(0, 0).start()
        q_copy(0, 1).start()

    pl.when(exists(-2) & lead)(lambda: list_copy(2, -2).start())

    def start_queries(span):
        for h in span:
            x_copy(2, h).start()

    start_queries(range(FIRST))
    pl.when(early)(lambda: start_queries(range(FIRST, heads)))
    for h in range(heads):
        for t in (0, 1):
            x_copy(t, h).start()
    pl.when(~early)(lambda: start_queries(range(FIRST, heads)))

    @pl.when(exists(1))
    def _():
        pl.when(late(f + 1))(lambda: pl.semaphore_wait(ready.at[0], 1))
        pl.when(lead)(lambda: list_copy(1, 1).start())
        q_copy(1, 0).start()

        @pl.when(exists(2) & lead)
        def _():
            pl.semaphore_wait(ready.at[1], 1)
            list_copy(3, 2).start()

        q_copy(1, 1).start()

    for copy in local:
        copy.wait()

    def scores(keys, queries):
        return lax.dot_general(
            keys, queries, (((1,), (1,)), ((), ())), preferred_element_type=jnp.float32
        ) * factor

    def gathered(values, weights):
        return lax.dot_general(
            values, weights, (((0,), (0,)), ((), ())), preferred_element_type=jnp.float32
        )

    def home(i, h):
        columns = head_of(places[i], h)
        x = scores(kh[:, columns], qh[:, columns])
        top = jnp.max(x, axis=0, keepdims=True)
        weights = jnp.exp2(x - top)
        whole = jnp.sum(weights, axis=0, keepdims=True)
        own_o[i, h] = gathered(vh[:, columns], weights.astype(jnp.bfloat16)) * (1.0 / whole)
        own_l[i, h : h + 1] = top + jnp.log2(whole)

    def send_pick(t, h):
        x_wait(t, h).wait_recv()

        def run(side):
            n = heard[2 + side, 0, table[-2 * step(side)][0]]
            pick[side, t, :, cut(h)] = kv[t][h][n]
            k_copy(side, t, h).start()

        on_sides(run, lambda side: exists(2 * step(side)))

    def near_block(side, i):
        return heard[side, places[i], table[-step(side)][0]]

    def weigh(side, i, h, both):
        queries = qn[side, i, :, cut(h)]
        x = [scores(kv[0][h][near_block(side, i)], queries)]
        if both:
            x.append(scores(mid[1 - side, 0, :, cut(h)], queries))
        top = functools.reduce(jnp.maximum, [jnp.max(y, axis=0, keepdims=True) for y in x])
        whole = jnp.zeros_like(top)
        for j, y in enumerate(x):
            weights = jnp.exp2(y - top)
            whole = whole + jnp.sum(weights, axis=0, keepdims=True)
            held[side, i, h, j] = weights.astype(jnp.bfloat16)
        rt[side, i, h : h + 1] = 1.0 / whole
        ps[side, i, h] = top + jnp.log2(whole)

    def answer(side, i, h, both):
        value = gathered(kv[1][h][near_block(side, i)], held[side, i, h, 0])
        if both:
            value = value + gathered(mid[1 - side, 1, :, cut(h)], held[side, i, h, 1])
        po[side, i, h] = (value * rt[side, i, h : h + 1]).astype(jnp.bfloat16)

    inner = ex(0) & ex(1)

    def between(side):
        return inner

    def serve(side, h, both):
        if h == 0:
            q_copy(side, 0, to=side).wait_recv()
            q_copy(side, 1, to=side).wait_recv()
        q_copy(side, 2 + h, to=side).wait_recv()
        if both:
            k_copy(side, 0, h, to=1 - side).wait_recv()
        for i in range(blocks):
            weigh(side, i, h, both)
        if both:
            k_copy(side, 1, h, to=1 - side).wait_recv()
        for i in range(blocks):
            answer(side, i, h, both)

    def reply(side, h):
        for i in range(blocks):
            s_copy(side, i, h).start()
        for i in reversed(range(blocks)):
            p_copy(side, i, h).start()

    def forward(h):
        send_pick(0, h)
        send_pick(1, h)

    def forward_queries(h):
        x_wait(2, h).wait_recv()
        on_sides(lambda side: q_copy(side, 2 + h).start())

    for h in range(heads):
        home(0, h)

    def chip_copy(i):
        return remote(heard.at[i], heard.at[i], cs.at[i], cr.at[i], head=0)

    def wait_lists():
        for i, d in enumerate(list_steps):

            @pl.when(exists(d) & lead)
            def _():
                list_wait(i, d).wait_recv()
                chip_copy(i).start()

            pl.when(exists(d) & ~lead)(lambda: chip_copy(i).wait_recv())

    @pl.when(early)
    def _():
        for h in range(heads):
            forward_queries(h)
            home(1, h)
        wait_lists()
        for h in range(heads):
            forward(h)

            @pl.when(inner)
            def _(h=h):
                serve(0, h, True)
                reply(0, h)

        for both, there in ((True, inner), (False, ~inner)):

            @pl.when(there)
            def _(both=both):
                for h in range(heads):
                    serve(1, h, both)
                    reply(1, h)

    @pl.when(~early)
    def _():
        for h in range(FIRST):
            forward_queries(h)
            home(1, h)
        wait_lists()
        forward(0)
        for h in range(FIRST, heads):
            home(1, h)
        for h in range(1, heads):
            forward(h)
            if h >= 2:
                pl.when(inner)(functools.partial(serve, 0, h - 2, True))

        for h in range(FIRST, heads):
            forward_queries(h)
        pl.when(inner)(functools.partial(serve, 0, heads - 2, True))

        @pl.when(inner)
        def _():
            for h in range(heads):
                if h == heads - 1:
                    serve(0, h, True)
                reply(0, h)
            for h in range(heads):
                serve(1, h, True)
                reply(1, h)

        @pl.when(~inner)
        def _():
            for h in range(heads):
                serve(0, h, False)
                reply(0, h)

    def merge(i, h, parts):
        rows = [own_l[i, h : h + 1]] + [lin[side, i, h] for side in parts]
        top = functools.reduce(jnp.maximum, rows)
        shares = [jnp.exp2(row - top) for row in rows]
        scale = 1.0 / functools.reduce(jnp.add, shares)
        value = own_o[i, h] * (shares[0] * scale)
        for side, share in zip(parts, shares[1:]):
            value = value + pin[side, i, h].astype(jnp.float32) * (share * scale)
        out[:, head_of(places[i], h)] = value.astype(jnp.bfloat16).T

    for h in range(heads):
        for i in range(blocks):
            wait_sides(s_copy, i, h)
            wait_sides(p_copy, i, h)
            pl.when(ex(0) & ex(1))(lambda: merge(i, h, (0, 1)))
            pl.when(ex(0) & ~ex(1))(lambda: merge(i, h, (0,)))
            pl.when(~ex(0) & ex(1))(lambda: merge(i, h, (1,)))
            pl.when(~ex(0) & ~ex(1))(lambda: merge(i, h, ()))

    for t in range(3):
        for h in range(heads):
            x_copy(t, h).wait_send()
    for i, d in enumerate(list_steps):

        @pl.when(exists(d) & lead)
        def _(i=i, d=d):
            list_copy(i, d).wait_send()
            chip_copy(i).wait_send()

    @on_sides
    def _(side):
        for i in range(2 + heads):
            q_copy(side, i).wait_send()
        for i in range(blocks):
            for h in range(heads):
                s_copy(side, i, h).wait_send()
                p_copy(side, i, h).wait_send()

        @pl.when(exists(2 * step(side)))
        def _():
            for t in (0, 1):
                for h in range(heads):
                    k_copy(side, t, h).wait_send()


def short(frames, blocks, queries, key_rows, value_rows, block_lists):
    rows, columns = queries.shape
    width = columns // blocks
    heads = width // DH
    lists = block_lists[0]
    dma = pltpu.SemaphoreType.DMA
    bf, f32 = jnp.bfloat16, jnp.float32
    vmem = pltpu.VMEM
    return pl.pallas_call(
        functools.partial(short_kernel, frames, blocks),
        out_shape=jax.ShapeDtypeStruct(queries.shape, queries.dtype),
        in_specs=[pl.BlockSpec(memory_space=pltpu.HBM)] * 4,
        out_specs=pl.BlockSpec(memory_space=pltpu.VMEM),
        scratch_shapes=[
            vmem((rows, columns), bf),
            vmem((rows, columns), bf),
            vmem((rows, columns), bf),
            [[vmem((blocks, BLOCK, DH), bf)] * heads] * 2,
            vmem((heads, BLOCK, DH), bf),
            vmem((2, blocks, BLOCK, width), bf),
            vmem((2, 2, BLOCK, width), bf),
            vmem((2, 2, BLOCK, width), bf),
            vmem((2, blocks, heads, 2, BLOCK, BLOCK), bf),
            vmem((2, blocks, 8, BLOCK), f32),
            vmem((2, blocks, heads, DH, BLOCK), bf),
            vmem((2, blocks, heads, 1, BLOCK), f32),
            vmem((2, blocks, heads, DH, BLOCK), bf),
            vmem((2, blocks, heads, 1, BLOCK), f32),
            vmem((blocks, heads, DH, BLOCK), f32),
            vmem((blocks, 8, BLOCK), f32),
            pltpu.SMEM((4,) + lists.shape, jnp.int32),
            dma((3 + 2 * heads,)),
            dma((3, heads)),
            dma((3, heads)),
            dma((2, 2 + heads)),
            dma((2, 2 + heads)),
            dma((2, 2, heads)),
            dma((2, 2, heads)),
            dma((2, blocks, heads)),
            dma((2, blocks, heads)),
            dma((2, blocks, heads)),
            dma((2, blocks, heads)),
            dma((4,)),
            dma((4,)),
            dma((4,)),
            dma((4,)),
            pltpu.SemaphoreType.REGULAR((2,)),
        ],
        compiler_params=pltpu.CompilerParams(
            collective_id=1, has_side_effects=True, vmem_limit_bytes=48 * 1024 * 1024
        ),
    )(*[pltpu.with_memory_space_constraint(x, pltpu.HBM) for x in (queries, key_rows, value_rows, lists)])


def solution(mesh):
    in_specs = (
        P(("groups", "tm", "space"), "head"),
        P(("groups", "tm", "space"), "head"),
        P(("groups", "tm", "space"), "head"),
        P(("groups", "tm"), None, None),
    )
    out_specs = P(("groups", "tm", "space"), "head")
    frames, blocks = mesh.shape["tm"], mesh.shape["space"]
    body = functools.partial(short if frames <= 4 and blocks == 2 else local, frames, blocks)
    return jax.shard_map(body, mesh=mesh, in_specs=in_specs, out_specs=out_specs, check_vma=False)
```

```python
import functools

import jax
import jax.numpy as jnp
from jax import lax
from jax.experimental import pallas as pl
from jax.experimental.pallas import tpu as pltpu
from jax.sharding import PartitionSpec as P

DH = 128
BLOCK = 128
MESH = pl.DeviceIdType.MESH
LOG2E = 1.4426950408889634
FIRST = 1


def group_table(blocks):
    near, middle, far = max(blocks // 2, 1), max(blocks // 4, 1), max(blocks // 8, 1)
    table = {0: (0, near, blocks)}
    start = near
    for step, count, union in (
        (1, near, blocks),
        (2, middle, max(blocks // 2, 1)),
        (4, far, max(blocks // 4, 1)),
    ):
        table[-step] = (start, count, union)
        table[step] = (start + count, count, union)
        start += 2 * count
    return table


def kernel(
    frames, blocks, q, k, v, lists_v, out,
    lists_s, qb, own, near, pick2, mid, pick2v, midv, pick4, far, heard, ob, peak, total, numer, held, stage, stage_sem,
    loc_sem, xs, xr, zs, zr, ms, mr, fs, fr, ls, lr, os_, or_,
):
    f = lax.axis_index("tm")
    s = lax.axis_index("space")
    width = qb.shape[2]
    heads = width // DH
    table = group_table(blocks)
    use_far = frames > 4
    scale = DH ** -0.5

    def cols(i):
        return pl.ds(pl.multiple_of(i * width, width), width)

    def at(step):
        return {"tm": f + step}

    def exists(step):
        return (f + step >= 0) & (f + step < frames)

    steps = (-1, 1) + ((-4, 4) if use_far else ())

    local = [
        pltpu.make_async_copy(q.at[:, cols(s)], qb.at[s], loc_sem.at[0]),
        pltpu.make_async_copy(k.at[:, cols(s)], own.at[0, s], loc_sem.at[1]),
        pltpu.make_async_copy(v.at[:, cols(s)], own.at[1, s], loc_sem.at[2]),
        pltpu.make_async_copy(lists_v, lists_s, loc_sem.at[3]),
    ]
    for t in range(3):
        for o in range(1, blocks):
            local.append(pltpu.make_async_copy(
                (k, v, q)[t].at[:, cols(lax.rem(s + o, blocks))], stage.at[t, o], stage_sem.at[t, o]
            ))
    for copy in local:
        copy.start()

    barrier = pltpu.get_barrier_semaphore()
    for o in range(1, blocks):
        pl.semaphore_signal(
            barrier, inc=1, device_id={"space": lax.rem(s + o, blocks)}, device_id_type=MESH
        )
    greeted = blocks - 1
    for step in steps:

        @pl.when(exists(step))
        def _(step=step):
            pl.semaphore_signal(barrier, inc=1, device_id=at(step), device_id_type=MESH)

        greeted = greeted + exists(step).astype(jnp.int32)
    for copy in local:
        copy.wait()
    pl.semaphore_wait(barrier, greeted)

    def list_copy(i, step):
        return pltpu.make_async_remote_copy(
            src_ref=lists_v, dst_ref=heard.at[i ^ 1], send_sem=ls.at[i], recv_sem=lr.at[i ^ 1],
            device_id=at(step), device_id_type=MESH,
        )

    def list_wait(i):
        return pltpu.make_async_remote_copy(
            src_ref=lists_v, dst_ref=heard.at[i], send_sem=ls.at[i], recv_sem=lr.at[i],
            device_id=at(steps[i]), device_id_type=MESH,
        )

    def x_copy(t, o):
        to = lax.rem(s + o, blocks)
        src = stage.at[t, o]
        dst = qb.at[s] if t == 2 else own.at[t, s]
        return pltpu.make_async_remote_copy(
            src_ref=src, dst_ref=dst, send_sem=xs.at[t, o], recv_sem=xr.at[t, o],
            device_id={"space": to}, device_id_type=MESH,
        )

    def z_copy(side, t, o):
        b = lax.rem(s - o + blocks, blocks)
        src = own.at[t, b]
        return pltpu.make_async_remote_copy(
            src_ref=src, dst_ref=near.at[side, t, b], send_sem=zs.at[side, t, o],
            recv_sem=zr.at[side, t, o], device_id=at(1 - 2 * side), device_id_type=MESH,
        )

    def m_copy(side, h):
        src, dst = (pick2.at[side], mid.at[side]) if h < 0 else (pick2v.at[side, h], midv.at[side, h])
        return pltpu.make_async_remote_copy(
            src_ref=src, dst_ref=dst, send_sem=ms.at[side, h + 1],
            recv_sem=mr.at[side, h + 1], device_id=at(1 - 2 * side), device_id_type=MESH,
        )

    def f_copy(side, t):
        return pltpu.make_async_remote_copy(
            src_ref=pick4.at[side, t], dst_ref=far.at[side, t], send_sem=fs.at[side, t],
            recv_sem=fr.at[side, t], device_id=at(4 - 8 * side), device_id_type=MESH,
        )

    def ahead(side):
        return exists(1 - 2 * side)

    def behind(side):
        return exists(2 * side - 1)

    for t in (0, 1):
        for o in range(1, blocks):
            x_copy(t, o).start()
        for side in (0, 1):

            @pl.when(ahead(side))
            def _(side=side, t=t):
                z_copy(side, t, 0).start()

    for i, step in enumerate(steps):

        @pl.when(exists(step))
        def _(i=i, step=step):
            list_copy(i, step).start()

    for t in (0, 1):
        for o in range(1, blocks):
            x_copy(t, o).wait_recv()
            for side in (0, 1):

                @pl.when(ahead(side))
                def _(side=side, t=t, o=o):
                    z_copy(side, t, o).start()

    for o in range(1, blocks):
        x_copy(2, o).start()

    def choose(i, distance, load, store):
        first, count, union = table[distance]
        seen, rank = [], []
        before = jnp.zeros((1, 1), jnp.int32)
        for c in range(blocks):
            hit = jnp.zeros((1, 1), jnp.int32)
            for b in range(blocks):
                for j in range(first, first + count):
                    hit = jnp.maximum(hit, (heard[i, b : b + 1, j : j + 1] == c).astype(jnp.int32))
            seen.append(hit)
            rank.append(before)
            before = before + hit
        for u in range(union):
            value = load(blocks - 1).astype(jnp.float32)
            for c in range(blocks - 1):
                mask = jnp.where(rank[c] == u, seen[c], 0)
                mask = jnp.broadcast_to(mask, value.shape)
                value = jnp.where(mask == 1, load(c).astype(jnp.float32), value)
            store(u, value.astype(jnp.bfloat16))

    def place(b, slot, distance):
        first, count, union = table[distance]
        number = lists_s[b, slot]
        if union == blocks:
            return number
        if union == 1:
            return 0
        position = jnp.int32(0)
        for c in range(blocks - 1):
            seen = jnp.int32(0)
            for other in range(blocks):
                for j in range(first, first + count):
                    seen = jnp.maximum(seen, (lists_s[other, j] == c).astype(jnp.int32))
            position = position + jnp.where(c < number, seen, 0)
        return position

    def attend(distance, keys, values, fresh=False):
        first, count, union = table[distance]
        for b in range(blocks):
            for j in range(count):
                n = place(b, first + j, distance)
                for h in range(heads):
                    cut = slice(h * DH, (h + 1) * DH)
                    scores = lax.dot_general(
                        qb[b, :, cut], keys(n, cut), (((1,), (1,)), ((), ())),
                        preferred_element_type=jnp.float32,
                    ) * scale
                    top = jnp.max(scores, axis=1, keepdims=True)
                    if fresh and j == 0:
                        weights = jnp.exp(scores - top)
                        peak[b, h] = jnp.broadcast_to(top, (BLOCK, DH))
                        total[b, h] = jnp.broadcast_to(
                            jnp.sum(weights, axis=1, keepdims=True), (BLOCK, DH)
                        )
                        numer[b, h] = jnp.dot(
                            weights.astype(jnp.bfloat16), values(n, cut),
                            preferred_element_type=jnp.float32,
                        )
                    else:
                        old = peak[b, h]
                        new = jnp.maximum(old, jnp.broadcast_to(top, (BLOCK, DH)))
                        fade = jnp.exp(old - new)
                        weights = jnp.exp(scores - new)
                        peak[b, h] = new
                        total[b, h] = total[b, h] * fade + jnp.broadcast_to(
                            jnp.sum(weights, axis=1, keepdims=True), (BLOCK, DH)
                        )
                        numer[b, h] = numer[b, h] * fade + jnp.dot(
                            weights.astype(jnp.bfloat16), values(n, cut),
                            preferred_element_type=jnp.float32,
                        )

    if use_far:
        for side in (0, 1):

            @pl.when(exists(4 - 8 * side))
            def _(side=side):
                i = 3 - side
                list_wait(i).wait_recv()
                for t in (0, 1):
                    choose(
                        i, -4 if side == 0 else 4,
                        lambda c: own[t, c],
                        lambda u, x: pick4.__setitem__((side, t, u), x),
                    )
                    f_copy(side, t).start()

    for i in (0, 1):

        @pl.when(exists(steps[i]))
        def _(i=i):
            list_wait(i).wait_recv()

    for side in (0, 1):

        @pl.when(behind(side))
        def _(side=side):
            for o in range(blocks):
                z_copy(side, 0, o).wait_recv()

        @pl.when(behind(side) & ahead(side))
        def _(side=side):
            choose(
                1 - side, -2 if side == 0 else 2,
                lambda c: near[side, 0, c],
                lambda u, x: pick2.__setitem__((side, u), x),
            )
            m_copy(side, -1).start()

    for o in range(1, blocks):
        x_copy(2, o).wait_recv()
    attend(0, lambda n, cut: own[0, n, :, cut], lambda n, cut: own[1, n, :, cut], fresh=True)

    for side in (0, 1):

        @pl.when(behind(side))
        def _(side=side):
            for o in range(blocks):
                z_copy(side, 1, o).wait_recv()

        @pl.when(behind(side) & ahead(side))
        def _(side=side):
            for h in range(heads):
                choose(
                    1 - side, -2 if side == 0 else 2,
                    lambda c: near[side, 1, c, :, h * DH : (h + 1) * DH],
                    lambda u, x: pick2v.__setitem__((side, h, u), x),
                )
                m_copy(side, h).start()

    for side in (0, 1):

        @pl.when(behind(side))
        def _(side=side):
            attend(
                -1 if side == 0 else 1,
                lambda n, cut: near[side, 0, n, :, cut], lambda n, cut: near[side, 1, n, :, cut],
            )

    if use_far:
        for side in (0, 1):

            @pl.when(exists(8 * side - 4))
            def _(side=side):
                for t in (0, 1):
                    f_copy(side, t).wait_recv()
                attend(
                    -4 if side == 0 else 4,
                    lambda n, cut: far[side, 0, n, :, cut], lambda n, cut: far[side, 1, n, :, cut],
                )

    for side in (0, 1):

        @pl.when(exists(4 * side - 2))
        def _(side=side):
            m_copy(side, -1).wait_recv()

    def mid_scores(b, h, side, j):
        distance = -2 if side == 0 else 2
        cut = slice(h * DH, (h + 1) * DH)
        n = place(b, table[distance][0] + j, distance)
        return lax.dot_general(
            qb[b, :, cut], mid[side, n, :, cut], (((1,), (1,)), ((), ())),
            preferred_element_type=jnp.float32,
        ) * scale

    def mid_weights(sides):
        slots = [(side, j) for side in sides for j in range(table[2][1])]
        for b in range(blocks):
            for h in range(heads):
                scores = [mid_scores(b, h, side, j) for side, j in slots]
                old = peak[b, h]
                new = old
                for x in scores:
                    top = jnp.max(x, axis=1, keepdims=True)
                    new = jnp.maximum(new, jnp.broadcast_to(top, (BLOCK, DH)))
                fade = jnp.exp(old - new)
                whole = total[b, h] * fade
                for (side, j), x in zip(slots, scores):
                    weights = jnp.exp(x - new)
                    whole = whole + jnp.broadcast_to(
                        jnp.sum(weights, axis=1, keepdims=True), (BLOCK, DH)
                    )
                    held[side, j, b, h] = weights.astype(jnp.bfloat16)
                total[b, h] = 1.0 / whole
                numer[b, h] = numer[b, h] * fade

    def o_copy(o, h):
        to = lax.rem(s + o, blocks)
        return pltpu.make_async_remote_copy(
            src_ref=ob.at[to, h], dst_ref=out.at[:, head_cols(s, h)],
            send_sem=os_.at[o, h], recv_sem=or_.at[o, h],
            device_id={"space": to}, device_id_type=MESH,
        )

    def head_cols(i, h):
        return pl.ds(pl.multiple_of(i * width + h * DH, DH), DH)

    def keep(h):
        return pltpu.make_async_copy(ob.at[s, h], out.at[:, head_cols(s, h)], os_.at[0, h])

    def finish(sides):
        for h in range(heads):
            for side in sides:
                m_copy(side, h).wait_recv()
            for o in list(range(1, blocks)) + [0]:
                b = lax.rem(s + o, blocks)
                value = numer[b, h]
                for side in sides:
                    distance = -2 if side == 0 else 2
                    for j in range(table[2][1]):
                        n = place(b, table[distance][0] + j, distance)
                        value = value + jnp.dot(
                            held[side, j, b, h], midv[side, h, n],
                            preferred_element_type=jnp.float32,
                        )
                ob[b, h] = (value * total[b, h]).astype(jnp.bfloat16)
                if o:
                    o_copy(o, h).start()
                else:
                    keep(h).start()

    def last(sides):
        mid_weights(sides)
        finish(sides)

    pl.when(exists(-2) & exists(2))(lambda: last((0, 1)))
    pl.when(exists(-2) & ~exists(2))(lambda: last((0,)))
    pl.when(~exists(-2) & exists(2))(lambda: last((1,)))
    pl.when(~exists(-2) & ~exists(2))(lambda: last(()))

    for t in (0, 1, 2):
        for o in range(1, blocks):
            x_copy(t, o).wait_send()
    for i, step in enumerate(steps):

        @pl.when(exists(step))
        def _(i=i, step=step):
            list_copy(i, step).wait_send()

    for side in (0, 1):

        @pl.when(ahead(side))
        def _(side=side):
            for t in (0, 1):
                for o in range(blocks):
                    z_copy(side, t, o).wait_send()

        @pl.when(behind(side) & ahead(side))
        def _(side=side):
            for h in range(-1, heads):
                m_copy(side, h).wait_send()

        if use_far:

            @pl.when(exists(4 - 8 * side))
            def _(side=side):
                for t in (0, 1):
                    f_copy(side, t).wait_send()

    for h in range(heads):
        keep(h).wait()
        for o in range(1, blocks):
            o_copy(o, h).wait_send()
            pltpu.make_async_remote_copy(
                src_ref=ob.at[s, h], dst_ref=out.at[:, head_cols(lax.rem(s - o + blocks, blocks), h)],
                send_sem=os_.at[o, h], recv_sem=or_.at[o, h],
                device_id={"space": lax.rem(s + o, blocks)}, device_id_type=MESH,
            ).wait_recv()


def local(frames, blocks, queries, key_rows, value_rows, block_lists):
    rows, columns = queries.shape
    width = columns // blocks
    heads = width // DH
    lists = block_lists[0]
    table = group_table(blocks)
    u2, u4 = table[2][2], table[4][2]
    far_rows = BLOCK if frames > 4 else 16
    dma = pltpu.SemaphoreType.DMA
    bf = jnp.bfloat16
    return pl.pallas_call(
        functools.partial(kernel, frames, blocks),
        out_shape=jax.ShapeDtypeStruct(queries.shape, queries.dtype),
        in_specs=[pl.BlockSpec(memory_space=pltpu.HBM)] * 4,
        out_specs=pl.BlockSpec(memory_space=pl.ANY),
        scratch_shapes=[
            pltpu.SMEM(lists.shape, jnp.int32),
            pltpu.VMEM((blocks, BLOCK, width), bf),
            pltpu.VMEM((2, blocks, BLOCK, width), bf),
            pltpu.VMEM((2, 2, blocks, BLOCK, width), bf),
            pltpu.VMEM((2, u2, BLOCK, width), bf),
            pltpu.VMEM((2, u2, BLOCK, width), bf),
            pltpu.VMEM((2, heads, u2, BLOCK, DH), bf),
            pltpu.VMEM((2, heads, u2, BLOCK, DH), bf),
            pltpu.VMEM((2, 2, u4, far_rows, width), bf),
            pltpu.VMEM((2, 2, u4, far_rows, width), bf),
            pltpu.VMEM((4,) + lists.shape, jnp.int32),
            pltpu.VMEM((blocks, heads, BLOCK, DH), bf),
            pltpu.VMEM((blocks, heads, BLOCK, DH), jnp.float32),
            pltpu.VMEM((blocks, heads, BLOCK, DH), jnp.float32),
            pltpu.VMEM((blocks, heads, BLOCK, DH), jnp.float32),
            pltpu.VMEM((2, table[2][1], blocks, heads, BLOCK, DH), bf),
            pltpu.VMEM((3, blocks, BLOCK, width), bf),
            dma((3, blocks)),
            dma((5,)),
            dma((3, blocks)),
            dma((3, blocks)),
            dma((2, 2, blocks)),
            dma((2, 2, blocks)),
            dma((2, 1 + heads)),
            dma((2, 1 + heads)),
            dma((2, 2)),
            dma((2, 2)),
            dma((4,)),
            dma((4,)),
            dma((blocks, heads)),
            dma((blocks, heads)),
        ],
        compiler_params=pltpu.CompilerParams(
            collective_id=0, has_side_effects=True, vmem_limit_bytes=48 * 1024 * 1024
        ),
    )(*[pltpu.with_memory_space_constraint(x, pltpu.HBM) for x in (queries, key_rows, value_rows, lists)])


def short_kernel(
    frames, blocks, q, k, v, lists_v, out,
    qh, kh, vh, kv, xq, qn, mid, pick, held, rt, po, ps, pin, lin, own_o, own_l, heard,
    loc_sem, xs, xr, qs, qr, ks, kr, ps_, pr, ss, sr, ls, lr, cs, cr, ready,
):
    f = lax.axis_index("tm")
    s = lax.axis_index("space")
    other = 1 - s
    width = qn.shape[3]
    heads = width // DH
    table = group_table(blocks)
    factor = DH ** -0.5 * LOG2E
    sides = (0, 1)
    early = f < frames // 2
    core = lax.axis_index("head")
    lead = core == 1

    def exists(step):
        return (f + step >= 0) & (f + step < frames)

    def step(side):
        return 2 * side - 1

    def ex(side):
        return exists(step(side))

    def half(i):
        return pl.ds(pl.multiple_of(i * width, width), width)

    def head_of(i, h):
        return pl.ds(pl.multiple_of(i * width + h * DH, DH), DH)

    def cut(h):
        return slice(h * DH, (h + 1) * DH)

    def remote(src, dst, send, recv, **where):
        return pltpu.make_async_remote_copy(
            src_ref=src, dst_ref=dst, send_sem=send, recv_sem=recv,
            device_id=where, device_id_type=MESH,
        )

    local = [
        pltpu.make_async_copy(q, qh, loc_sem.at[0]),
        pltpu.make_async_copy(k, kh, loc_sem.at[1]),
        pltpu.make_async_copy(v, vh, loc_sem.at[2]),
    ]
    for t in (0, 1):
        for h in range(heads):
            local.append(pltpu.make_async_copy(
                (k, v)[t].at[:, head_of(s, h)], kv[t][h].at[s], loc_sem.at[3 + t * heads + h]
            ))
    for copy in local:
        copy.start()

    def late(frame):
        return frame >= frames // 2

    def greet(semaphore, d):
        pl.semaphore_signal(semaphore, inc=1, device_id={"tm": f + d}, device_id_type=MESH)

    barrier = pltpu.get_barrier_semaphore()
    pl.semaphore_signal(barrier, inc=1, device_id={"space": other}, device_id_type=MESH)
    pl.when(exists(2) & lead)(lambda: greet(barrier, 2))

    @pl.when(~lead)
    def _():
        pl.semaphore_signal(barrier, inc=1, device_id={"head": 1}, device_id_type=MESH)

    pl.when(exists(1))(lambda: greet(barrier, 1))
    pl.when(exists(-1) & ~late(f))(lambda: greet(barrier, -1))
    greeted = 1 + exists(-1).astype(jnp.int32)
    greeted = greeted + (exists(-2) & lead).astype(jnp.int32) + lead.astype(jnp.int32)
    pl.semaphore_wait(barrier, greeted + (exists(1) & ~late(f + 1)).astype(jnp.int32))
    pl.when(exists(-1) & late(f))(lambda: greet(ready.at[0], -1))
    pl.when(exists(-2) & lead)(lambda: greet(ready.at[1], -2))

    def list_copy(i, d):
        return remote(lists_v, heard.at[i ^ 1], ls.at[i], lr.at[i ^ 1], tm=f + d)

    def list_wait(i, d):
        return remote(lists_v, heard.at[i], ls.at[i], lr.at[i], tm=f + d)

    list_steps = (-1, 1, -2, 2)

    places = (s, other)

    def x_copy(t, h):
        src = (k, v, q)[t].at[:, head_of(other, h)]
        dst = xq.at[h] if t == 2 else kv[t][h].at[s]
        return remote(src, dst, xs.at[t, h], xr.at[t, h], space=other)

    def x_wait(t, h):
        src = (k, v, q)[t].at[:, head_of(other, h)]
        dst = xq.at[h] if t == 2 else kv[t][h].at[other]
        return remote(src, dst, xs.at[t, h], xr.at[t, h], space=other)

    def q_copy(side, i, to=None):
        to = 1 - side if to is None else to
        if i < 2:
            part = width // 2
            src = q.at[:, pl.ds(pl.multiple_of(s * width + i * part, DH), part)]
            dst = qn.at[to, 0, :, slice(i * part, (i + 1) * part)]
        else:
            src, dst = xq.at[i - 2], qn.at[to, 1, :, cut(i - 2)]
        return remote(src, dst, qs.at[side, i], qr.at[to, i], tm=f + step(side))

    def k_copy(side, t, h, to=None):
        to = 1 - side if to is None else to
        return remote(
            pick.at[side, t, :, cut(h)], mid.at[to, t, :, cut(h)], ks.at[side, t, h],
            kr.at[to, t, h], tm=f + step(side),
        )

    def p_copy(side, i, h, to=None):
        to = 1 - side if to is None else to
        return remote(
            po.at[side, i, h], pin.at[to, i, h], ps_.at[side, i, h], pr.at[to, i, h],
            tm=f + step(side), space=places[i],
        )

    def s_copy(side, i, h, to=None):
        to = 1 - side if to is None else to
        return remote(
            ps.at[side, i, pl.ds(h - 1, 2)], lin.at[to, i, pl.ds(h - 1, 2)],
            ss.at[side, i, h], sr.at[to, i, h],
            tm=f + step(side), space=places[i],
        )

    def on_sides(run, there=ex):
        for side in sides:
            pl.when(there(side))(functools.partial(run, side))

    def wait_sides(copy, *key, there=ex):
        on_sides(lambda side: copy(side, *key, to=side).wait_recv(), there)

    @pl.when(exists(-1))
    def _():
        pl.when(lead)(lambda: list_copy(0, -1).start())
        q_copy(0, 0).start()
        q_copy(0, 1).start()

    pl.when(exists(-2) & lead)(lambda: list_copy(2, -2).start())

    def start_queries(span):
        for h in span:
            x_copy(2, h).start()

    start_queries(range(FIRST))
    pl.when(early)(lambda: start_queries(range(FIRST, heads)))
    for h in range(heads):
        for t in (0, 1):
            x_copy(t, h).start()
    pl.when(~early)(lambda: start_queries(range(FIRST, heads)))

    @pl.when(exists(1))
    def _():
        pl.when(late(f + 1))(lambda: pl.semaphore_wait(ready.at[0], 1))
        pl.when(lead)(lambda: list_copy(1, 1).start())
        q_copy(1, 0).start()

        @pl.when(exists(2) & lead)
        def _():
            pl.semaphore_wait(ready.at[1], 1)
            list_copy(3, 2).start()

        q_copy(1, 1).start()

    for copy in local:
        copy.wait()

    def scores(keys, queries):
        return lax.dot_general(
            keys, queries, (((1,), (1,)), ((), ())), preferred_element_type=jnp.float32
        ) * factor

    def gathered(values, weights):
        return lax.dot_general(
            values, weights, (((0,), (0,)), ((), ())), preferred_element_type=jnp.float32
        )

    def home(i, h):
        columns = head_of(places[i], h)
        x = scores(kh[:, columns], qh[:, columns])
        top = jnp.max(x, axis=0, keepdims=True)
        weights = jnp.exp2(x - top)
        whole = jnp.sum(weights, axis=0, keepdims=True)
        own_o[i, h] = gathered(vh[:, columns], weights.astype(jnp.bfloat16)) * (1.0 / whole)
        own_l[i, h : h + 1] = top + jnp.log2(whole)

    def send_pick(t, h):
        x_wait(t, h).wait_recv()

        def run(side):
            n = heard[2 + side, 0, table[-2 * step(side)][0]]
            pick[side, t, :, cut(h)] = kv[t][h][n]
            k_copy(side, t, h).start()

        on_sides(run, lambda side: exists(2 * step(side)))

    def near_block(side, i):
        return heard[side, places[i], table[-step(side)][0]]

    def weigh(side, i, h, both):
        queries = qn[side, i, :, cut(h)]
        x = [scores(kv[0][h][near_block(side, i)], queries)]
        if both:
            x.append(scores(mid[1 - side, 0, :, cut(h)], queries))
        top = functools.reduce(jnp.maximum, [jnp.max(y, axis=0, keepdims=True) for y in x])
        whole = jnp.zeros_like(top)
        for j, y in enumerate(x):
            weights = jnp.exp2(y - top)
            whole = whole + jnp.sum(weights, axis=0, keepdims=True)
            held[side, i, h, j] = weights.astype(jnp.bfloat16)
        rt[side, i, h : h + 1] = 1.0 / whole
        ps[side, i, h] = top + jnp.log2(whole)

    def answer(side, i, h, both):
        value = gathered(kv[1][h][near_block(side, i)], held[side, i, h, 0])
        if both:
            value = value + gathered(mid[1 - side, 1, :, cut(h)], held[side, i, h, 1])
        po[side, i, h] = (value * rt[side, i, h : h + 1]).astype(jnp.bfloat16)

    inner = ex(0) & ex(1)

    def between(side):
        return inner

    def serve(side, h, both):
        if h == 0:
            q_copy(side, 0, to=side).wait_recv()
            q_copy(side, 1, to=side).wait_recv()
        q_copy(side, 2 + h, to=side).wait_recv()
        if both:
            k_copy(side, 0, h, to=1 - side).wait_recv()
        for i in range(blocks):
            weigh(side, i, h, both)
        if both:
            k_copy(side, 1, h, to=1 - side).wait_recv()
        for i in range(blocks):
            answer(side, i, h, both)

    def reply(side, h):
        if h % 2:
            for i in range(blocks):
                s_copy(side, i, h).start()
        for i in reversed(range(blocks)):
            p_copy(side, i, h).start()

    def forward(h):
        send_pick(0, h)
        send_pick(1, h)

    def forward_queries(h):
        x_wait(2, h).wait_recv()
        on_sides(lambda side: q_copy(side, 2 + h).start())

    for h in range(heads):
        home(0, h)

    def chip_copy(i):
        return remote(heard.at[i], heard.at[i], cs.at[i], cr.at[i], head=0)

    def wait_lists():
        for i, d in enumerate(list_steps):

            @pl.when(exists(d) & lead)
            def _():
                list_wait(i, d).wait_recv()
                chip_copy(i).start()

            pl.when(exists(d) & ~lead)(lambda: chip_copy(i).wait_recv())

    def answer_below(h):
        serve(0, h, True)
        reply(0, h)

    @pl.when(early)
    def _():
        for h in range(heads):
            forward_queries(h)
            home(1, h)
        wait_lists()
        for h in range(heads):
            forward(h)
            if h >= 1:
                pl.when(inner)(functools.partial(answer_below, h - 1))
        for h in range(heads - 1, heads):
            pl.when(inner)(functools.partial(answer_below, h))

        for both, there in ((True, inner), (False, ~inner)):

            @pl.when(there)
            def _(both=both):
                for h in range(heads):
                    serve(1, h, both)
                    reply(1, h)

    @pl.when(~early)
    def _():
        for h in range(FIRST):
            forward_queries(h)
            home(1, h)
        wait_lists()
        forward(0)
        for h in range(FIRST, heads):
            home(1, h)
        for h in range(1, heads):
            forward(h)
            if h >= 2:
                pl.when(inner)(functools.partial(serve, 0, h - 2, True))

        for h in range(FIRST, heads):
            forward_queries(h)
        pl.when(inner)(functools.partial(serve, 0, heads - 2, True))

        @pl.when(inner)
        def _():
            for h in range(heads):
                if h == heads - 1:
                    serve(0, h, True)
                reply(0, h)
            for h in range(heads):
                serve(1, h, True)
                reply(1, h)

        @pl.when(~inner)
        def _():
            for h in range(heads):
                serve(0, h, False)
                reply(0, h)

    def merge(i, h, parts):
        rows = [own_l[i, h : h + 1]] + [lin[side, i, h] for side in parts]
        top = functools.reduce(jnp.maximum, rows)
        shares = [jnp.exp2(row - top) for row in rows]
        scale = 1.0 / functools.reduce(jnp.add, shares)
        value = own_o[i, h] * (shares[0] * scale)
        for side, share in zip(parts, shares[1:]):
            value = value + pin[side, i, h].astype(jnp.float32) * (share * scale)
        out[:, head_of(places[i], h)] = value.astype(jnp.bfloat16).T

    for h in range(heads):
        for i in range(blocks):
            if h % 2 == 0:
                wait_sides(s_copy, i, h + 1)
            wait_sides(p_copy, i, h)
            pl.when(ex(0) & ex(1))(lambda: merge(i, h, (0, 1)))
            pl.when(ex(0) & ~ex(1))(lambda: merge(i, h, (0,)))
            pl.when(~ex(0) & ex(1))(lambda: merge(i, h, (1,)))
            pl.when(~ex(0) & ~ex(1))(lambda: merge(i, h, ()))

    for t in range(3):
        for h in range(heads):
            x_copy(t, h).wait_send()
    for i, d in enumerate(list_steps):

        @pl.when(exists(d) & lead)
        def _(i=i, d=d):
            list_copy(i, d).wait_send()
            chip_copy(i).wait_send()

    @on_sides
    def _(side):
        for i in range(2 + heads):
            q_copy(side, i).wait_send()
        for i in range(blocks):
            for h in range(heads):
                if h % 2:
                    s_copy(side, i, h).wait_send()
                p_copy(side, i, h).wait_send()

        @pl.when(exists(2 * step(side)))
        def _():
            for t in (0, 1):
                for h in range(heads):
                    k_copy(side, t, h).wait_send()


def short(frames, blocks, queries, key_rows, value_rows, block_lists):
    rows, columns = queries.shape
    width = columns // blocks
    heads = width // DH
    lists = block_lists[0]
    dma = pltpu.SemaphoreType.DMA
    bf, f32 = jnp.bfloat16, jnp.float32
    vmem = pltpu.VMEM
    return pl.pallas_call(
        functools.partial(short_kernel, frames, blocks),
        out_shape=jax.ShapeDtypeStruct(queries.shape, queries.dtype),
        in_specs=[pl.BlockSpec(memory_space=pltpu.HBM)] * 4,
        out_specs=pl.BlockSpec(memory_space=pltpu.VMEM),
        scratch_shapes=[
            vmem((rows, columns), bf),
            vmem((rows, columns), bf),
            vmem((rows, columns), bf),
            [[vmem((blocks, BLOCK, DH), bf)] * heads] * 2,
            vmem((heads, BLOCK, DH), bf),
            vmem((2, blocks, BLOCK, width), bf),
            vmem((2, 2, BLOCK, width), bf),
            vmem((2, 2, BLOCK, width), bf),
            vmem((2, blocks, heads, 2, BLOCK, BLOCK), bf),
            vmem((2, blocks, 8, BLOCK), f32),
            vmem((2, blocks, heads, DH, BLOCK), bf),
            vmem((2, blocks, heads, 1, BLOCK), f32),
            vmem((2, blocks, heads, DH, BLOCK), bf),
            vmem((2, blocks, heads, 1, BLOCK), f32),
            vmem((blocks, heads, DH, BLOCK), f32),
            vmem((blocks, 8, BLOCK), f32),
            pltpu.SMEM((4,) + lists.shape, jnp.int32),
            dma((3 + 2 * heads,)),
            dma((3, heads)),
            dma((3, heads)),
            dma((2, 2 + heads)),
            dma((2, 2 + heads)),
            dma((2, 2, heads)),
            dma((2, 2, heads)),
            dma((2, blocks, heads)),
            dma((2, blocks, heads)),
            dma((2, blocks, heads)),
            dma((2, blocks, heads)),
            dma((4,)),
            dma((4,)),
            dma((4,)),
            dma((4,)),
            pltpu.SemaphoreType.REGULAR((2,)),
        ],
        compiler_params=pltpu.CompilerParams(
            collective_id=1, has_side_effects=True, vmem_limit_bytes=48 * 1024 * 1024
        ),
    )(*[pltpu.with_memory_space_constraint(x, pltpu.HBM) for x in (queries, key_rows, value_rows, lists)])


def solution(mesh):
    in_specs = (
        P(("groups", "tm", "space"), "head"),
        P(("groups", "tm", "space"), "head"),
        P(("groups", "tm", "space"), "head"),
        P(("groups", "tm"), None, None),
    )
    out_specs = P(("groups", "tm", "space"), "head")
    frames, blocks = mesh.shape["tm"], mesh.shape["space"]
    body = functools.partial(short if frames <= 4 and blocks == 2 else local, frames, blocks)
    return jax.shard_map(body, mesh=mesh, in_specs=in_specs, out_specs=out_specs, check_vma=False)
```

```python
import functools

import jax
import jax.numpy as jnp
from jax import lax
from jax.experimental import pallas as pl
from jax.experimental.pallas import tpu as pltpu
from jax.sharding import PartitionSpec as P

DH = 128
BLOCK = 128
MESH = pl.DeviceIdType.MESH
LOG2E = 1.4426950408889634
FIRST = 1


def group_table(blocks):
    near, middle, far = max(blocks // 2, 1), max(blocks // 4, 1), max(blocks // 8, 1)
    table = {0: (0, near, blocks)}
    start = near
    for step, count, union in (
        (1, near, blocks),
        (2, middle, max(blocks // 2, 1)),
        (4, far, max(blocks // 4, 1)),
    ):
        table[-step] = (start, count, union)
        table[step] = (start + count, count, union)
        start += 2 * count
    return table


def kernel(
    frames, blocks, q, k, v, lists_v, out,
    lists_s, qb, own, near, pick2, mid, pick2v, midv, pick4, far, heard, ob, peak, total, numer, held, stage, stage_sem,
    loc_sem, xs, xr, zs, zr, ms, mr, fs, fr, ls, lr, os_, or_,
):
    f = lax.axis_index("tm")
    s = lax.axis_index("space")
    width = qb.shape[2]
    heads = width // DH
    table = group_table(blocks)
    use_far = frames > 4
    scale = DH ** -0.5

    def cols(i):
        return pl.ds(pl.multiple_of(i * width, width), width)

    def at(step):
        return {"tm": f + step}

    def exists(step):
        return (f + step >= 0) & (f + step < frames)

    steps = (-1, 1) + ((-4, 4) if use_far else ())

    local = [
        pltpu.make_async_copy(q.at[:, cols(s)], qb.at[s], loc_sem.at[0]),
        pltpu.make_async_copy(k.at[:, cols(s)], own.at[0, s], loc_sem.at[1]),
        pltpu.make_async_copy(v.at[:, cols(s)], own.at[1, s], loc_sem.at[2]),
        pltpu.make_async_copy(lists_v, lists_s, loc_sem.at[3]),
    ]
    for t in range(3):
        for o in range(1, blocks):
            local.append(pltpu.make_async_copy(
                (k, v, q)[t].at[:, cols(lax.rem(s + o, blocks))], stage.at[t, o], stage_sem.at[t, o]
            ))
    for copy in local:
        copy.start()

    barrier = pltpu.get_barrier_semaphore()
    for o in range(1, blocks):
        pl.semaphore_signal(
            barrier, inc=1, device_id={"space": lax.rem(s + o, blocks)}, device_id_type=MESH
        )
    greeted = blocks - 1
    for step in steps:

        @pl.when(exists(step))
        def _(step=step):
            pl.semaphore_signal(barrier, inc=1, device_id=at(step), device_id_type=MESH)

        greeted = greeted + exists(step).astype(jnp.int32)
    for copy in local:
        copy.wait()
    pl.semaphore_wait(barrier, greeted)

    def list_copy(i, step):
        return pltpu.make_async_remote_copy(
            src_ref=lists_v, dst_ref=heard.at[i ^ 1], send_sem=ls.at[i], recv_sem=lr.at[i ^ 1],
            device_id=at(step), device_id_type=MESH,
        )

    def list_wait(i):
        return pltpu.make_async_remote_copy(
            src_ref=lists_v, dst_ref=heard.at[i], send_sem=ls.at[i], recv_sem=lr.at[i],
            device_id=at(steps[i]), device_id_type=MESH,
        )

    def x_copy(t, o):
        to = lax.rem(s + o, blocks)
        src = stage.at[t, o]
        dst = qb.at[s] if t == 2 else own.at[t, s]
        return pltpu.make_async_remote_copy(
            src_ref=src, dst_ref=dst, send_sem=xs.at[t, o], recv_sem=xr.at[t, o],
            device_id={"space": to}, device_id_type=MESH,
        )

    def z_copy(side, t, o):
        b = lax.rem(s - o + blocks, blocks)
        src = own.at[t, b]
        return pltpu.make_async_remote_copy(
            src_ref=src, dst_ref=near.at[side, t, b], send_sem=zs.at[side, t, o],
            recv_sem=zr.at[side, t, o], device_id=at(1 - 2 * side), device_id_type=MESH,
        )

    def m_copy(side, h):
        src, dst = (pick2.at[side], mid.at[side]) if h < 0 else (pick2v.at[side, h], midv.at[side, h])
        return pltpu.make_async_remote_copy(
            src_ref=src, dst_ref=dst, send_sem=ms.at[side, h + 1],
            recv_sem=mr.at[side, h + 1], device_id=at(1 - 2 * side), device_id_type=MESH,
        )

    def f_copy(side, t):
        return pltpu.make_async_remote_copy(
            src_ref=pick4.at[side, t], dst_ref=far.at[side, t], send_sem=fs.at[side, t],
            recv_sem=fr.at[side, t], device_id=at(4 - 8 * side), device_id_type=MESH,
        )

    def ahead(side):
        return exists(1 - 2 * side)

    def behind(side):
        return exists(2 * side - 1)

    for t in (0, 1):
        for o in range(1, blocks):
            x_copy(t, o).start()
        for side in (0, 1):

            @pl.when(ahead(side))
            def _(side=side, t=t):
                z_copy(side, t, 0).start()

    for i, step in enumerate(steps):

        @pl.when(exists(step))
        def _(i=i, step=step):
            list_copy(i, step).start()

    for t in (0, 1):
        for o in range(1, blocks):
            x_copy(t, o).wait_recv()
            for side in (0, 1):

                @pl.when(ahead(side))
                def _(side=side, t=t, o=o):
                    z_copy(side, t, o).start()

    for o in range(1, blocks):
        x_copy(2, o).start()

    def choose(i, distance, load, store):
        first, count, union = table[distance]
        seen, rank = [], []
        before = jnp.zeros((1, 1), jnp.int32)
        for c in range(blocks):
            hit = jnp.zeros((1, 1), jnp.int32)
            for b in range(blocks):
                for j in range(first, first + count):
                    hit = jnp.maximum(hit, (heard[i, b : b + 1, j : j + 1] == c).astype(jnp.int32))
            seen.append(hit)
            rank.append(before)
            before = before + hit
        for u in range(union):
            value = load(blocks - 1).astype(jnp.float32)
            for c in range(blocks - 1):
                mask = jnp.where(rank[c] == u, seen[c], 0)
                mask = jnp.broadcast_to(mask, value.shape)
                value = jnp.where(mask == 1, load(c).astype(jnp.float32), value)
            store(u, value.astype(jnp.bfloat16))

    def place(b, slot, distance):
        first, count, union = table[distance]
        number = lists_s[b, slot]
        if union == blocks:
            return number
        if union == 1:
            return 0
        position = jnp.int32(0)
        for c in range(blocks - 1):
            seen = jnp.int32(0)
            for other in range(blocks):
                for j in range(first, first + count):
                    seen = jnp.maximum(seen, (lists_s[other, j] == c).astype(jnp.int32))
            position = position + jnp.where(c < number, seen, 0)
        return position

    def attend(distance, keys, values, fresh=False):
        first, count, union = table[distance]
        for b in range(blocks):
            for j in range(count):
                n = place(b, first + j, distance)
                for h in range(heads):
                    cut = slice(h * DH, (h + 1) * DH)
                    scores = lax.dot_general(
                        qb[b, :, cut], keys(n, cut), (((1,), (1,)), ((), ())),
                        preferred_element_type=jnp.float32,
                    ) * scale
                    top = jnp.max(scores, axis=1, keepdims=True)
                    if fresh and j == 0:
                        weights = jnp.exp(scores - top)
                        peak[b, h] = jnp.broadcast_to(top, (BLOCK, DH))
                        total[b, h] = jnp.broadcast_to(
                            jnp.sum(weights, axis=1, keepdims=True), (BLOCK, DH)
                        )
                        numer[b, h] = jnp.dot(
                            weights.astype(jnp.bfloat16), values(n, cut),
                            preferred_element_type=jnp.float32,
                        )
                    else:
                        old = peak[b, h]
                        new = jnp.maximum(old, jnp.broadcast_to(top, (BLOCK, DH)))
                        fade = jnp.exp(old - new)
                        weights = jnp.exp(scores - new)
                        peak[b, h] = new
                        total[b, h] = total[b, h] * fade + jnp.broadcast_to(
                            jnp.sum(weights, axis=1, keepdims=True), (BLOCK, DH)
                        )
                        numer[b, h] = numer[b, h] * fade + jnp.dot(
                            weights.astype(jnp.bfloat16), values(n, cut),
                            preferred_element_type=jnp.float32,
                        )

    if use_far:
        for side in (0, 1):

            @pl.when(exists(4 - 8 * side))
            def _(side=side):
                i = 3 - side
                list_wait(i).wait_recv()
                for t in (0, 1):
                    choose(
                        i, -4 if side == 0 else 4,
                        lambda c: own[t, c],
                        lambda u, x: pick4.__setitem__((side, t, u), x),
                    )
                    f_copy(side, t).start()

    for i in (0, 1):

        @pl.when(exists(steps[i]))
        def _(i=i):
            list_wait(i).wait_recv()

    for side in (0, 1):

        @pl.when(behind(side))
        def _(side=side):
            for o in range(blocks):
                z_copy(side, 0, o).wait_recv()

        @pl.when(behind(side) & ahead(side))
        def _(side=side):
            choose(
                1 - side, -2 if side == 0 else 2,
                lambda c: near[side, 0, c],
                lambda u, x: pick2.__setitem__((side, u), x),
            )
            m_copy(side, -1).start()

    for o in range(1, blocks):
        x_copy(2, o).wait_recv()
    attend(0, lambda n, cut: own[0, n, :, cut], lambda n, cut: own[1, n, :, cut], fresh=True)

    for side in (0, 1):

        @pl.when(behind(side))
        def _(side=side):
            for o in range(blocks):
                z_copy(side, 1, o).wait_recv()

        @pl.when(behind(side) & ahead(side))
        def _(side=side):
            for h in range(heads):
                choose(
                    1 - side, -2 if side == 0 else 2,
                    lambda c: near[side, 1, c, :, h * DH : (h + 1) * DH],
                    lambda u, x: pick2v.__setitem__((side, h, u), x),
                )
                m_copy(side, h).start()

    for side in (0, 1):

        @pl.when(behind(side))
        def _(side=side):
            attend(
                -1 if side == 0 else 1,
                lambda n, cut: near[side, 0, n, :, cut], lambda n, cut: near[side, 1, n, :, cut],
            )

    if use_far:
        for side in (0, 1):

            @pl.when(exists(8 * side - 4))
            def _(side=side):
                for t in (0, 1):
                    f_copy(side, t).wait_recv()
                attend(
                    -4 if side == 0 else 4,
                    lambda n, cut: far[side, 0, n, :, cut], lambda n, cut: far[side, 1, n, :, cut],
                )

    for side in (0, 1):

        @pl.when(exists(4 * side - 2))
        def _(side=side):
            m_copy(side, -1).wait_recv()

    def mid_scores(b, h, side, j):
        distance = -2 if side == 0 else 2
        cut = slice(h * DH, (h + 1) * DH)
        n = place(b, table[distance][0] + j, distance)
        return lax.dot_general(
            qb[b, :, cut], mid[side, n, :, cut], (((1,), (1,)), ((), ())),
            preferred_element_type=jnp.float32,
        ) * scale

    def mid_weights(sides):
        slots = [(side, j) for side in sides for j in range(table[2][1])]
        for b in range(blocks):
            for h in range(heads):
                scores = [mid_scores(b, h, side, j) for side, j in slots]
                old = peak[b, h]
                new = old
                for x in scores:
                    top = jnp.max(x, axis=1, keepdims=True)
                    new = jnp.maximum(new, jnp.broadcast_to(top, (BLOCK, DH)))
                fade = jnp.exp(old - new)
                whole = total[b, h] * fade
                for (side, j), x in zip(slots, scores):
                    weights = jnp.exp(x - new)
                    whole = whole + jnp.broadcast_to(
                        jnp.sum(weights, axis=1, keepdims=True), (BLOCK, DH)
                    )
                    held[side, j, b, h] = weights.astype(jnp.bfloat16)
                total[b, h] = 1.0 / whole
                numer[b, h] = numer[b, h] * fade

    def o_copy(o, h):
        to = lax.rem(s + o, blocks)
        return pltpu.make_async_remote_copy(
            src_ref=ob.at[to, h], dst_ref=out.at[:, head_cols(s, h)],
            send_sem=os_.at[o, h], recv_sem=or_.at[o, h],
            device_id={"space": to}, device_id_type=MESH,
        )

    def head_cols(i, h):
        return pl.ds(pl.multiple_of(i * width + h * DH, DH), DH)

    def keep(h):
        return pltpu.make_async_copy(ob.at[s, h], out.at[:, head_cols(s, h)], os_.at[0, h])

    def finish(sides):
        for h in range(heads):
            for side in sides:
                m_copy(side, h).wait_recv()
            for o in list(range(1, blocks)) + [0]:
                b = lax.rem(s + o, blocks)
                value = numer[b, h]
                for side in sides:
                    distance = -2 if side == 0 else 2
                    for j in range(table[2][1]):
                        n = place(b, table[distance][0] + j, distance)
                        value = value + jnp.dot(
                            held[side, j, b, h], midv[side, h, n],
                            preferred_element_type=jnp.float32,
                        )
                ob[b, h] = (value * total[b, h]).astype(jnp.bfloat16)
                if o:
                    o_copy(o, h).start()
                else:
                    keep(h).start()

    def last(sides):
        mid_weights(sides)
        finish(sides)

    pl.when(exists(-2) & exists(2))(lambda: last((0, 1)))
    pl.when(exists(-2) & ~exists(2))(lambda: last((0,)))
    pl.when(~exists(-2) & exists(2))(lambda: last((1,)))
    pl.when(~exists(-2) & ~exists(2))(lambda: last(()))

    for t in (0, 1, 2):
        for o in range(1, blocks):
            x_copy(t, o).wait_send()
    for i, step in enumerate(steps):

        @pl.when(exists(step))
        def _(i=i, step=step):
            list_copy(i, step).wait_send()

    for side in (0, 1):

        @pl.when(ahead(side))
        def _(side=side):
            for t in (0, 1):
                for o in range(blocks):
                    z_copy(side, t, o).wait_send()

        @pl.when(behind(side) & ahead(side))
        def _(side=side):
            for h in range(-1, heads):
                m_copy(side, h).wait_send()

        if use_far:

            @pl.when(exists(4 - 8 * side))
            def _(side=side):
                for t in (0, 1):
                    f_copy(side, t).wait_send()

    for h in range(heads):
        keep(h).wait()
        for o in range(1, blocks):
            o_copy(o, h).wait_send()
            pltpu.make_async_remote_copy(
                src_ref=ob.at[s, h], dst_ref=out.at[:, head_cols(lax.rem(s - o + blocks, blocks), h)],
                send_sem=os_.at[o, h], recv_sem=or_.at[o, h],
                device_id={"space": lax.rem(s + o, blocks)}, device_id_type=MESH,
            ).wait_recv()


def local(frames, blocks, queries, key_rows, value_rows, block_lists):
    rows, columns = queries.shape
    width = columns // blocks
    heads = width // DH
    lists = block_lists[0]
    table = group_table(blocks)
    u2, u4 = table[2][2], table[4][2]
    far_rows = BLOCK if frames > 4 else 16
    dma = pltpu.SemaphoreType.DMA
    bf = jnp.bfloat16
    return pl.pallas_call(
        functools.partial(kernel, frames, blocks),
        out_shape=jax.ShapeDtypeStruct(queries.shape, queries.dtype),
        in_specs=[pl.BlockSpec(memory_space=pltpu.HBM)] * 4,
        out_specs=pl.BlockSpec(memory_space=pl.ANY),
        scratch_shapes=[
            pltpu.SMEM(lists.shape, jnp.int32),
            pltpu.VMEM((blocks, BLOCK, width), bf),
            pltpu.VMEM((2, blocks, BLOCK, width), bf),
            pltpu.VMEM((2, 2, blocks, BLOCK, width), bf),
            pltpu.VMEM((2, u2, BLOCK, width), bf),
            pltpu.VMEM((2, u2, BLOCK, width), bf),
            pltpu.VMEM((2, heads, u2, BLOCK, DH), bf),
            pltpu.VMEM((2, heads, u2, BLOCK, DH), bf),
            pltpu.VMEM((2, 2, u4, far_rows, width), bf),
            pltpu.VMEM((2, 2, u4, far_rows, width), bf),
            pltpu.VMEM((4,) + lists.shape, jnp.int32),
            pltpu.VMEM((blocks, heads, BLOCK, DH), bf),
            pltpu.VMEM((blocks, heads, BLOCK, DH), jnp.float32),
            pltpu.VMEM((blocks, heads, BLOCK, DH), jnp.float32),
            pltpu.VMEM((blocks, heads, BLOCK, DH), jnp.float32),
            pltpu.VMEM((2, table[2][1], blocks, heads, BLOCK, DH), bf),
            pltpu.VMEM((3, blocks, BLOCK, width), bf),
            dma((3, blocks)),
            dma((5,)),
            dma((3, blocks)),
            dma((3, blocks)),
            dma((2, 2, blocks)),
            dma((2, 2, blocks)),
            dma((2, 1 + heads)),
            dma((2, 1 + heads)),
            dma((2, 2)),
            dma((2, 2)),
            dma((4,)),
            dma((4,)),
            dma((blocks, heads)),
            dma((blocks, heads)),
        ],
        compiler_params=pltpu.CompilerParams(
            collective_id=0, has_side_effects=True, vmem_limit_bytes=48 * 1024 * 1024
        ),
    )(*[pltpu.with_memory_space_constraint(x, pltpu.HBM) for x in (queries, key_rows, value_rows, lists)])


def short_kernel(
    frames, blocks, q, k, v, lists_v, out,
    qh, kh, vh, kv, xq, qn, mid, pick, held, rt, po, ps, pin, lin, own_o, own_l, heard,
    loc_sem, xs, xr, qs, qr, ks, kr, ps_, pr, ss, sr, ls, lr, cs, cr, ready,
):
    f = lax.axis_index("tm")
    s = lax.axis_index("space")
    other = 1 - s
    width = qn.shape[3]
    heads = width // DH
    table = group_table(blocks)
    factor = DH ** -0.5 * LOG2E
    sides = (0, 1)
    early = f < frames // 2
    core = lax.axis_index("head")
    lead = core == 1

    def exists(step):
        return (f + step >= 0) & (f + step < frames)

    def step(side):
        return 2 * side - 1

    def ex(side):
        return exists(step(side))

    def half(i):
        return pl.ds(pl.multiple_of(i * width, width), width)

    def head_of(i, h):
        return pl.ds(pl.multiple_of(i * width + h * DH, DH), DH)

    def cut(h):
        return slice(h * DH, (h + 1) * DH)

    def remote(src, dst, send, recv, **where):
        return pltpu.make_async_remote_copy(
            src_ref=src, dst_ref=dst, send_sem=send, recv_sem=recv,
            device_id=where, device_id_type=MESH,
        )

    local = [
        pltpu.make_async_copy(q, qh, loc_sem.at[0]),
        pltpu.make_async_copy(k, kh, loc_sem.at[1]),
        pltpu.make_async_copy(v, vh, loc_sem.at[2]),
    ]
    for t in (0, 1):
        for h in range(heads):
            local.append(pltpu.make_async_copy(
                (k, v)[t].at[:, head_of(s, h)], kv[t][h].at[s], loc_sem.at[3 + t * heads + h]
            ))
    for copy in local:
        copy.start()

    def late(frame):
        return frame >= frames // 2

    def greet(semaphore, d):
        pl.semaphore_signal(semaphore, inc=1, device_id={"tm": f + d}, device_id_type=MESH)

    barrier = pltpu.get_barrier_semaphore()
    pl.semaphore_signal(barrier, inc=1, device_id={"space": other}, device_id_type=MESH)
    pl.when(exists(2) & lead)(lambda: greet(barrier, 2))

    @pl.when(~lead)
    def _():
        pl.semaphore_signal(barrier, inc=1, device_id={"head": 1}, device_id_type=MESH)

    pl.when(exists(1))(lambda: greet(barrier, 1))
    pl.when(exists(-1) & ~late(f))(lambda: greet(barrier, -1))
    greeted = 1 + exists(-1).astype(jnp.int32)
    greeted = greeted + (exists(-2) & lead).astype(jnp.int32) + lead.astype(jnp.int32)
    pl.semaphore_wait(barrier, greeted + (exists(1) & ~late(f + 1)).astype(jnp.int32))
    pl.when(exists(-1) & late(f))(lambda: greet(ready.at[0], -1))
    pl.when(exists(-2) & lead)(lambda: greet(ready.at[1], -2))

    def list_copy(i, d):
        return remote(lists_v, heard.at[i ^ 1], ls.at[i], lr.at[i ^ 1], tm=f + d)

    def list_wait(i, d):
        return remote(lists_v, heard.at[i], ls.at[i], lr.at[i], tm=f + d)

    list_steps = (-1, 1, -2, 2)

    places = (s, other)

    def x_copy(t, h):
        src = (k, v, q)[t].at[:, head_of(other, h)]
        dst = xq.at[h] if t == 2 else kv[t][h].at[s]
        return remote(src, dst, xs.at[t, h], xr.at[t, h], space=other)

    def x_wait(t, h):
        src = (k, v, q)[t].at[:, head_of(other, h)]
        dst = xq.at[h] if t == 2 else kv[t][h].at[other]
        return remote(src, dst, xs.at[t, h], xr.at[t, h], space=other)

    def q_copy(side, i, to=None):
        to = 1 - side if to is None else to
        if i < 2:
            part = width // 2
            src = q.at[:, pl.ds(pl.multiple_of(s * width + i * part, DH), part)]
            dst = qn.at[to, 0, :, slice(i * part, (i + 1) * part)]
        else:
            src, dst = xq.at[i - 2], qn.at[to, 1, :, cut(i - 2)]
        return remote(src, dst, qs.at[side, i], qr.at[to, i], tm=f + step(side))

    def k_copy(side, t, h, to=None):
        to = 1 - side if to is None else to
        return remote(
            pick.at[side, t, :, cut(h)], mid.at[to, t, :, cut(h)], ks.at[side, t, h],
            kr.at[to, t, h], tm=f + step(side),
        )

    def p_copy(side, i, h, to=None):
        to = 1 - side if to is None else to
        return remote(
            po.at[side, i, h], pin.at[to, i, h], ps_.at[side, i, h], pr.at[to, i, h],
            tm=f + step(side), space=places[i],
        )

    def s_copy(side, i, h, to=None):
        to = 1 - side if to is None else to
        return remote(
            ps.at[side, i, h], lin.at[to, i, h], ss.at[side, i, h], sr.at[to, i, h],
            tm=f + step(side), space=places[i],
        )

    def on_sides(run, there=ex):
        for side in sides:
            pl.when(there(side))(functools.partial(run, side))

    def wait_sides(copy, *key, there=ex):
        on_sides(lambda side: copy(side, *key, to=side).wait_recv(), there)

    @pl.when(exists(-1))
    def _():
        pl.when(lead)(lambda: list_copy(0, -1).start())
        q_copy(0, 0).start()
        q_copy(0, 1).start()

    pl.when(exists(-2) & lead)(lambda: list_copy(2, -2).start())

    def start_queries(span):
        for h in span:
            x_copy(2, h).start()

    start_queries(range(FIRST))
    pl.when(early)(lambda: start_queries(range(FIRST, heads)))
    for h in range(heads):
        for t in (0, 1):
            x_copy(t, h).start()
    pl.when(~early)(lambda: start_queries(range(FIRST, heads)))

    @pl.when(exists(1))
    def _():
        pl.when(late(f + 1))(lambda: pl.semaphore_wait(ready.at[0], 1))
        pl.when(lead)(lambda: list_copy(1, 1).start())
        q_copy(1, 0).start()

        @pl.when(exists(2) & lead)
        def _():
            pl.semaphore_wait(ready.at[1], 1)
            list_copy(3, 2).start()

        q_copy(1, 1).start()

    for copy in local:
        copy.wait()

    def scores(keys, queries):
        return lax.dot_general(
            keys, queries, (((1,), (1,)), ((), ())), preferred_element_type=jnp.float32
        ) * factor

    def gathered(values, weights):
        return lax.dot_general(
            values, weights, (((0,), (0,)), ((), ())), preferred_element_type=jnp.float32
        )

    def home(i, h):
        columns = head_of(places[i], h)
        x = scores(kh[:, columns], qh[:, columns])
        top = jnp.max(x, axis=0, keepdims=True)
        weights = jnp.exp2(x - top)
        whole = jnp.sum(weights, axis=0, keepdims=True)
        own_o[i, h] = gathered(vh[:, columns], weights.astype(jnp.bfloat16)) * (1.0 / whole)
        own_l[i, h : h + 1] = top + jnp.log2(whole)

    def send_pick(t, h):
        x_wait(t, h).wait_recv()

        def run(side):
            n = heard[2 + side, 0, table[-2 * step(side)][0]]
            pick[side, t, :, cut(h)] = kv[t][h][n]
            k_copy(side, t, h).start()

        on_sides(run, lambda side: exists(2 * step(side)))

    def near_block(side, i):
        return heard[side, places[i], table[-step(side)][0]]

    def weigh(side, i, h, both):
        queries = qn[side, i, :, cut(h)]
        x = [scores(kv[0][h][near_block(side, i)], queries)]
        if both:
            x.append(scores(mid[1 - side, 0, :, cut(h)], queries))
        top = functools.reduce(jnp.maximum, [jnp.max(y, axis=0, keepdims=True) for y in x])
        whole = jnp.zeros_like(top)
        for j, y in enumerate(x):
            weights = jnp.exp2(y - top)
            whole = whole + jnp.sum(weights, axis=0, keepdims=True)
            held[side, i, h, j] = weights.astype(jnp.bfloat16)
        rt[side, i, h : h + 1] = 1.0 / whole
        ps[side, i, h] = top + jnp.log2(whole)

    def answer(side, i, h, both):
        value = gathered(kv[1][h][near_block(side, i)], held[side, i, h, 0])
        if both:
            value = value + gathered(mid[1 - side, 1, :, cut(h)], held[side, i, h, 1])
        po[side, i, h] = (value * rt[side, i, h : h + 1]).astype(jnp.bfloat16)

    inner = ex(0) & ex(1)

    def between(side):
        return inner

    def serve(side, h, both, send=False):
        if h == 0:
            q_copy(side, 0, to=side).wait_recv()
            q_copy(side, 1, to=side).wait_recv()
        q_copy(side, 2 + h, to=side).wait_recv()
        if both:
            k_copy(side, 0, h, to=1 - side).wait_recv()
        for i in range(blocks):
            weigh(side, i, h, both)
        if both:
            k_copy(side, 1, h, to=1 - side).wait_recv()
        if send:
            for i in range(blocks):
                s_copy(side, i, h).start()
        for i in reversed(range(blocks)):
            answer(side, i, h, both)
            if send:
                p_copy(side, i, h).start()

    def reply(side, h):
        for i in range(blocks):
            s_copy(side, i, h).start()
        for i in reversed(range(blocks)):
            p_copy(side, i, h).start()

    def forward(h):
        send_pick(0, h)
        send_pick(1, h)

    def forward_queries(h):
        x_wait(2, h).wait_recv()
        on_sides(lambda side: q_copy(side, 2 + h).start())

    for h in range(heads):
        home(0, h)

    def chip_copy(i):
        return remote(heard.at[i], heard.at[i], cs.at[i], cr.at[i], head=0)

    def wait_lists():
        for i, d in enumerate(list_steps):

            @pl.when(exists(d) & lead)
            def _():
                list_wait(i, d).wait_recv()
                chip_copy(i).start()

            pl.when(exists(d) & ~lead)(lambda: chip_copy(i).wait_recv())

    @pl.when(early)
    def _():
        for h in range(heads):
            forward_queries(h)
            home(1, h)
        wait_lists()
        for h in range(heads):
            forward(h)

            @pl.when(inner)
            def _(h=h):
                serve(0, h, True, True)

        for both, there in ((True, inner), (False, ~inner)):

            @pl.when(there)
            def _(both=both):
                for h in range(heads):
                    serve(1, h, both, True)

    @pl.when(~early)
    def _():
        for h in range(FIRST):
            forward_queries(h)
            home(1, h)
        wait_lists()
        forward(0)
        for h in range(FIRST, heads):
            home(1, h)
        for h in range(1, heads):
            forward(h)
            if h >= 2:
                pl.when(inner)(functools.partial(serve, 0, h - 2, True))

        for h in range(FIRST, heads):
            forward_queries(h)
        pl.when(inner)(functools.partial(serve, 0, heads - 2, True))

        @pl.when(inner)
        def _():
            for h in range(heads):
                if h == heads - 1:
                    serve(0, h, True)
                reply(0, h)
            for h in range(heads):
                serve(1, h, True, True)

        @pl.when(~inner)
        def _():
            for h in range(heads):
                serve(0, h, False, True)

    def merge(i, h, parts):
        rows = [own_l[i, h : h + 1]] + [lin[side, i, h] for side in parts]
        top = functools.reduce(jnp.maximum, rows)
        shares = [jnp.exp2(row - top) for row in rows]
        scale = 1.0 / functools.reduce(jnp.add, shares)
        value = own_o[i, h] * (shares[0] * scale)
        for side, share in zip(parts, shares[1:]):
            value = value + pin[side, i, h].astype(jnp.float32) * (share * scale)
        out[:, head_of(places[i], h)] = value.astype(jnp.bfloat16).T

    for h in range(heads):
        for i in range(blocks):
            wait_sides(s_copy, i, h)
            wait_sides(p_copy, i, h)
            pl.when(ex(0) & ex(1))(lambda: merge(i, h, (0, 1)))
            pl.when(ex(0) & ~ex(1))(lambda: merge(i, h, (0,)))
            pl.when(~ex(0) & ex(1))(lambda: merge(i, h, (1,)))
            pl.when(~ex(0) & ~ex(1))(lambda: merge(i, h, ()))

    for t in range(3):
        for h in range(heads):
            x_copy(t, h).wait_send()
    for i, d in enumerate(list_steps):

        @pl.when(exists(d) & lead)
        def _(i=i, d=d):
            list_copy(i, d).wait_send()
            chip_copy(i).wait_send()

    @on_sides
    def _(side):
        for i in range(2 + heads):
            q_copy(side, i).wait_send()
        for i in range(blocks):
            for h in range(heads):
                s_copy(side, i, h).wait_send()
                p_copy(side, i, h).wait_send()

        @pl.when(exists(2 * step(side)))
        def _():
            for t in (0, 1):
                for h in range(heads):
                    k_copy(side, t, h).wait_send()


def short(frames, blocks, queries, key_rows, value_rows, block_lists):
    rows, columns = queries.shape
    width = columns // blocks
    heads = width // DH
    lists = block_lists[0]
    dma = pltpu.SemaphoreType.DMA
    bf, f32 = jnp.bfloat16, jnp.float32
    vmem = pltpu.VMEM
    return pl.pallas_call(
        functools.partial(short_kernel, frames, blocks),
        out_shape=jax.ShapeDtypeStruct(queries.shape, queries.dtype),
        in_specs=[pl.BlockSpec(memory_space=pltpu.HBM)] * 4,
        out_specs=pl.BlockSpec(memory_space=pltpu.VMEM),
        scratch_shapes=[
            vmem((rows, columns), bf),
            vmem((rows, columns), bf),
            vmem((rows, columns), bf),
            [[vmem((blocks, BLOCK, DH), bf)] * heads] * 2,
            vmem((heads, BLOCK, DH), bf),
            vmem((2, blocks, BLOCK, width), bf),
            vmem((2, 2, BLOCK, width), bf),
            vmem((2, 2, BLOCK, width), bf),
            vmem((2, blocks, heads, 2, BLOCK, BLOCK), bf),
            vmem((2, blocks, 8, BLOCK), f32),
            vmem((2, blocks, heads, DH, BLOCK), bf),
            vmem((2, blocks, heads, 1, BLOCK), f32),
            vmem((2, blocks, heads, DH, BLOCK), bf),
            vmem((2, blocks, heads, 1, BLOCK), f32),
            vmem((blocks, heads, DH, BLOCK), f32),
            vmem((blocks, 8, BLOCK), f32),
            pltpu.SMEM((4,) + lists.shape, jnp.int32),
            dma((3 + 2 * heads,)),
            dma((3, heads)),
            dma((3, heads)),
            dma((2, 2 + heads)),
            dma((2, 2 + heads)),
            dma((2, 2, heads)),
            dma((2, 2, heads)),
            dma((2, blocks, heads)),
            dma((2, blocks, heads)),
            dma((2, blocks, heads)),
            dma((2, blocks, heads)),
            dma((4,)),
            dma((4,)),
            dma((4,)),
            dma((4,)),
            pltpu.SemaphoreType.REGULAR((2,)),
        ],
        compiler_params=pltpu.CompilerParams(
            collective_id=1, has_side_effects=True, vmem_limit_bytes=48 * 1024 * 1024
        ),
    )(*[pltpu.with_memory_space_constraint(x, pltpu.HBM) for x in (queries, key_rows, value_rows, lists)])


def solution(mesh):
    in_specs = (
        P(("groups", "tm", "space"), "head"),
        P(("groups", "tm", "space"), "head"),
        P(("groups", "tm", "space"), "head"),
        P(("groups", "tm"), None, None),
    )
    out_specs = P(("groups", "tm", "space"), "head")
    frames, blocks = mesh.shape["tm"], mesh.shape["space"]
    body = functools.partial(short if frames <= 4 and blocks == 2 else local, frames, blocks)
    return jax.shard_map(body, mesh=mesh, in_specs=in_specs, out_specs=out_specs, check_vma=False)
```
